32 devices in a mesh: row: 8 (over z, x), col: 4 (over y, core).
Axes of the slice: x: 2, y: 2, z: 4, core: 2. Of those that a mesh axis runs over, the one named last changes fastest.
Arguments:
- amplitudes: float32 [4096, 4096], P('row', 'col'), may hold values from -1 to 1, as said below
- interaction: float32 [4096, 4096], P('row', 'col'), may hold values from -9 to 9, as said below
- occ_energy: float32 [4], replicated, may hold values from -2.5 to -0.5
- vir_energy: float32 [1024], replicated, may hold values from 0.2 to 4
Outputs:
- updated: float32 [4096, 4096], P('row', 'col')
- residual: float32 [4096, 4096], P('row', 'col')
The draws below stay inside these ranges and needn't reach their ends.
Inputs may be any that keep to these rules, and one draw needn't show every extreme that they name: amplitudes is symmetric: it equals its transpose exactly. interaction is symmetric: it equals its transpose exactly.
All inputs are finite; a program needn't handle non-finite values.
Results may differ from the reference program's by a relative error of at most 0.000057.
Values sent between devices are 32-bit elements; how exact they have to be, the bound alone decides.
No kernel may reach another device: no remote copies, remote signals or barrier semaphores. Data moves between devices by JAX's collectives and lax.ppermute only.
A program may use at most 64 MiB of HBM per device.

```python
import jax
import jax.numpy as jnp
from jax import lax

VIRT = 1024
OCC_W = 4
PAIRS = 4096


def symmetric_draw(key, spread):
    base = jnp.clip(jax.random.normal(key, (PAIRS, PAIRS), jnp.float32), -6.0, 6.0)
    return (base + base.T) * (spread * 0.7071)


def draw_amplitudes(key, part):
    return symmetric_draw(jax.random.fold_in(key, 11), 0.1)


def draw_interaction(key, part):
    return symmetric_draw(jax.random.fold_in(key, 23), 10.0 / PAIRS ** 0.5)


def setup_inputs(seed: int = 0) -> dict:
    keys = jax.random.split(jax.random.key(seed), 5)
    amplitudes = draw_amplitudes(jax.random.fold_in(keys[4], 71), 0)
    interaction = draw_interaction(jax.random.fold_in(keys[4], 71), 0)
    occ_energy = jnp.clip(jax.random.uniform(keys[2], (OCC_W,), jnp.float32, -2.5, -0.5), -2.5, -0.5)
    vir_energy = jnp.clip(jax.random.uniform(keys[3], (VIRT,), jnp.float32, 0.2, 4.0), 0.2, 4.0)
    return {"amplitudes": amplitudes, "interaction": interaction, "occ_energy": occ_energy, "vir_energy": vir_energy}


def reference(amplitudes, interaction, occ_energy, vir_energy):
    product = jnp.dot(amplitudes, interaction, precision=lax.Precision.HIGHEST, preferred_element_type=jnp.float32)
    gaps = (vir_energy[None, :] - occ_energy[:, None]).reshape(-1)
    denom = gaps[:, None] + gaps[None, :]
    residual = interaction + product + product.T + denom * amplitudes
    updated = amplitudes - residual / denom
    return updated, residual
```

```python
import jax
import jax.numpy as jnp
from jax import lax
from jax.sharding import PartitionSpec as P

CHUNKS = 2
PAD = 8


def swapped(block, axis, distance):
    count = lax.axis_size(axis)
    route = []
    for low in range(count):
        high = low | 1 << distance
        if high != low and high < count:
            route += [(low, high), (high, low)]
    return lax.ppermute(block, axis, route)


def from_behind(block, axis, distance):
    devices = range(lax.axis_size(axis))
    route = [(i - distance, i) for i in devices if i - distance in devices]
    return lax.ppermute(block, axis, route)


def contract(left_tile, right_tile):
    right_panel = lax.all_gather(right_tile, "row", axis=0, tiled=True)
    return jnp.dot(
        lax.all_gather(left_tile, "col", axis=1, tiled=True),
        right_panel,
        precision=lax.Precision.HIGHEST,
        preferred_element_type=jnp.float32,
    )


def diagonal_tile(tile, row_place, col_place):
    tile_rows = tile.shape[0]
    col_count = lax.axis_size("col")
    ratio = lax.axis_size("row") // col_count
    ratio_bits = ratio.bit_length() - 1
    row_bits = lax.axis_size("row").bit_length() - 1
    blocks = tile.reshape(tile_rows, ratio, tile_rows).transpose(1, 2, 0)
    for bit_index in range(row_bits):
        row_flag = row_place // 2**bit_index % 2
        if bit_index < ratio_bits:
            lower = 2**bit_index
            grouped = blocks.reshape(ratio // (2 * lower), 2, lower, tile_rows, tile_rows)
            zero_half = grouped[:, 0]
            one_half = grouped[:, 1]
            outgoing = jnp.where(row_flag == 0, one_half, zero_half)
            incoming = swapped(outgoing, "row", bit_index)
            new_zero = jnp.where(row_flag == 1, incoming, zero_half)
            new_one = jnp.where(row_flag == 0, incoming, one_half)
            blocks = jnp.stack([new_zero, new_one], axis=1).reshape(ratio, tile_rows, tile_rows)
        else:
            col_flag = col_place // 2 ** (bit_index - ratio_bits) % 2
            stride = 2**bit_index * col_count - 2 ** (bit_index - ratio_bits)
            from_above = from_behind(blocks, ("row", "col"), -stride)
            from_below = from_behind(blocks, ("row", "col"), stride)
            incoming = jnp.where(row_flag == 0, from_above, from_below)
            blocks = jnp.where(row_flag != col_flag, incoming, blocks)
    return blocks.transpose(1, 0, 2).reshape(tile_rows, ratio * tile_rows)


def general_sum(amplitudes, interaction):
    product = contract(amplitudes, interaction)
    mirrored = diagonal_tile(product, lax.axis_index("row"), lax.axis_index("col"))
    return product + mirrored


def routed(block, target):
    rows, cols = lax.axis_size("row"), lax.axis_size("col")
    route = []
    for r in range(rows):
        for c in range(cols):
            place = target(r, c)
            if place is not None:
                route.append((r * cols + c, place[0] * cols + place[1]))
    return lax.ppermute(block, ("row", "col"), route)


def crossed(left, right):
    return lax.dot_general(
        left,
        right,
        (((0,), (0,)), ((), ())),
        precision=lax.Precision.HIGH,
        preferred_element_type=jnp.float32,
    )


def is_near(r, c):
    return r >> 2 == c >> 1


def flipped(z, x, c):
    return x if z < c else 1 - x


def near_target(r, c):
    z, x = r >> 1, r & 1
    if not is_near(r, c):
        return None
    if z == c:
        return (r ^ 1, c)
    return (2 * c + flipped(z, x, c), z)


def far_target(r, c):
    z, x = r >> 1, r & 1
    if not is_near(r, c):
        return None
    return (2 * c + flipped(z ^ 2, x, c), z ^ 2)


def split_sum(amplitudes, interaction):
    n = amplitudes.shape[0]
    w = n // CHUNKS
    r = lax.axis_index("row")
    c = lax.axis_index("col")
    z, x = r // 2, r % 2
    near = r // 4 == c // 2
    odd = (z + c) % 2 == 1

    def half(panel, place):
        return lax.dynamic_slice_in_dim(panel, place * n, n, axis=1)

    own = jnp.concatenate([amplitudes, interaction], axis=0)
    turned = jnp.concatenate([interaction, amplitudes], axis=0)
    sides = {"send": 1 - x, "keep": x}
    left = {}
    for side, place in sides.items():
        left[0, side] = half(own, place)
    for side, place in sides.items():
        left[2, side] = routed(left[0, side], lambda r, c: (r, c ^ 2))
    for side, place in sides.items():
        left[1, side] = routed(left[0, side], lambda r, c: (r, c ^ 1))
    for side, place in sides.items():
        left[3, side] = routed(left[2, side], lambda r, c: (r, c ^ 1))

    right = {side: half(turned, place) for side, place in sides.items()}
    line = lax.broadcasted_iota(jnp.int32, (n, w), 0)
    lane = lax.broadcasted_iota(jnp.int32, (n, w), 1)

    def part(d, side, k):
        other = "keep" if side == "send" else "send"
        same = right[side][:, k * w : (k + 1) * w]
        cross = right[other][:, k * w : (k + 1) * w]
        if d == 0:
            diagonal = crossed(left[0, side], same)
            aside = crossed(left[0, side], cross)
            packed = jnp.where(line >= lane + k * w, diagonal, aside)
            extra = jnp.sum(jnp.where(line == lane + k * w, aside, 0.0), axis=0, keepdims=True)
            return jnp.concatenate([packed, jnp.broadcast_to(extra, (PAD, w))], axis=0)
        block = crossed(left[d, side], jnp.where((c ^ d) < c, same, cross))
        if d == 1:
            block = jnp.pad(block, ((0, PAD), (0, 0)))
        return block

    def reduced(first, k):
        outgoing = jnp.stack([part(first, "send", k), part(first + 1, "send", k)])
        incoming = routed(outgoing, lambda r, c: (r ^ 1, c))
        even_sum = part(first, "keep", k) + incoming[0]
        odd_sum = part(first + 1, "keep", k) + incoming[1]
        passed = routed(jnp.where(odd, even_sum, odd_sum), lambda r, c: (r ^ 2, c))
        return jnp.where(odd, odd_sum, even_sum) + passed

    mine, theirs = [], []
    near_sums = []
    for k in range(CHUNKS):
        total = reduced(0, k)
        total = total + routed(total, lambda r, c: None if is_near(r, c) else (r ^ 4, c))
        near_sums.append((total, routed(total[:n], near_target)))
    for k in range(CHUNKS):
        total = reduced(2, k)
        total = total + routed(total, lambda r, c: (r ^ 4, c))
        back = routed(total, far_target)
        near_total, near_back = near_sums[k]
        mine.append(jnp.where(near, near_total[:n], total))
        theirs.append(jnp.where(near, near_back, back))
    extra = jnp.concatenate([near_total[n : n + 1] for near_total, _ in near_sums], axis=1)

    mine = jnp.concatenate(mine, axis=1)
    theirs = jnp.concatenate(theirs, axis=1).T
    line = lax.broadcasted_iota(jnp.int32, (n, n), 0)
    lane = lax.broadcasted_iota(jnp.int32, (n, n), 1)
    middle = z == c
    diagonal = jnp.where(line >= lane, mine, mine.T)
    aside = jnp.where(line < lane, mine, jnp.where(line > lane, theirs, extra))
    first = jnp.where(middle, diagonal, mine)
    second = jnp.where(middle, aside, theirs)
    place = jnp.where(z <= c, x, 1 - x)
    return jnp.concatenate(
        [jnp.where(place == 0, first, second), jnp.where(place == 0, second, first)], axis=1
    )


def local(amplitudes, interaction, occ_energy, vir_energy):
    tile_rows, tile_cols = amplitudes.shape
    rows, cols = lax.axis_size("row"), lax.axis_size("col")
    row_place = lax.axis_index("row")
    col_place = lax.axis_index("col")
    if cols == 4 and rows == 2 * cols and tile_cols == 2 * tile_rows:
        both = split_sum(amplitudes, interaction)
    else:
        both = general_sum(amplitudes, interaction)
    gaps = (vir_energy[None, :] - occ_energy[:, None]).reshape(-1)
    row_gap = lax.dynamic_slice_in_dim(gaps, row_place * tile_rows, tile_rows, 0)
    col_gap = lax.dynamic_slice_in_dim(gaps, col_place * tile_cols, tile_cols, 0)
    denom = row_gap[:, None] + col_gap[None, :]
    residual = interaction + both + denom * amplitudes
    updated = amplitudes - residual / denom
    return (updated, residual)


def solution(mesh):
    return jax.shard_map(
        local,
        mesh=mesh,
        in_specs=(P("row", "col"), P("row", "col"), P(), P()),
        out_specs=(P("row", "col"), P("row", "col")),
        check_vma=False,
    )
```

```python
import functools

import jax
import jax.numpy as jnp
from jax import lax
from jax.experimental import pallas as pl
from jax.experimental.pallas import tpu as pltpu
from jax.sharding import PartitionSpec as P


CHUNKS = 4
PAD = 8


def swapped(block, axis, distance):
    count = lax.axis_size(axis)
    route = []
    for low in range(count):
        high = low | 1 << distance
        if high != low and high < count:
            route += [(low, high), (high, low)]
    return lax.ppermute(block, axis, route)


def from_behind(block, axis, distance):
    devices = range(lax.axis_size(axis))
    route = [(i - distance, i) for i in devices if i - distance in devices]
    return lax.ppermute(block, axis, route)


def contract(left_tile, right_tile):
    right_panel = lax.all_gather(right_tile, "row", axis=0, tiled=True)
    return jnp.dot(
        lax.all_gather(left_tile, "col", axis=1, tiled=True),
        right_panel,
        precision=lax.Precision.HIGHEST,
        preferred_element_type=jnp.float32,
    )


def diagonal_tile(tile, row_place, col_place):
    tile_rows = tile.shape[0]
    col_count = lax.axis_size("col")
    ratio = lax.axis_size("row") // col_count
    ratio_bits = ratio.bit_length() - 1
    row_bits = lax.axis_size("row").bit_length() - 1
    blocks = tile.reshape(tile_rows, ratio, tile_rows).transpose(1, 2, 0)
    for bit_index in range(row_bits):
        row_flag = row_place // 2**bit_index % 2
        if bit_index < ratio_bits:
            lower = 2**bit_index
            grouped = blocks.reshape(ratio // (2 * lower), 2, lower, tile_rows, tile_rows)
            zero_half = grouped[:, 0]
            one_half = grouped[:, 1]
            outgoing = jnp.where(row_flag == 0, one_half, zero_half)
            incoming = swapped(outgoing, "row", bit_index)
            new_zero = jnp.where(row_flag == 1, incoming, zero_half)
            new_one = jnp.where(row_flag == 0, incoming, one_half)
            blocks = jnp.stack([new_zero, new_one], axis=1).reshape(ratio, tile_rows, tile_rows)
        else:
            col_flag = col_place // 2 ** (bit_index - ratio_bits) % 2
            stride = 2**bit_index * col_count - 2 ** (bit_index - ratio_bits)
            from_above = from_behind(blocks, ("row", "col"), -stride)
            from_below = from_behind(blocks, ("row", "col"), stride)
            incoming = jnp.where(row_flag == 0, from_above, from_below)
            blocks = jnp.where(row_flag != col_flag, incoming, blocks)
    return blocks.transpose(1, 0, 2).reshape(tile_rows, ratio * tile_rows)


def general_sum(amplitudes, interaction):
    product = contract(amplitudes, interaction)
    mirrored = diagonal_tile(product, lax.axis_index("row"), lax.axis_index("col"))
    return product + mirrored


def routed(block, target):
    rows, cols = lax.axis_size("row"), lax.axis_size("col")
    route = []
    for r in range(rows):
        for c in range(cols):
            place = target(r, c)
            if place is not None:
                route.append((r * cols + c, place[0] * cols + place[1]))
    return lax.ppermute(block, ("row", "col"), route)


def is_near(r, c):
    return r >> 2 == c >> 1


def flipped(z, x, c):
    return x if z < c else 1 - x


def near_target(r, c):
    z, x = r >> 1, r & 1
    if not is_near(r, c):
        return None
    if z == c:
        return (r ^ 1, c)
    return (2 * c + flipped(z, x, c), z)


def far_target(r, c):
    z, x = r >> 1, r & 1
    if not is_near(r, c):
        return None
    return (2 * c + flipped(z ^ 2, x, c), z ^ 2)


X_PLACE, ODD, TURN_1, TURN_2, NEAR, MIDDLE, PLACE = range(7)
VMEM = 40 * 2**20


def params():
    return pltpu.CompilerParams(vmem_limit_bytes=VMEM)


def zeros(count):
    return (0,) * count


def call(kernel, shapes, meta, args, in_specs=None, out_specs=None, scratch=(), aliases=None):
    if in_specs is None:
        in_specs = [None] * len(args)
    if out_specs is None:
        out_specs = [None] * len(shapes)
    whole = lambda a: pl.BlockSpec(a.shape, lambda i, m: zeros(len(a.shape)))
    return pl.pallas_call(
        kernel,
        out_shape=list(shapes),
        grid_spec=pltpu.PrefetchScalarGridSpec(
            num_scalar_prefetch=1,
            grid=(1,),
            in_specs=[s or whole(a) for s, a in zip(in_specs, args)],
            out_specs=[s or whole(a) for s, a in zip(out_specs, shapes)],
            scratch_shapes=list(scratch),
        ),
        input_output_aliases=aliases or {},
        compiler_params=params(),
    )(meta, *args)


def shaped(*shape):
    return jax.ShapeDtypeStruct(shape, jnp.float32)


def halves(value):
    high = value.astype(jnp.bfloat16)
    return high, (value - high.astype(jnp.float32)).astype(jnp.bfloat16)


def left_of(t, v):
    t_high, t_low = halves(t)
    v_high, v_low = halves(v)
    return jnp.concatenate([t_high, t_high, t_low, v_high, v_high, v_low], axis=0)


def right_of(t, v):
    t_high, t_low = halves(t)
    v_high, v_low = halves(v)
    return jnp.concatenate([v_high, v_low, v_high, t_high, t_low, t_high], axis=0)


def crossed(left, right):
    return lax.dot_general(
        left, right, (((0,), (0,)), ((), ())), preferred_element_type=jnp.float32
    )


def placed(place, n, offset=0, size=None):
    return pl.ds(pl.multiple_of(place * n + offset, 128), size or n)


def pick_kernel(side, first, m, t_ref, v_ref, out_ref, sems):
    n = t_ref.shape[0]
    cols = placed(m[X_PLACE] ^ side, n, first, out_ref.shape[2])
    copies = [
        pltpu.make_async_copy(ref.at[:, cols], out_ref.at[i], sems.at[i])
        for i, ref in enumerate((t_ref, v_ref))
    ]
    for copy in copies:
        copy.start()
    for copy in copies:
        copy.wait()


def pick(meta, t, v, side, first, count):
    n = t.shape[0]
    w = n // CHUNKS
    hbm = pl.BlockSpec(memory_space=pltpu.MemorySpace.HBM)
    return call(
        functools.partial(pick_kernel, side, first * w),
        [shaped(2, n, count * w)],
        meta,
        [t, v],
        in_specs=[hbm, hbm],
        scratch=[pltpu.SemaphoreType.DMA((2,))],
    )[0]


def middle_block(m, side, k, w, t_ref, v_ref, store):
    n = t_ref.shape[0]
    half = m[X_PLACE] ^ side
    cols = placed(half, n, k * w, w)
    left = left_of(t_ref[:, cols], v_ref[:, cols])
    same, cross = placed(half, n), placed(1 - half, n)
    diagonal = crossed(left, right_of(t_ref[:, same], v_ref[:, same]))
    aside = crossed(left, right_of(t_ref[:, cross], v_ref[:, cross]))
    line = lax.broadcasted_iota(jnp.int32, (w, n), 0) + k * w
    lane = lax.broadcasted_iota(jnp.int32, (w, n), 1)
    extra = jnp.sum(jnp.where(line == lane, aside, 0.0), axis=0, keepdims=True)
    store(jnp.where(line >= lane, diagonal, aside), jnp.broadcast_to(extra, (PAD, n)))


def next_block(m, side, k, w, at_ref, av_ref, t_ref, v_ref, store):
    n = t_ref.shape[0]
    cols = placed(m[X_PLACE] ^ side, n, k * w, w)
    half = placed(m[TURN_1] ^ side, n)
    left = left_of(at_ref[:, cols], av_ref[:, cols])
    store(
        crossed(left, right_of(t_ref[:, half], v_ref[:, half])), jnp.zeros((PAD, n), jnp.float32)
    )


def stored(out_ref, place, w):
    def store(block, pad):
        out_ref[place, :w, :] = block
        out_ref[place, w:, :] = pad

    return store


def middle_kernel(side, k, w, m, t_ref, v_ref, out_ref):
    middle_block(m, side, k, w, t_ref, v_ref, stored(out_ref, 0, w))


def middle_part(meta, t, v, side, k):
    n = t.shape[0]
    w = n // CHUNKS
    return call(
        functools.partial(middle_kernel, side, k, w),
        [shaped(2, w + PAD, n)],
        meta,
        [t, v],
        out_specs=[pl.BlockSpec((1, w + PAD, n), lambda i, m: (0, 0, 0))],
    )[0]


def next_kernel(side, k, w, m, _, at_ref, av_ref, t_ref, v_ref, out_ref):
    next_block(m, side, k, w, at_ref, av_ref, t_ref, v_ref, stored(out_ref, 0, w))


def next_part(meta, base, at, av, t, v, side, k):
    n = t.shape[0]
    w = n // CHUNKS
    return call(
        functools.partial(next_kernel, side, k, w),
        [shaped(*base.shape)],
        meta,
        [base, at, av, t, v],
        in_specs=[pl.BlockSpec(memory_space=pl.ANY), None, None, None, None],
        out_specs=[pl.BlockSpec((1, w + PAD, n), lambda i, m: (1, 0, 0))],
        aliases={1: 0},
    )[0]


def near_kernel(side, chunks, w, m, at_ref, av_ref, t_ref, v_ref, *outs):
    for out_ref, k in zip(outs, chunks):
        middle_block(m, side, k, w, t_ref, v_ref, stored(out_ref, 0, w))
        next_block(m, side, k, w, at_ref, av_ref, t_ref, v_ref, stored(out_ref, 1, w))


def near_parts(meta, at, av, t, v, side, chunks):
    n = t.shape[0]
    w = n // CHUNKS
    return call(
        functools.partial(near_kernel, side, chunks, w),
        [shaped(2, w + PAD, n) for _ in chunks],
        meta,
        [at, av, t, v],
    )


def far_kernel(side, m, a_ref, b_ref, t_ref, v_ref, *outs):
    n = t_ref.shape[0]
    w = outs[0].shape[1]
    half = placed(m[TURN_2] ^ side, n)
    right = right_of(t_ref[:, half], v_ref[:, half])
    for d, ref in enumerate((a_ref, b_ref)):
        for i, out_ref in enumerate(outs):
            cols = slice(i * w, (i + 1) * w)
            out_ref[d] = crossed(left_of(ref[0, :, cols], ref[1, :, cols]), right)


def far_parts(meta, a, b, t, v, side):
    n = t.shape[0]
    w = n // CHUNKS
    return call(
        functools.partial(far_kernel, side),
        [shaped(2, w, n)] * (a.shape[2] // w),
        meta,
        [a, b, t, v],
    )


def fold_kernel(_, keep_pass, come_pass, keep_stay, come_stay, pass_ref, stay_ref):
    pass_ref[...] = keep_pass[0] + come_pass[0]
    stay_ref[...] = keep_stay[0] + come_stay[0]


def fold(meta, keep, come):
    _, lines, n = keep.shape
    leave = pl.BlockSpec((1, lines, n), lambda i, m: (1 - m[ODD], 0, 0))
    stay = pl.BlockSpec((1, lines, n), lambda i, m: (m[ODD], 0, 0))
    return call(
        fold_kernel,
        [shaped(lines, n)] * 2,
        meta,
        [keep, come, keep, come],
        in_specs=[leave, leave, stay, stay],
    )


def add_kernel(_, a_ref, b_ref, out_ref):
    out_ref[...] = a_ref[...] + b_ref[...]


def add(meta, a, b):
    return call(add_kernel, [shaped(*a.shape)], meta, [a, b])[0]


def join_kernel(w, count, _, *refs):
    out_ref = refs[2 * count]
    extra = None
    for k in range(count):
        a_ref, b_ref = refs[k], refs[count + k]
        out_ref[k * w : (k + 1) * w, :] = a_ref[:w, :] + b_ref[:w, :]
        if a_ref.shape[0] > w:
            pad = a_ref[w:, :] + b_ref[w:, :]
            extra = pad if extra is None else extra + pad
    if extra is not None:
        refs[2 * count + 1][...] = extra


def join(meta, parts, comes):
    n = parts[0].shape[1]
    w = n // CHUNKS
    shapes = [shaped(len(parts) * w, n)]
    if parts[0].shape[0] > w:
        shapes.append(shaped(PAD, n))
    return call(functools.partial(join_kernel, w, len(parts)), shapes, meta, [*parts, *comes])


def closing(t, v, row, col, value):
    denom = row + col
    residual = v + value + denom * t
    return t - residual / denom, residual


def most_kernel(m, *refs):
    near_own, near_back, extra_ref, *refs = refs
    far_own, far_back = refs[:3], refs[3:5]
    t_ref, v_ref, row_ref, col_ref, new_ref, res_ref = refs[5:]
    n = t_ref.shape[0]
    place = m[PLACE]

    def write(first, count, half, value):
        rows = pl.ds(first, count)
        new_ref[rows, half], res_ref[rows, half] = closing(
            t_ref[rows, half], v_ref[rows, half], row_ref[rows, :], col_ref[:, half], value
        )

    @pl.when(m[NEAR] == 0)
    def _():
        first = 0
        for ref in far_own:
            write(first, ref.shape[0], placed(place, n), ref[...])
            first += ref.shape[0]
        first = 0
        for ref in far_back:
            count = ref.shape[0]
            write(0, n, placed(1 - place, n, first, count), ref[...].T)
            first += count

    @pl.when((m[NEAR] == 1) & (m[MIDDLE] == 0))
    def _():
        write(0, n, placed(place, n), near_own[...])
        write(0, n, placed(1 - place, n), near_back[...].T)

    @pl.when(m[MIDDLE] == 1)
    def _():
        line = lax.broadcasted_iota(jnp.int32, (n, n), 0)
        lane = lax.broadcasted_iota(jnp.int32, (n, n), 1)
        own = near_own[...]
        write(0, n, placed(place, n), jnp.where(line >= lane, own, own.T))
        lower = jnp.where(line > lane, near_back[...].T, extra_ref[:1, :])
        write(0, n, placed(1 - place, n), jnp.where(line < lane, own, lower))


def most(meta, t, *args):
    return call(most_kernel, [shaped(*t.shape)] * 2, meta, args)


def last_kernel(m, back_ref, new_in, res_in, t_ref, v_ref, row_ref, col_ref, new_ref, res_ref):
    @pl.when(m[NEAR] == 1)
    def _():
        new_ref[...] = new_in[...]
        res_ref[...] = res_in[...]

    @pl.when(m[NEAR] == 0)
    def _():
        new_ref[...], res_ref[...] = closing(
            t_ref[...], v_ref[...], row_ref[...], col_ref[...], back_ref[...].T
        )


def last(meta, back, new, res, t, v, row_gap, col_gap):
    n = t.shape[0]
    w = n // CHUNKS
    at = lambda i, m: (0, (2 - m[PLACE]) * CHUNKS - 1)
    block = pl.BlockSpec((n, w), at)
    return call(
        last_kernel,
        [shaped(*t.shape)] * 2,
        meta,
        [back, new, res, t, v, row_gap, col_gap],
        in_specs=[None, block, block, block, block, None, pl.BlockSpec((1, w), at)],
        out_specs=[block, block],
        aliases={2: 0, 3: 1},
    )


def split_update(t, v, row_gap, col_gap):
    r = lax.axis_index("row")
    c = lax.axis_index("col")
    z, x = r // 2, r % 2
    slot = lax.iota(jnp.int32, 8)
    values = {
        X_PLACE: x,
        ODD: (z + c) % 2,
        TURN_1: jnp.where(c % 2 == 1, x, 1 - x),
        TURN_2: jnp.where(c // 2 == 1, x, 1 - x),
        NEAR: r // 4 == c // 2,
        MIDDLE: z == c,
        PLACE: jnp.where(z <= c, x, 1 - x),
    }
    meta = jnp.zeros((8,), jnp.int32)
    for index, value in values.items():
        meta = jnp.where(slot == index, value.astype(jnp.int32), meta)

    across = lambda block: routed(block, lambda r, c: (r, c ^ 2))
    beside = lambda block: routed(block, lambda r, c: (r, c ^ 1))
    over_x = lambda block: routed(block, lambda r, c: (r ^ 1, c))
    over_z = lambda block: routed(block, lambda r, c: (r ^ 2, c))
    over_far = lambda block: routed(block, lambda r, c: (r ^ 4, c))
    to_near = lambda block: routed(block, lambda r, c: None if is_near(r, c) else (r ^ 4, c))
    back_near = lambda block: routed(block, near_target)
    back_far = lambda block: routed(block, far_target)

    next_t = beside(t)
    next_v = beside(v)
    send, keep = {}, {}
    base = middle_part(meta, t, v, 1, 0)
    send["n", 0] = next_part(meta, base, next_t, next_v, t, v, 1, 0)
    for side, chunks in NEAR_GROUPS:
        blocks = near_parts(meta, next_t, next_v, t, v, side, chunks)
        for k, block in zip(chunks, blocks):
            (send if side else keep)["n", k] = block
    for tag, side, first, count in FAR_GROUPS:
        piece = pick(meta, t, v, side, first, count)
        piece = across(piece)
        other = beside(piece)
        blocks = far_parts(meta, piece, other, t, v, side)
        for i, block in enumerate(blocks):
            (send if side else keep)["f", first + i] = block
    total, come = {}, {}
    for tag in "nf":
        for k in range(CHUNKS):
            key = tag, k
            arrived = over_x(send[key])
            leave, stay = fold(meta, keep[key], arrived)
            arrived = over_z(leave)
            total[key] = add(meta, stay, arrived)
            come[key] = (to_near if tag == "n" else over_far)(total[key])

    def joined(tag, chunks):
        return join(meta, [total[tag, k] for k in chunks], [come[tag, k] for k in chunks])

    near_own, extra = joined("n", range(CHUNKS))
    near_back = back_near(near_own)
    far_own, far_back = [], []
    for chunks in ((0, 1), (2,), (3,)):
        far_own += joined("f", chunks)
        far_back.append(back_far(far_own[-1]))
    new, res = most(
        meta, t, near_own, near_back, extra, *far_own, *far_back[:2], t, v, row_gap, col_gap
    )
    return last(meta, far_back[2], new, res, t, v, row_gap, col_gap)


NEAR_GROUPS = ((1, (1, 2, 3)), (0, (0, 1, 2, 3)))
FAR_GROUPS = (("s0", 1, 0, 2), ("k0", 0, 0, 2), ("s1", 1, 2, 2), ("k1", 0, 2, 1), ("k2", 0, 3, 1))


def gap_slices(shape, occ_energy, vir_energy):
    tile_rows, tile_cols = shape
    gaps = (vir_energy[None, :] - occ_energy[:, None]).reshape(-1)
    row_gap = lax.dynamic_slice_in_dim(gaps, lax.axis_index("row") * tile_rows, tile_rows, 0)
    col_gap = lax.dynamic_slice_in_dim(gaps, lax.axis_index("col") * tile_cols, tile_cols, 0)
    return row_gap[:, None], col_gap[None, :]


def split_local(amplitudes, interaction, occ_energy, vir_energy):
    gaps = gap_slices(amplitudes.shape, occ_energy, vir_energy)
    return tuple(split_update(amplitudes, interaction, *gaps))


def general_local(amplitudes, interaction, occ_energy, vir_energy):
    row_gap, col_gap = gap_slices(amplitudes.shape, occ_energy, vir_energy)
    denom = row_gap + col_gap
    residual = interaction + general_sum(amplitudes, interaction) + denom * amplitudes
    updated = amplitudes - residual / denom
    return (updated, residual)


def solution(mesh):
    rows, cols = mesh.shape["row"], mesh.shape["col"]
    split = cols == 4 and rows == 2 * cols
    return jax.shard_map(
        split_local if split else general_local,
        mesh=mesh,
        in_specs=(P("row", "col"), P("row", "col"), P(), P()),
        out_specs=(P("row", "col"), P("row", "col")),
        check_vma=False,
    )
```

```python
import functools

import jax
import jax.numpy as jnp
from jax import lax
from jax.experimental import pallas as pl
from jax.experimental.pallas import tpu as pltpu
from jax.sharding import PartitionSpec as P


CHUNKS = 4
PAD = 8


def swapped(block, axis, distance):
    count = lax.axis_size(axis)
    route = []
    for low in range(count):
        high = low | 1 << distance
        if high != low and high < count:
            route += [(low, high), (high, low)]
    return lax.ppermute(block, axis, route)


def from_behind(block, axis, distance):
    devices = range(lax.axis_size(axis))
    route = [(i - distance, i) for i in devices if i - distance in devices]
    return lax.ppermute(block, axis, route)


def contract(left_tile, right_tile):
    right_panel = lax.all_gather(right_tile, "row", axis=0, tiled=True)
    return jnp.dot(
        lax.all_gather(left_tile, "col", axis=1, tiled=True),
        right_panel,
        precision=lax.Precision.HIGHEST,
        preferred_element_type=jnp.float32,
    )


def diagonal_tile(tile, row_place, col_place):
    tile_rows = tile.shape[0]
    col_count = lax.axis_size("col")
    ratio = lax.axis_size("row") // col_count
    ratio_bits = ratio.bit_length() - 1
    row_bits = lax.axis_size("row").bit_length() - 1
    blocks = tile.reshape(tile_rows, ratio, tile_rows).transpose(1, 2, 0)
    for bit_index in range(row_bits):
        row_flag = row_place // 2**bit_index % 2
        if bit_index < ratio_bits:
            lower = 2**bit_index
            grouped = blocks.reshape(ratio // (2 * lower), 2, lower, tile_rows, tile_rows)
            zero_half = grouped[:, 0]
            one_half = grouped[:, 1]
            outgoing = jnp.where(row_flag == 0, one_half, zero_half)
            incoming = swapped(outgoing, "row", bit_index)
            new_zero = jnp.where(row_flag == 1, incoming, zero_half)
            new_one = jnp.where(row_flag == 0, incoming, one_half)
            blocks = jnp.stack([new_zero, new_one], axis=1).reshape(ratio, tile_rows, tile_rows)
        else:
            col_flag = col_place // 2 ** (bit_index - ratio_bits) % 2
            stride = 2**bit_index * col_count - 2 ** (bit_index - ratio_bits)
            from_above = from_behind(blocks, ("row", "col"), -stride)
            from_below = from_behind(blocks, ("row", "col"), stride)
            incoming = jnp.where(row_flag == 0, from_above, from_below)
            blocks = jnp.where(row_flag != col_flag, incoming, blocks)
    return blocks.transpose(1, 0, 2).reshape(tile_rows, ratio * tile_rows)


def general_sum(amplitudes, interaction):
    product = contract(amplitudes, interaction)
    mirrored = diagonal_tile(product, lax.axis_index("row"), lax.axis_index("col"))
    return product + mirrored


def routed(block, target):
    rows, cols = lax.axis_size("row"), lax.axis_size("col")
    route = []
    for r in range(rows):
        for c in range(cols):
            place = target(r, c)
            if place is not None:
                route.append((r * cols + c, place[0] * cols + place[1]))
    return lax.ppermute(block, ("row", "col"), route)


def is_near(r, c):
    return r >> 2 == c >> 1


def flipped(z, x, c):
    return x if z < c else 1 - x


def near_target(r, c):
    z, x = r >> 1, r & 1
    if not is_near(r, c):
        return None
    if z == c:
        return (r ^ 1, c)
    return (2 * c + flipped(z, x, c), z)


def far_target(r, c):
    z, x = r >> 1, r & 1
    if not is_near(r, c):
        return None
    return (2 * c + flipped(z ^ 2, x, c), z ^ 2)


X_PLACE, ODD, TURN_1, TURN_2, NEAR, MIDDLE, PLACE = range(7)
VMEM = 40 * 2**20


def params():
    return pltpu.CompilerParams(vmem_limit_bytes=VMEM)


def zeros(count):
    return (0,) * count


def call(kernel, shapes, meta, args, in_specs=None, out_specs=None, scratch=(), aliases=None):
    if in_specs is None:
        in_specs = [None] * len(args)
    if out_specs is None:
        out_specs = [None] * len(shapes)
    whole = lambda a: pl.BlockSpec(a.shape, lambda i, m: zeros(len(a.shape)))
    return pl.pallas_call(
        kernel,
        out_shape=list(shapes),
        grid_spec=pltpu.PrefetchScalarGridSpec(
            num_scalar_prefetch=1,
            grid=(1,),
            in_specs=[s or whole(a) for s, a in zip(in_specs, args)],
            out_specs=[s or whole(a) for s, a in zip(out_specs, shapes)],
            scratch_shapes=list(scratch),
        ),
        input_output_aliases=aliases or {},
        compiler_params=params(),
    )(meta, *args)


def shaped(*shape):
    return jax.ShapeDtypeStruct(shape, jnp.float32)


def halves(value):
    high = value.astype(jnp.bfloat16)
    return high, (value - high.astype(jnp.float32)).astype(jnp.bfloat16)


def joined_left(t_high, t_low, v_high, v_low):
    return jnp.concatenate([t_high, t_high, t_low, v_high, v_high, v_low], axis=1)


def left_of(t, v):
    t_high, t_low = halves(t.T)
    v_high, v_low = halves(v.T)
    return joined_left(t_high, t_low, v_high, v_low)


def own_left(own_ref, cols):
    return joined_left(*(own_ref[i, :, cols].T for i in range(4)))


def own_right(own_ref, cols):
    return jnp.concatenate([own_ref[i, :, cols] for i in (2, 3, 2, 0, 1, 0)], axis=0)


def crossed(left, right):
    return jnp.dot(left, right, preferred_element_type=jnp.float32)


def placed(place, n, offset=0, size=None):
    return pl.ds(pl.multiple_of(place * n + offset, 128), size or n)


def pick_kernel(side, first, m, t_ref, v_ref, out_ref, sems):
    n = t_ref.shape[0]
    cols = placed(m[X_PLACE] ^ side, n, first, out_ref.shape[2])
    copies = [
        pltpu.make_async_copy(ref.at[:, cols], out_ref.at[i], sems.at[i])
        for i, ref in enumerate((t_ref, v_ref))
    ]
    for copy in copies:
        copy.start()
    for copy in copies:
        copy.wait()


def pick(meta, t, v, side, first, count):
    n = t.shape[0]
    w = n // CHUNKS
    hbm = pl.BlockSpec(memory_space=pltpu.MemorySpace.HBM)
    return call(
        functools.partial(pick_kernel, side, first * w),
        [shaped(2, n, count * w)],
        meta,
        [t, v],
        in_specs=[hbm, hbm],
        scratch=[pltpu.SemaphoreType.DMA((2,))],
    )[0]


def prep_kernel(_, t_ref, v_ref, own_ref):
    own_ref[0], own_ref[1] = halves(t_ref[...])
    own_ref[2], own_ref[3] = halves(v_ref[...])


def prep(meta, t, v):
    return call(prep_kernel, [jax.ShapeDtypeStruct((4, *t.shape), jnp.bfloat16)], meta, [t, v])[0]


def middle_block(m, side, chunks, own_ref, outs):
    n = own_ref.shape[1]
    w = n // CHUNKS
    half = m[X_PLACE] ^ side
    left = own_left(own_ref, placed(half, n, chunks[0] * w, len(chunks) * w))
    diagonal = crossed(left, own_right(own_ref, placed(half, n)))
    aside = crossed(left, own_right(own_ref, placed(1 - half, n)))
    lane = lax.broadcasted_iota(jnp.int32, (w, n), 1)
    for i, (k, out_ref) in enumerate(zip(chunks, outs)):
        line = lax.broadcasted_iota(jnp.int32, (w, n), 0) + k * w
        rows = slice(i * w, (i + 1) * w)
        out_ref[0, :w, :] = jnp.where(line >= lane, diagonal[rows], aside[rows])
        extra = jnp.sum(jnp.where(line == lane, aside[rows], 0.0), axis=0, keepdims=True)
        out_ref[0, w:, :] = jnp.broadcast_to(extra, (PAD, n))


def middle_kernel(side, k, m, own_ref, out_ref):
    middle_block(m, side, (k,), own_ref, [out_ref])


def middle_part(meta, own, side, k):
    n = own.shape[1]
    w = n // CHUNKS
    return call(
        functools.partial(middle_kernel, side, k),
        [shaped(2, w + PAD, n)],
        meta,
        [own],
        out_specs=[pl.BlockSpec((1, w + PAD, n), lambda i, m: (0, 0, 0))],
    )[0]


def next_part(meta, base, at, av, own, side, k):
    n = own.shape[1]
    w = n // CHUNKS
    block = pl.BlockSpec((n, w), lambda i, m: (0, (m[X_PLACE] ^ side) * CHUNKS + k))
    return call(
        functools.partial(next_kernel_blocked, side),
        [shaped(*base.shape)],
        meta,
        [base, at, av, own],
        in_specs=[pl.BlockSpec(memory_space=pl.ANY), block, block, None],
        out_specs=[pl.BlockSpec((1, w + PAD, n), lambda i, m: (1, 0, 0))],
        aliases={1: 0},
    )[0]


def next_kernel_blocked(side, m, _, at_ref, av_ref, own_ref, out_ref):
    n = own_ref.shape[1]
    w = at_ref.shape[1]
    right = own_right(own_ref, placed(m[TURN_1] ^ side, n))
    out_ref[0, :w, :] = crossed(left_of(at_ref[...], av_ref[...]), right)
    out_ref[0, w:, :] = jnp.zeros((PAD, n), jnp.float32)


def near_parts(meta, at, av, own, side, chunks):
    n = own.shape[1]
    w = n // CHUNKS
    half = pl.BlockSpec((n, n), lambda i, m: (0, m[X_PLACE] ^ side))
    return call(
        functools.partial(near_half_kernel, side, chunks),
        [shaped(2, w + PAD, n) for _ in chunks],
        meta,
        [at, av, own],
        in_specs=[half, half, None],
    )


def near_half_kernel(side, chunks, m, at_ref, av_ref, own_ref, *outs):
    n = own_ref.shape[1]
    w = n // CHUNKS
    middle_block(m, side, chunks, own_ref, outs)
    cols = slice(chunks[0] * w, (chunks[-1] + 1) * w)
    right = own_right(own_ref, placed(m[TURN_1] ^ side, n))
    block = crossed(left_of(at_ref[:, cols], av_ref[:, cols]), right)
    for i, out_ref in enumerate(outs):
        out_ref[1, :w, :] = block[i * w : (i + 1) * w]
        out_ref[1, w:, :] = jnp.zeros((PAD, n), jnp.float32)


def far_kernel(side, m, a_ref, b_ref, own_ref, *outs):
    n = own_ref.shape[1]
    w = outs[0].shape[1]
    count = len(outs)
    right = own_right(own_ref, placed(m[TURN_2] ^ side, n))
    left = jnp.concatenate([left_of(ref[0], ref[1]) for ref in (a_ref, b_ref)], axis=0)
    block = crossed(left, right)
    for d in range(2):
        for i, out_ref in enumerate(outs):
            first = (d * count + i) * w
            out_ref[d] = block[first : first + w]


def far_parts(meta, a, b, own, side):
    n = own.shape[1]
    w = n // CHUNKS
    return call(
        functools.partial(far_kernel, side),
        [shaped(2, w, n)] * (a.shape[2] // w),
        meta,
        [a, b, own],
    )


def fold_kernel(_, keep_pass, come_pass, keep_stay, come_stay, pass_ref, stay_ref):
    pass_ref[...] = keep_pass[0] + come_pass[0]
    stay_ref[...] = keep_stay[0] + come_stay[0]


def fold(meta, keep, come):
    _, lines, n = keep.shape
    leave = pl.BlockSpec((1, lines, n), lambda i, m: (1 - m[ODD], 0, 0))
    stay = pl.BlockSpec((1, lines, n), lambda i, m: (m[ODD], 0, 0))
    return call(
        fold_kernel,
        [shaped(lines, n)] * 2,
        meta,
        [keep, come, keep, come],
        in_specs=[leave, leave, stay, stay],
    )


def add_kernel(_, a_ref, b_ref, out_ref):
    out_ref[...] = a_ref[...] + b_ref[...]


def add(meta, a, b):
    return call(add_kernel, [shaped(*a.shape)], meta, [a, b])[0]


def join_kernel(w, count, _, *refs):
    out_ref = refs[2 * count]
    extra = None
    for k in range(count):
        a_ref, b_ref = refs[k], refs[count + k]
        out_ref[k * w : (k + 1) * w, :] = a_ref[:w, :] + b_ref[:w, :]
        if a_ref.shape[0] > w:
            pad = a_ref[w:, :] + b_ref[w:, :]
            extra = pad if extra is None else extra + pad
    if extra is not None:
        refs[2 * count + 1][...] = extra


def join(meta, parts, comes):
    n = parts[0].shape[1]
    w = n // CHUNKS
    shapes = [shaped(len(parts) * w, n)]
    if parts[0].shape[0] > w:
        shapes.append(shaped(PAD, n))
    return call(functools.partial(join_kernel, w, len(parts)), shapes, meta, [*parts, *comes])


def closing(t, v, row, col, value):
    denom = row + col
    residual = v + value + denom * t
    return t - residual / denom, residual


def most_kernel(m, *refs):
    near_own, near_back, extra_ref, far_own, far_back = refs[:5]
    t_ref, v_ref, row_ref, col_ref, new_ref, res_ref = refs[5:]
    n = t_ref.shape[0]
    place = m[PLACE]

    def write(count, half, value):
        rows = pl.ds(0, count)
        new_ref[rows, half], res_ref[rows, half] = closing(
            t_ref[rows, half], v_ref[rows, half], row_ref[rows, :], col_ref[:, half], value
        )

    @pl.when(m[NEAR] == 0)
    def _():
        count = far_own.shape[0]
        write(count, placed(place, n), far_own[...])
        write(n, placed(1 - place, n, 0, count), far_back[...].T)

    @pl.when((m[NEAR] == 1) & (m[MIDDLE] == 0))
    def _():
        write(n, placed(place, n), near_own[...])
        write(n, placed(1 - place, n), near_back[...].T)

    @pl.when(m[MIDDLE] == 1)
    def _():
        line = lax.broadcasted_iota(jnp.int32, (n, n), 0)
        lane = lax.broadcasted_iota(jnp.int32, (n, n), 1)
        own = near_own[...]
        write(n, placed(place, n), jnp.where(line >= lane, own, own.T))
        lower = jnp.where(line > lane, near_back[...].T, extra_ref[:1, :])
        write(n, placed(1 - place, n), jnp.where(line < lane, own, lower))


def most(meta, t, *args):
    return call(most_kernel, [shaped(*t.shape)] * 2, meta, args)


def late_kernel(turned, m, value_ref, new_in, res_in, t_ref, v_ref, row_ref, col_ref, new_ref, res_ref):
    @pl.when(m[NEAR] == 1)
    def _():
        new_ref[...] = new_in[...]
        res_ref[...] = res_in[...]

    @pl.when(m[NEAR] == 0)
    def _():
        value = value_ref[...].T if turned else value_ref[...]
        new_ref[...], res_ref[...] = closing(
            t_ref[...], v_ref[...], row_ref[...], col_ref[...], value
        )


def late(meta, turned, chunk, value, new, res, t, v, row_gap, col_gap):
    w, n = value.shape
    if turned:
        at = lambda i, m: (0, (1 - m[PLACE]) * CHUNKS + chunk)
        block = pl.BlockSpec((n, w), at)
        row, col = None, pl.BlockSpec((1, w), at)
    else:
        at = lambda i, m: (chunk, m[PLACE])
        block = pl.BlockSpec((w, n), at)
        row = pl.BlockSpec((w, 1), lambda i, m: (chunk, 0))
        col = pl.BlockSpec((1, n), lambda i, m: (0, m[PLACE]))
    return call(
        functools.partial(late_kernel, turned),
        [shaped(*t.shape)] * 2,
        meta,
        [value, new, res, t, v, row_gap, col_gap],
        in_specs=[None, block, block, block, block, row, col],
        out_specs=[block, block],
        aliases={2: 0, 3: 1},
    )


def split_update(t, v, row_gap, col_gap):
    r = lax.axis_index("row")
    c = lax.axis_index("col")
    z, x = r // 2, r % 2
    slot = lax.iota(jnp.int32, 8)
    values = {
        X_PLACE: x,
        ODD: (z + c) % 2,
        TURN_1: jnp.where(c % 2 == 1, x, 1 - x),
        TURN_2: jnp.where(c // 2 == 1, x, 1 - x),
        NEAR: r // 4 == c // 2,
        MIDDLE: z == c,
        PLACE: jnp.where(z <= c, x, 1 - x),
    }
    meta = jnp.zeros((8,), jnp.int32)
    for index, value in values.items():
        meta = jnp.where(slot == index, value.astype(jnp.int32), meta)

    across = lambda block: routed(block, lambda r, c: (r, c ^ 2))
    beside = lambda block: routed(block, lambda r, c: (r, c ^ 1))
    over_x = lambda block: routed(block, lambda r, c: (r ^ 1, c))
    over_z = lambda block: routed(block, lambda r, c: (r ^ 2, c))
    over_far = lambda block: routed(block, lambda r, c: (r ^ 4, c))
    to_near = lambda block: routed(block, lambda r, c: None if is_near(r, c) else (r ^ 4, c))
    back_near = lambda block: routed(block, near_target)
    back_far = lambda block: routed(block, far_target)

    next_t = beside(t)
    next_v = beside(v)
    own = prep(meta, t, v)
    send, keep = {}, {}
    base = middle_part(meta, own, 1, 0)
    send["n", 0] = next_part(meta, base, next_t, next_v, own, 1, 0)
    for side, chunks in NEAR_GROUPS:
        blocks = near_parts(meta, next_t, next_v, own, side, chunks)
        for k, block in zip(chunks, blocks):
            (send if side else keep)["n", k] = block
    for tag, side, first, count in FAR_GROUPS:
        piece = pick(meta, t, v, side, first, count)
        piece = across(piece)
        other = beside(piece)
        blocks = far_parts(meta, piece, other, own, side)
        for i, block in enumerate(blocks):
            (send if side else keep)["f", first + i] = block
    total, come = {}, {}
    for tag in "nf":
        for k in range(CHUNKS):
            key = tag, k
            arrived = over_x(send[key])
            leave, stay = fold(meta, keep[key], arrived)
            arrived = over_z(leave)
            total[key] = add(meta, stay, arrived)
            come[key] = (to_near if tag == "n" else over_far)(total[key])

    def joined(tag, chunks):
        return join(meta, [total[tag, k] for k in chunks], [come[tag, k] for k in chunks])

    near_own, extra = joined("n", range(CHUNKS))
    near_back = back_near(near_own)
    far_own, far_back = [], []
    for chunks in ((0, 1), (2,), (3,)):
        far_own += joined("f", chunks)
        far_back.append(back_far(far_own[-1]))
    fixed = (t, v, row_gap, col_gap)
    pair = most(meta, t, near_own, near_back, extra, far_own[0], far_back[0], *fixed)
    for i in (1, 2):
        pair = late(meta, False, i + 1, far_own[i], *pair, *fixed)
        pair = late(meta, True, i + 1, far_back[i], *pair, *fixed)
    return pair


NEAR_GROUPS = ((1, (1, 2, 3)), (0, (0,)), (0, (1, 2, 3)))
FAR_GROUPS = (("s0", 1, 0, 2), ("k0", 0, 0, 2), ("s1", 1, 2, 2), ("k1", 0, 2, 1), ("k2", 0, 3, 1))


def gap_slices(shape, occ_energy, vir_energy):
    tile_rows, tile_cols = shape
    gaps = (vir_energy[None, :] - occ_energy[:, None]).reshape(-1)
    row_gap = lax.dynamic_slice_in_dim(gaps, lax.axis_index("row") * tile_rows, tile_rows, 0)
    col_gap = lax.dynamic_slice_in_dim(gaps, lax.axis_index("col") * tile_cols, tile_cols, 0)
    return row_gap[:, None], col_gap[None, :]


def split_local(amplitudes, interaction, occ_energy, vir_energy):
    gaps = gap_slices(amplitudes.shape, occ_energy, vir_energy)
    return tuple(split_update(amplitudes, interaction, *gaps))


def general_local(amplitudes, interaction, occ_energy, vir_energy):
    row_gap, col_gap = gap_slices(amplitudes.shape, occ_energy, vir_energy)
    denom = row_gap + col_gap
    residual = interaction + general_sum(amplitudes, interaction) + denom * amplitudes
    updated = amplitudes - residual / denom
    return (updated, residual)


def solution(mesh):
    rows, cols = mesh.shape["row"], mesh.shape["col"]
    split = cols == 4 and rows == 2 * cols
    return jax.shard_map(
        split_local if split else general_local,
        mesh=mesh,
        in_specs=(P("row", "col"), P("row", "col"), P(), P()),
        out_specs=(P("row", "col"), P("row", "col")),
        check_vma=False,
    )
```

```python
import functools

import jax
import jax.numpy as jnp
from jax import lax
from jax.experimental import pallas as pl
from jax.experimental.pallas import tpu as pltpu
from jax.sharding import PartitionSpec as P


CHUNKS = 4
PAD = 8


def swapped(block, axis, distance):
    count = lax.axis_size(axis)
    route = []
    for low in range(count):
        high = low | 1 << distance
        if high != low and high < count:
            route += [(low, high), (high, low)]
    return lax.ppermute(block, axis, route)


def from_behind(block, axis, distance):
    devices = range(lax.axis_size(axis))
    route = [(i - distance, i) for i in devices if i - distance in devices]
    return lax.ppermute(block, axis, route)


def contract(left_tile, right_tile):
    right_panel = lax.all_gather(right_tile, "row", axis=0, tiled=True)
    return jnp.dot(
        lax.all_gather(left_tile, "col", axis=1, tiled=True),
        right_panel,
        precision=lax.Precision.HIGHEST,
        preferred_element_type=jnp.float32,
    )


def diagonal_tile(tile, row_place, col_place):
    tile_rows = tile.shape[0]
    col_count = lax.axis_size("col")
    ratio = lax.axis_size("row") // col_count
    ratio_bits = ratio.bit_length() - 1
    row_bits = lax.axis_size("row").bit_length() - 1
    blocks = tile.reshape(tile_rows, ratio, tile_rows).transpose(1, 2, 0)
    for bit_index in range(row_bits):
        row_flag = row_place // 2**bit_index % 2
        if bit_index < ratio_bits:
            lower = 2**bit_index
            grouped = blocks.reshape(ratio // (2 * lower), 2, lower, tile_rows, tile_rows)
            zero_half = grouped[:, 0]
            one_half = grouped[:, 1]
            outgoing = jnp.where(row_flag == 0, one_half, zero_half)
            incoming = swapped(outgoing, "row", bit_index)
            new_zero = jnp.where(row_flag == 1, incoming, zero_half)
            new_one = jnp.where(row_flag == 0, incoming, one_half)
            blocks = jnp.stack([new_zero, new_one], axis=1).reshape(ratio, tile_rows, tile_rows)
        else:
            col_flag = col_place // 2 ** (bit_index - ratio_bits) % 2
            stride = 2**bit_index * col_count - 2 ** (bit_index - ratio_bits)
            from_above = from_behind(blocks, ("row", "col"), -stride)
            from_below = from_behind(blocks, ("row", "col"), stride)
            incoming = jnp.where(row_flag == 0, from_above, from_below)
            blocks = jnp.where(row_flag != col_flag, incoming, blocks)
    return blocks.transpose(1, 0, 2).reshape(tile_rows, ratio * tile_rows)


def general_sum(amplitudes, interaction):
    product = contract(amplitudes, interaction)
    mirrored = diagonal_tile(product, lax.axis_index("row"), lax.axis_index("col"))
    return product + mirrored


def routed(block, target):
    rows, cols = lax.axis_size("row"), lax.axis_size("col")
    route = []
    for r in range(rows):
        for c in range(cols):
            place = target(r, c)
            if place is not None:
                route.append((r * cols + c, place[0] * cols + place[1]))
    return lax.ppermute(block, ("row", "col"), route)


def is_near(r, c):
    return r >> 2 == c >> 1


def flipped(z, x, c):
    return x if z < c else 1 - x


def near_target(r, c):
    z, x = r >> 1, r & 1
    if not is_near(r, c):
        return None
    if z == c:
        return (r ^ 1, c)
    return (2 * c + flipped(z, x, c), z)


def far_target(r, c):
    z, x = r >> 1, r & 1
    if not is_near(r, c):
        return None
    return (2 * c + flipped(z ^ 2, x, c), z ^ 2)


X_PLACE, ODD, TURN_1, TURN_2, NEAR, MIDDLE, PLACE = range(7)
VMEM = 40 * 2**20


def params():
    return pltpu.CompilerParams(vmem_limit_bytes=VMEM)


def zeros(count):
    return (0,) * count


def call(kernel, shapes, meta, args, in_specs=None, out_specs=None, scratch=(), aliases=None):
    if in_specs is None:
        in_specs = [None] * len(args)
    if out_specs is None:
        out_specs = [None] * len(shapes)
    whole = lambda a: pl.BlockSpec(a.shape, lambda i, m: zeros(len(a.shape)))
    return pl.pallas_call(
        kernel,
        out_shape=list(shapes),
        grid_spec=pltpu.PrefetchScalarGridSpec(
            num_scalar_prefetch=1,
            grid=(1,),
            in_specs=[s or whole(a) for s, a in zip(in_specs, args)],
            out_specs=[s or whole(a) for s, a in zip(out_specs, shapes)],
            scratch_shapes=list(scratch),
        ),
        input_output_aliases=aliases or {},
        compiler_params=params(),
    )(meta, *args)


def shaped(*shape):
    return jax.ShapeDtypeStruct(shape, jnp.float32)


def halves(value):
    high = value.astype(jnp.bfloat16)
    return high, (value - high.astype(jnp.float32)).astype(jnp.bfloat16)


def joined_left(t_high, t_low, v_high, v_low):
    return jnp.concatenate([t_high, t_high, t_low, v_high, v_high, v_low], axis=1)


def left_of(t, v):
    t_high, t_low = halves(t.T)
    v_high, v_low = halves(v.T)
    return joined_left(t_high, t_low, v_high, v_low)


def own_left(own_ref, cols):
    return joined_left(*(own_ref[i, :, cols].T for i in range(4)))


def own_right(own_ref, cols):
    return jnp.concatenate([own_ref[i, :, cols] for i in (2, 3, 2, 0, 1, 0)], axis=0)


def crossed(left, right):
    return jnp.dot(left, right, preferred_element_type=jnp.float32)


def placed(place, n, offset=0, size=None):
    return pl.ds(pl.multiple_of(place * n + offset, 128), size or n)


def pick_kernel(side, first, m, t_ref, v_ref, out_ref, sems):
    n = t_ref.shape[0]
    cols = placed(m[X_PLACE] ^ side, n, first, out_ref.shape[2])
    copies = [
        pltpu.make_async_copy(ref.at[:, cols], out_ref.at[i], sems.at[i])
        for i, ref in enumerate((t_ref, v_ref))
    ]
    for copy in copies:
        copy.start()
    for copy in copies:
        copy.wait()


def pick(meta, t, v, side, first, count):
    n = t.shape[0]
    w = n // CHUNKS
    hbm = pl.BlockSpec(memory_space=pltpu.MemorySpace.HBM)
    return call(
        functools.partial(pick_kernel, side, first * w),
        [shaped(2, n, count * w)],
        meta,
        [t, v],
        in_specs=[hbm, hbm],
        scratch=[pltpu.SemaphoreType.DMA((2,))],
    )[0]


def prep_kernel(_, t_ref, v_ref, own_ref):
    own_ref[0], own_ref[1] = halves(t_ref[...])
    own_ref[2], own_ref[3] = halves(v_ref[...])


def prep(meta, t, v):
    return call(prep_kernel, [jax.ShapeDtypeStruct((4, *t.shape), jnp.bfloat16)], meta, [t, v])[0]


def middle_block(m, side, chunks, own_ref, outs):
    n = own_ref.shape[1]
    w = n // CHUNKS
    half = m[X_PLACE] ^ side
    left = own_left(own_ref, placed(half, n, chunks[0] * w, len(chunks) * w))
    diagonal = crossed(left, own_right(own_ref, placed(half, n)))
    aside = crossed(left, own_right(own_ref, placed(1 - half, n)))
    lane = lax.broadcasted_iota(jnp.int32, (w, n), 1)
    for i, (k, out_ref) in enumerate(zip(chunks, outs)):
        line = lax.broadcasted_iota(jnp.int32, (w, n), 0) + k * w
        rows = slice(i * w, (i + 1) * w)
        out_ref[0, :w, :] = jnp.where(line >= lane, diagonal[rows], aside[rows])
        extra = jnp.sum(jnp.where(line == lane, aside[rows], 0.0), axis=0, keepdims=True)
        out_ref[0, w:, :] = jnp.broadcast_to(extra, (PAD, n))


def middle_kernel(side, k, m, own_ref, out_ref):
    middle_block(m, side, (k,), own_ref, [out_ref])


def middle_part(meta, own, side, k):
    n = own.shape[1]
    w = n // CHUNKS
    return call(
        functools.partial(middle_kernel, side, k),
        [shaped(2, w + PAD, n)],
        meta,
        [own],
        out_specs=[pl.BlockSpec((1, w + PAD, n), lambda i, m: (0, 0, 0))],
    )[0]


def next_part(meta, base, at, av, own, side, k):
    n = own.shape[1]
    w = n // CHUNKS
    block = pl.BlockSpec((n, w), lambda i, m: (0, (m[X_PLACE] ^ side) * CHUNKS + k))
    return call(
        functools.partial(next_kernel_blocked, side),
        [shaped(*base.shape)],
        meta,
        [base, at, av, own],
        in_specs=[pl.BlockSpec(memory_space=pl.ANY), block, block, None],
        out_specs=[pl.BlockSpec((1, w + PAD, n), lambda i, m: (1, 0, 0))],
        aliases={1: 0},
    )[0]


def next_kernel_blocked(side, m, _, at_ref, av_ref, own_ref, out_ref):
    n = own_ref.shape[1]
    w = at_ref.shape[1]
    right = own_right(own_ref, placed(m[TURN_1] ^ side, n))
    out_ref[0, :w, :] = crossed(left_of(at_ref[...], av_ref[...]), right)
    out_ref[0, w:, :] = jnp.zeros((PAD, n), jnp.float32)


def near_parts(meta, at, av, own, side, chunks):
    n = own.shape[1]
    w = n // CHUNKS
    half = pl.BlockSpec((n, n), lambda i, m: (0, m[X_PLACE] ^ side))
    return call(
        functools.partial(near_half_kernel, side, chunks),
        [shaped(2, w + PAD, n) for _ in chunks],
        meta,
        [at, av, own],
        in_specs=[half, half, None],
    )


def near_half_kernel(side, chunks, m, at_ref, av_ref, own_ref, *outs):
    n = own_ref.shape[1]
    w = n // CHUNKS
    middle_block(m, side, chunks, own_ref, outs)
    cols = slice(chunks[0] * w, (chunks[-1] + 1) * w)
    right = own_right(own_ref, placed(m[TURN_1] ^ side, n))
    block = crossed(left_of(at_ref[:, cols], av_ref[:, cols]), right)
    for i, out_ref in enumerate(outs):
        out_ref[1, :w, :] = block[i * w : (i + 1) * w]
        out_ref[1, w:, :] = jnp.zeros((PAD, n), jnp.float32)


def far_kernel(side, m, a_ref, b_ref, own_ref, *outs):
    n = own_ref.shape[1]
    w = outs[0].shape[1]
    count = len(outs)
    right = own_right(own_ref, placed(m[TURN_2] ^ side, n))
    left = jnp.concatenate([left_of(ref[0], ref[1]) for ref in (a_ref, b_ref)], axis=0)
    block = crossed(left, right)
    for d in range(2):
        for i, out_ref in enumerate(outs):
            first = (d * count + i) * w
            out_ref[d] = block[first : first + w]


def far_parts(meta, a, b, own, side):
    n = own.shape[1]
    w = n // CHUNKS
    return call(
        functools.partial(far_kernel, side),
        [shaped(2, w, n)] * (a.shape[2] // w),
        meta,
        [a, b, own],
    )


def fold_kernel(_, keep_pass, come_pass, keep_stay, come_stay, pass_ref, stay_ref):
    pass_ref[...] = keep_pass[0] + come_pass[0]
    stay_ref[...] = keep_stay[0] + come_stay[0]


def fold(meta, keep, come):
    _, lines, n = keep.shape
    leave = pl.BlockSpec((1, lines, n), lambda i, m: (1 - m[ODD], 0, 0))
    stay = pl.BlockSpec((1, lines, n), lambda i, m: (m[ODD], 0, 0))
    return call(
        fold_kernel,
        [shaped(lines, n)] * 2,
        meta,
        [keep, come, keep, come],
        in_specs=[leave, leave, stay, stay],
    )


def add_kernel(_, a_ref, b_ref, out_ref):
    out_ref[...] = a_ref[...] + b_ref[...]


def add(meta, a, b):
    return call(add_kernel, [shaped(*a.shape)], meta, [a, b])[0]


def join_kernel(w, count, _, *refs):
    out_ref = refs[2 * count]
    extra = None
    for k in range(count):
        a_ref, b_ref = refs[k], refs[count + k]
        out_ref[k * w : (k + 1) * w, :] = a_ref[:w, :] + b_ref[:w, :]
        if a_ref.shape[0] > w:
            pad = a_ref[w:, :] + b_ref[w:, :]
            extra = pad if extra is None else extra + pad
    if extra is not None:
        refs[2 * count + 1][...] = extra


def join(meta, parts, comes):
    n = parts[0].shape[1]
    w = n // CHUNKS
    shapes = [shaped(len(parts) * w, n)]
    if parts[0].shape[0] > w:
        shapes.append(shaped(PAD, n))
    return call(functools.partial(join_kernel, w, len(parts)), shapes, meta, [*parts, *comes])


def closing(t, v, row, col, value):
    denom = row + col
    residual = v + value + denom * t
    return t - residual / denom, residual


def most_kernel(m, *refs):
    near_own, near_back, extra_ref = refs[:3]
    far_own, far_back = refs[3:5], refs[5:7]
    t_ref, v_ref, row_ref, col_ref, new_ref, res_ref = refs[7:]
    n = t_ref.shape[0]
    place = m[PLACE]

    def write(first, count, half, value):
        rows = pl.ds(first, count)
        new_ref[rows, half], res_ref[rows, half] = closing(
            t_ref[rows, half], v_ref[rows, half], row_ref[rows, :], col_ref[:, half], value
        )

    @pl.when(m[NEAR] == 0)
    def _():
        first = 0
        for own_ref, back_ref in zip(far_own, far_back):
            count = own_ref.shape[0]
            write(first, count, placed(place, n), own_ref[...])
            write(0, n, placed(1 - place, n, first, count), back_ref[...].T)
            first += count

    @pl.when((m[NEAR] == 1) & (m[MIDDLE] == 0))
    def _():
        write(0, n, placed(place, n), near_own[...])
        write(0, n, placed(1 - place, n), near_back[...].T)

    @pl.when(m[MIDDLE] == 1)
    def _():
        line = lax.broadcasted_iota(jnp.int32, (n, n), 0)
        lane = lax.broadcasted_iota(jnp.int32, (n, n), 1)
        own = near_own[...]
        write(0, n, placed(place, n), jnp.where(line >= lane, own, own.T))
        lower = jnp.where(line > lane, near_back[...].T, extra_ref[:1, :])
        write(0, n, placed(1 - place, n), jnp.where(line < lane, own, lower))


def most(meta, t, *args):
    return call(most_kernel, [shaped(*t.shape)] * 2, meta, args)


def late_kernel(turned, m, value_ref, _, __, t_ref, v_ref, row_ref, col_ref, new_ref, res_ref, new, res, sems):
    n, w = max(value_ref.shape), min(value_ref.shape)

    @pl.when(m[NEAR] == 0)
    def _():
        value = value_ref[...].T if turned else value_ref[...]
        new[...], res[...] = closing(
            t_ref[...], v_ref[...], row_ref[...], col_ref[...], value
        )
        if turned:
            rows, cols = pl.ds(0, n), placed(1 - m[PLACE], n, n - w, w)
        else:
            rows, cols = pl.ds(n - w, w), placed(m[PLACE], n)
        copies = [
            pltpu.make_async_copy(source, target.at[rows, cols], sems.at[i])
            for i, (source, target) in enumerate(((new, new_ref), (res, res_ref)))
        ]
        for copy in copies:
            copy.start()
        for copy in copies:
            copy.wait()


def late(meta, turned, value, new, res, t, v, row_gap, col_gap):
    w, n = value.shape
    if turned:
        at = lambda i, m: (0, (2 - m[PLACE]) * CHUNKS - 1)
        block = pl.BlockSpec((n, w), at)
        row, col = None, pl.BlockSpec((1, w), at)
    else:
        block = pl.BlockSpec((w, n), lambda i, m: (CHUNKS - 1, m[PLACE]))
        row = pl.BlockSpec((w, 1), lambda i, m: (CHUNKS - 1, 0))
        col = pl.BlockSpec((1, n), lambda i, m: (0, m[PLACE]))
    hbm = pl.BlockSpec(memory_space=pl.ANY)
    return call(
        functools.partial(late_kernel, turned),
        [shaped(*t.shape)] * 2,
        meta,
        [value, new, res, t, v, row_gap, col_gap],
        in_specs=[None, hbm, hbm, block, block, row, col],
        out_specs=[hbm, hbm],
        scratch=[pltpu.VMEM(block.block_shape, jnp.float32)] * 2 + [pltpu.SemaphoreType.DMA((2,))],
        aliases={2: 0, 3: 1},
    )


def split_update(t, v, row_gap, col_gap):
    r = lax.axis_index("row")
    c = lax.axis_index("col")
    z, x = r // 2, r % 2
    slot = lax.iota(jnp.int32, 8)
    values = {
        X_PLACE: x,
        ODD: (z + c) % 2,
        TURN_1: jnp.where(c % 2 == 1, x, 1 - x),
        TURN_2: jnp.where(c // 2 == 1, x, 1 - x),
        NEAR: r // 4 == c // 2,
        MIDDLE: z == c,
        PLACE: jnp.where(z <= c, x, 1 - x),
    }
    meta = jnp.zeros((8,), jnp.int32)
    for index, value in values.items():
        meta = jnp.where(slot == index, value.astype(jnp.int32), meta)

    across = lambda block: routed(block, lambda r, c: (r, c ^ 2))
    beside = lambda block: routed(block, lambda r, c: (r, c ^ 1))
    over_x = lambda block: routed(block, lambda r, c: (r ^ 1, c))
    over_z = lambda block: routed(block, lambda r, c: (r ^ 2, c))
    over_far = lambda block: routed(block, lambda r, c: (r ^ 4, c))
    to_near = lambda block: routed(block, lambda r, c: None if is_near(r, c) else (r ^ 4, c))
    back_near = lambda block: routed(block, near_target)
    back_far = lambda block: routed(block, far_target)

    next_t = beside(t)
    next_v = beside(v)
    own = prep(meta, t, v)
    send, keep = {}, {}
    base = middle_part(meta, own, 1, 0)
    send["n", 0] = next_part(meta, base, next_t, next_v, own, 1, 0)
    for side, chunks in NEAR_GROUPS:
        blocks = near_parts(meta, next_t, next_v, own, side, chunks)
        for k, block in zip(chunks, blocks):
            (send if side else keep)["n", k] = block
    for tag, side, first, count in FAR_GROUPS:
        piece = pick(meta, t, v, side, first, count)
        piece = across(piece)
        other = beside(piece)
        blocks = far_parts(meta, piece, other, own, side)
        for i, block in enumerate(blocks):
            (send if side else keep)["f", first + i] = block
    total, come = {}, {}
    for tag in "nf":
        for k in range(CHUNKS):
            key = tag, k
            arrived = over_x(send[key])
            leave, stay = fold(meta, keep[key], arrived)
            arrived = over_z(leave)
            total[key] = add(meta, stay, arrived)
            come[key] = (to_near if tag == "n" else over_far)(total[key])

    def joined(tag, chunks):
        return join(meta, [total[tag, k] for k in chunks], [come[tag, k] for k in chunks])

    near_own, extra = joined("n", range(CHUNKS))
    near_back = back_near(near_own)
    far_own, far_back = [], []
    for chunks in ((0, 1), (2,), (3,)):
        far_own += joined("f", chunks)
        far_back.append(back_far(far_own[-1]))
    fixed = (t, v, row_gap, col_gap)
    pair = most(meta, t, near_own, near_back, extra, *far_own[:2], *far_back[:2], *fixed)
    pair = late(meta, False, far_own[2], *pair, *fixed)
    return late(meta, True, far_back[2], *pair, *fixed)


NEAR_GROUPS = ((1, (1, 2, 3)), (0, (0,)), (0, (1, 2, 3)))
FAR_GROUPS = (("s0", 1, 0, 2), ("k0", 0, 0, 2), ("s1", 1, 2, 2), ("k1", 0, 2, 1), ("k2", 0, 3, 1))


def gap_slices(shape, occ_energy, vir_energy):
    tile_rows, tile_cols = shape
    gaps = (vir_energy[None, :] - occ_energy[:, None]).reshape(-1)
    row_gap = lax.dynamic_slice_in_dim(gaps, lax.axis_index("row") * tile_rows, tile_rows, 0)
    col_gap = lax.dynamic_slice_in_dim(gaps, lax.axis_index("col") * tile_cols, tile_cols, 0)
    return row_gap[:, None], col_gap[None, :]


def split_local(amplitudes, interaction, occ_energy, vir_energy):
    gaps = gap_slices(amplitudes.shape, occ_energy, vir_energy)
    return tuple(split_update(amplitudes, interaction, *gaps))


def general_local(amplitudes, interaction, occ_energy, vir_energy):
    row_gap, col_gap = gap_slices(amplitudes.shape, occ_energy, vir_energy)
    denom = row_gap + col_gap
    residual = interaction + general_sum(amplitudes, interaction) + denom * amplitudes
    updated = amplitudes - residual / denom
    return (updated, residual)


def solution(mesh):
    rows, cols = mesh.shape["row"], mesh.shape["col"]
    split = cols == 4 and rows == 2 * cols
    return jax.shard_map(
        split_local if split else general_local,
        mesh=mesh,
        in_specs=(P("row", "col"), P("row", "col"), P(), P()),
        out_specs=(P("row", "col"), P("row", "col")),
        check_vma=False,
    )
```

```python
import functools

import jax
import jax.numpy as jnp
from jax import lax
from jax.experimental import pallas as pl
from jax.experimental.pallas import tpu as pltpu
from jax.sharding import PartitionSpec as P


CHUNKS = 4
PAD = 8


def swapped(block, axis, distance):
    count = lax.axis_size(axis)
    route = []
    for low in range(count):
        high = low | 1 << distance
        if high != low and high < count:
            route += [(low, high), (high, low)]
    return lax.ppermute(block, axis, route)


def from_behind(block, axis, distance):
    devices = range(lax.axis_size(axis))
    route = [(i - distance, i) for i in devices if i - distance in devices]
    return lax.ppermute(block, axis, route)


def contract(left_tile, right_tile):
    right_panel = lax.all_gather(right_tile, "row", axis=0, tiled=True)
    return jnp.dot(
        lax.all_gather(left_tile, "col", axis=1, tiled=True),
        right_panel,
        precision=lax.Precision.HIGHEST,
        preferred_element_type=jnp.float32,
    )


def diagonal_tile(tile, row_place, col_place):
    tile_rows = tile.shape[0]
    col_count = lax.axis_size("col")
    ratio = lax.axis_size("row") // col_count
    ratio_bits = ratio.bit_length() - 1
    row_bits = lax.axis_size("row").bit_length() - 1
    blocks = tile.reshape(tile_rows, ratio, tile_rows).transpose(1, 2, 0)
    for bit_index in range(row_bits):
        row_flag = row_place // 2**bit_index % 2
        if bit_index < ratio_bits:
            lower = 2**bit_index
            grouped = blocks.reshape(ratio // (2 * lower), 2, lower, tile_rows, tile_rows)
            zero_half = grouped[:, 0]
            one_half = grouped[:, 1]
            outgoing = jnp.where(row_flag == 0, one_half, zero_half)
            incoming = swapped(outgoing, "row", bit_index)
            new_zero = jnp.where(row_flag == 1, incoming, zero_half)
            new_one = jnp.where(row_flag == 0, incoming, one_half)
            blocks = jnp.stack([new_zero, new_one], axis=1).reshape(ratio, tile_rows, tile_rows)
        else:
            col_flag = col_place // 2 ** (bit_index - ratio_bits) % 2
            stride = 2**bit_index * col_count - 2 ** (bit_index - ratio_bits)
            from_above = from_behind(blocks, ("row", "col"), -stride)
            from_below = from_behind(blocks, ("row", "col"), stride)
            incoming = jnp.where(row_flag == 0, from_above, from_below)
            blocks = jnp.where(row_flag != col_flag, incoming, blocks)
    return blocks.transpose(1, 0, 2).reshape(tile_rows, ratio * tile_rows)


def general_sum(amplitudes, interaction):
    product = contract(amplitudes, interaction)
    mirrored = diagonal_tile(product, lax.axis_index("row"), lax.axis_index("col"))
    return product + mirrored


def routed(block, target):
    rows, cols = lax.axis_size("row"), lax.axis_size("col")
    route = []
    for r in range(rows):
        for c in range(cols):
            place = target(r, c)
            if place is not None:
                route.append((r * cols + c, place[0] * cols + place[1]))
    return lax.ppermute(block, ("row", "col"), route)


def is_near(r, c):
    return r >> 2 == c >> 1


def flips(z, c):
    return (z > c) ^ ((z ^ c) == 3)


def flipped(z, x, c):
    return x ^ flips(z, c)


def near_target(r, c):
    z, x = r >> 1, r & 1
    if not is_near(r, c):
        return None
    if z == c:
        return (r ^ 1, c)
    return (2 * c + flipped(z, x, c), z)


def far_target(r, c):
    z, x = r >> 1, r & 1
    if not is_near(r, c):
        return None
    return (2 * c + flipped(z ^ 2, x, c), z ^ 2)


X_PLACE, ODD, TURN_1, TURN_2, TURN_3, NEAR, MIDDLE, PLACE = range(8)
VMEM = 40 * 2**20


def params():
    return pltpu.CompilerParams(vmem_limit_bytes=VMEM)


def zeros(count):
    return (0,) * count


def call(kernel, shapes, meta, args, in_specs=None, out_specs=None, scratch=(), aliases=None):
    if in_specs is None:
        in_specs = [None] * len(args)
    if out_specs is None:
        out_specs = [None] * len(shapes)
    whole = lambda a: pl.BlockSpec(a.shape, lambda i, m: zeros(len(a.shape)))
    return pl.pallas_call(
        kernel,
        out_shape=list(shapes),
        grid_spec=pltpu.PrefetchScalarGridSpec(
            num_scalar_prefetch=1,
            grid=(1,),
            in_specs=[s or whole(a) for s, a in zip(in_specs, args)],
            out_specs=[s or whole(a) for s, a in zip(out_specs, shapes)],
            scratch_shapes=list(scratch),
        ),
        input_output_aliases=aliases or {},
        compiler_params=params(),
    )(meta, *args)


def shaped(*shape):
    return jax.ShapeDtypeStruct(shape, jnp.float32)


def halves(value):
    high = value.astype(jnp.bfloat16)
    return high, (value - high.astype(jnp.float32)).astype(jnp.bfloat16)


def joined_left(t_high, t_low, v_high, v_low):
    return jnp.concatenate([t_high, t_high, t_low, v_high, v_high, v_low], axis=1)


def left_of(t, v):
    t_high, t_low = halves(t.T)
    v_high, v_low = halves(v.T)
    return joined_left(t_high, t_low, v_high, v_low)


def own_left(own_ref, cols):
    return joined_left(*(own_ref[i, :, cols].T for i in range(4)))


def own_right(own_ref, cols):
    return jnp.concatenate([own_ref[i, :, cols] for i in (2, 3, 2, 0, 1, 0)], axis=0)


def crossed(left, right):
    return jnp.dot(left, right, preferred_element_type=jnp.float32)


def placed(place, n, offset=0, size=None):
    return pl.ds(pl.multiple_of(place * n + offset, 128), size or n)


def pick_kernel(side, first, m, t_ref, v_ref, out_ref, sems):
    n = t_ref.shape[0]
    cols = placed(m[X_PLACE] ^ side, n, first, out_ref.shape[2])
    copies = [
        pltpu.make_async_copy(ref.at[:, cols], out_ref.at[i], sems.at[i])
        for i, ref in enumerate((t_ref, v_ref))
    ]
    for copy in copies:
        copy.start()
    for copy in copies:
        copy.wait()


def pick(meta, t, v, side, first, count):
    n = t.shape[0]
    w = n // CHUNKS
    hbm = pl.BlockSpec(memory_space=pltpu.MemorySpace.HBM)
    return call(
        functools.partial(pick_kernel, side, first * w),
        [shaped(2, n, count * w)],
        meta,
        [t, v],
        in_specs=[hbm, hbm],
        scratch=[pltpu.SemaphoreType.DMA((2,))],
    )[0]


def prep_kernel(_, t_ref, v_ref, own_ref):
    own_ref[0], own_ref[1] = halves(t_ref[...])
    own_ref[2], own_ref[3] = halves(v_ref[...])


def prep(meta, t, v):
    return call(prep_kernel, [jax.ShapeDtypeStruct((4, *t.shape), jnp.bfloat16)], meta, [t, v])[0]


def middle_block(m, side, chunks, own_ref, outs):
    n = own_ref.shape[1]
    w = n // CHUNKS
    half = m[X_PLACE] ^ side
    left = own_left(own_ref, placed(half, n, chunks[0] * w, len(chunks) * w))
    diagonal = crossed(left, own_right(own_ref, placed(half, n)))
    aside = crossed(left, own_right(own_ref, placed(1 - half, n)))
    lane = lax.broadcasted_iota(jnp.int32, (w, n), 1)
    for i, (k, out_ref) in enumerate(zip(chunks, outs)):
        line = lax.broadcasted_iota(jnp.int32, (w, n), 0) + k * w
        rows = slice(i * w, (i + 1) * w)
        out_ref[0, :w, :] = jnp.where(line >= lane, diagonal[rows], aside[rows])
        extra = jnp.sum(jnp.where(line == lane, aside[rows], 0.0), axis=0, keepdims=True)
        out_ref[0, w:, :] = jnp.broadcast_to(extra, (PAD, n))


def middle_kernel(side, k, m, own_ref, out_ref):
    middle_block(m, side, (k,), own_ref, [out_ref])


def middle_part(meta, own, side, k):
    n = own.shape[1]
    w = n // CHUNKS
    return call(
        functools.partial(middle_kernel, side, k),
        [shaped(2, w + PAD, n)],
        meta,
        [own],
        out_specs=[pl.BlockSpec((1, w + PAD, n), lambda i, m: (0, 0, 0))],
    )[0]


def next_part(meta, base, at, av, own, side, k):
    n = own.shape[1]
    w = n // CHUNKS
    block = pl.BlockSpec((n, w), lambda i, m: (0, (m[X_PLACE] ^ side) * CHUNKS + k))
    return call(
        functools.partial(next_kernel_blocked, side),
        [shaped(*base.shape)],
        meta,
        [base, at, av, own],
        in_specs=[pl.BlockSpec(memory_space=pl.ANY), block, block, None],
        out_specs=[pl.BlockSpec((1, w + PAD, n), lambda i, m: (1, 0, 0))],
        aliases={1: 0},
    )[0]


def next_kernel_blocked(side, m, _, at_ref, av_ref, own_ref, out_ref):
    n = own_ref.shape[1]
    w = at_ref.shape[1]
    right = own_right(own_ref, placed(m[TURN_1] ^ side, n))
    out_ref[0, :w, :] = crossed(left_of(at_ref[...], av_ref[...]), right)
    out_ref[0, w:, :] = jnp.zeros((PAD, n), jnp.float32)


def near_parts(meta, at, av, own, side, chunks):
    n = own.shape[1]
    w = n // CHUNKS
    half = pl.BlockSpec((n, n), lambda i, m: (0, m[X_PLACE] ^ side))
    return call(
        functools.partial(near_half_kernel, side, chunks),
        [shaped(2, w + PAD, n) for _ in chunks],
        meta,
        [at, av, own],
        in_specs=[half, half, None],
    )


def near_half_kernel(side, chunks, m, at_ref, av_ref, own_ref, *outs):
    n = own_ref.shape[1]
    w = n // CHUNKS
    middle_block(m, side, chunks, own_ref, outs)
    cols = slice(chunks[0] * w, (chunks[-1] + 1) * w)
    right = own_right(own_ref, placed(m[TURN_1] ^ side, n))
    block = crossed(left_of(at_ref[:, cols], av_ref[:, cols]), right)
    for i, out_ref in enumerate(outs):
        out_ref[1, :w, :] = block[i * w : (i + 1) * w]
        out_ref[1, w:, :] = jnp.zeros((PAD, n), jnp.float32)


def far_kernel(side, m, a_ref, b_ref, own_ref, *outs):
    n = own_ref.shape[1]
    w = outs[0].shape[1]
    for d, (ref, turn) in enumerate(((a_ref, TURN_2), (b_ref, TURN_3))):
        right = own_right(own_ref, placed(m[turn] ^ side, n))
        block = crossed(left_of(ref[0], ref[1]), right)
        for i, out_ref in enumerate(outs):
            out_ref[d] = block[i * w : (i + 1) * w]


def far_parts(meta, a, b, own, side):
    n = own.shape[1]
    w = n // CHUNKS
    return call(
        functools.partial(far_kernel, side),
        [shaped(2, w, n)] * (a.shape[2] // w),
        meta,
        [a, b, own],
    )


def fold_kernel(_, keep_pass, come_pass, keep_stay, come_stay, pass_ref, stay_ref):
    pass_ref[...] = keep_pass[0] + come_pass[0]
    stay_ref[...] = keep_stay[0] + come_stay[0]


def fold(meta, keep, come):
    _, lines, n = keep.shape
    leave = pl.BlockSpec((1, lines, n), lambda i, m: (1 - m[ODD], 0, 0))
    stay = pl.BlockSpec((1, lines, n), lambda i, m: (m[ODD], 0, 0))
    return call(
        fold_kernel,
        [shaped(lines, n)] * 2,
        meta,
        [keep, come, keep, come],
        in_specs=[leave, leave, stay, stay],
    )


def add_kernel(_, a_ref, b_ref, out_ref):
    out_ref[...] = a_ref[...] + b_ref[...]


def add(meta, a, b):
    return call(add_kernel, [shaped(*a.shape)], meta, [a, b])[0]


def join_kernel(w, count, _, *refs):
    out_ref = refs[2 * count]
    extra = None
    for k in range(count):
        a_ref, b_ref = refs[k], refs[count + k]
        out_ref[k * w : (k + 1) * w, :] = a_ref[:w, :] + b_ref[:w, :]
        if a_ref.shape[0] > w:
            pad = a_ref[w:, :] + b_ref[w:, :]
            extra = pad if extra is None else extra + pad
    if extra is not None:
        refs[2 * count + 1][...] = extra


def join(meta, parts, comes):
    n = parts[0].shape[1]
    w = n // CHUNKS
    shapes = [shaped(len(parts) * w, n)]
    if parts[0].shape[0] > w:
        shapes.append(shaped(PAD, n))
    return call(functools.partial(join_kernel, w, len(parts)), shapes, meta, [*parts, *comes])


def closing(t, v, row, col, value):
    denom = row + col
    residual = v + value + denom * t
    return t - residual / denom, residual


def most_kernel(m, *refs):
    near_own, near_back, extra_ref = refs[:3]
    far_own, far_back = refs[3:5], refs[5:7]
    t_ref, v_ref, row_ref, col_ref, new_ref, res_ref = refs[7:]
    n = t_ref.shape[0]
    place = m[PLACE]

    def write(first, count, half, value):
        rows = pl.ds(first, count)
        new_ref[rows, half], res_ref[rows, half] = closing(
            t_ref[rows, half], v_ref[rows, half], row_ref[rows, :], col_ref[:, half], value
        )

    @pl.when(m[NEAR] == 0)
    def _():
        first = 0
        for own_ref, back_ref in zip(far_own, far_back):
            count = own_ref.shape[0]
            write(first, count, placed(place, n), own_ref[...])
            write(0, n, placed(1 - place, n, first, count), back_ref[...].T)
            first += count

    @pl.when((m[NEAR] == 1) & (m[MIDDLE] == 0))
    def _():
        write(0, n, placed(place, n), near_own[...])
        write(0, n, placed(1 - place, n), near_back[...].T)

    @pl.when(m[MIDDLE] == 1)
    def _():
        line = lax.broadcasted_iota(jnp.int32, (n, n), 0)
        lane = lax.broadcasted_iota(jnp.int32, (n, n), 1)
        own = near_own[...]
        write(0, n, placed(place, n), jnp.where(line >= lane, own, own.T))
        lower = jnp.where(line > lane, near_back[...].T, extra_ref[:1, :])
        write(0, n, placed(1 - place, n), jnp.where(line < lane, own, lower))


def most(meta, t, *args):
    return call(most_kernel, [shaped(*t.shape)] * 2, meta, args)


def late_kernel(turned, m, value_ref, _, __, t_ref, v_ref, row_ref, col_ref, new_ref, res_ref, new, res, sems):
    n, w = max(value_ref.shape), min(value_ref.shape)

    @pl.when(m[NEAR] == 0)
    def _():
        value = value_ref[...].T if turned else value_ref[...]
        new[...], res[...] = closing(
            t_ref[...], v_ref[...], row_ref[...], col_ref[...], value
        )
        if turned:
            rows, cols = pl.ds(0, n), placed(1 - m[PLACE], n, n - w, w)
        else:
            rows, cols = pl.ds(n - w, w), placed(m[PLACE], n)
        copies = [
            pltpu.make_async_copy(source, target.at[rows, cols], sems.at[i])
            for i, (source, target) in enumerate(((new, new_ref), (res, res_ref)))
        ]
        for copy in copies:
            copy.start()
        for copy in copies:
            copy.wait()


def late(meta, turned, value, new, res, t, v, row_gap, col_gap):
    w, n = value.shape
    if turned:
        at = lambda i, m: (0, (2 - m[PLACE]) * CHUNKS - 1)
        block = pl.BlockSpec((n, w), at)
        row, col = None, pl.BlockSpec((1, w), at)
    else:
        block = pl.BlockSpec((w, n), lambda i, m: (CHUNKS - 1, m[PLACE]))
        row = pl.BlockSpec((w, 1), lambda i, m: (CHUNKS - 1, 0))
        col = pl.BlockSpec((1, n), lambda i, m: (0, m[PLACE]))
    hbm = pl.BlockSpec(memory_space=pl.ANY)
    return call(
        functools.partial(late_kernel, turned),
        [shaped(*t.shape)] * 2,
        meta,
        [value, new, res, t, v, row_gap, col_gap],
        in_specs=[None, hbm, hbm, block, block, row, col],
        out_specs=[hbm, hbm],
        scratch=[pltpu.VMEM(block.block_shape, jnp.float32)] * 2 + [pltpu.SemaphoreType.DMA((2,))],
        aliases={2: 0, 3: 1},
    )


def split_update(t, v, row_gap, col_gap):
    r = lax.axis_index("row")
    c = lax.axis_index("col")
    z, x = r // 2, r % 2
    slot = lax.iota(jnp.int32, 8)
    values = {
        X_PLACE: x,
        ODD: (z + c) % 2,
        TURN_1: x ^ flips(c ^ 1, c),
        TURN_2: x ^ flips(c ^ 2, c),
        TURN_3: x ^ flips(c ^ 3, c),
        NEAR: r // 4 == c // 2,
        MIDDLE: z == c,
        PLACE: x ^ flips(z, c),
    }
    meta = jnp.zeros((8,), jnp.int32)
    for index, value in values.items():
        meta = jnp.where(slot == index, value.astype(jnp.int32), meta)

    across = lambda block: routed(block, lambda r, c: (r, c ^ 2))
    beside = lambda block: routed(block, lambda r, c: (r, c ^ 1))
    over_x = lambda block: routed(block, lambda r, c: (r ^ 1, c))
    over_z = lambda block: routed(block, lambda r, c: (r ^ 2, c))
    over_far = lambda block: routed(block, lambda r, c: (r ^ 4, c))
    to_near = lambda block: routed(block, lambda r, c: None if is_near(r, c) else (r ^ 4, c))
    back_near = lambda block: routed(block, near_target)
    back_far = lambda block: routed(block, far_target)

    next_t = beside(t)
    next_v = beside(v)
    own = prep(meta, t, v)
    send, keep = {}, {}
    base = middle_part(meta, own, 1, 0)
    send["n", 0] = next_part(meta, base, next_t, next_v, own, 1, 0)
    for side, chunks in NEAR_GROUPS:
        blocks = near_parts(meta, next_t, next_v, own, side, chunks)
        for k, block in zip(chunks, blocks):
            (send if side else keep)["n", k] = block
    for tag, side, first, count in FAR_GROUPS:
        piece = pick(meta, t, v, side, first, count)
        piece = across(piece)
        other = beside(piece)
        blocks = far_parts(meta, piece, other, own, side)
        for i, block in enumerate(blocks):
            (send if side else keep)["f", first + i] = block
    total, come = {}, {}
    for tag in "nf":
        for k in range(CHUNKS):
            key = tag, k
            arrived = over_x(send[key])
            leave, stay = fold(meta, keep[key], arrived)
            arrived = over_z(leave)
            total[key] = add(meta, stay, arrived)
            come[key] = (to_near if tag == "n" else over_far)(total[key])

    def joined(tag, chunks):
        return join(meta, [total[tag, k] for k in chunks], [come[tag, k] for k in chunks])

    near_own, extra = joined("n", range(CHUNKS))
    near_back = back_near(near_own)
    far_own, far_back = [], []
    for chunks in ((0, 1), (2,), (3,)):
        far_own += joined("f", chunks)
        far_back.append(back_far(far_own[-1]))
    fixed = (t, v, row_gap, col_gap)
    pair = most(meta, t, near_own, near_back, extra, *far_own[:2], *far_back[:2], *fixed)
    pair = late(meta, False, far_own[2], *pair, *fixed)
    return late(meta, True, far_back[2], *pair, *fixed)


NEAR_GROUPS = ((1, (1, 2, 3)), (0, (0,)), (0, (1, 2, 3)))
FAR_GROUPS = (("s0", 1, 0, 2), ("k0", 0, 0, 2), ("s1", 1, 2, 2), ("k1", 0, 2, 2))


def gap_slices(shape, occ_energy, vir_energy):
    tile_rows, tile_cols = shape
    gaps = (vir_energy[None, :] - occ_energy[:, None]).reshape(-1)
    row_gap = lax.dynamic_slice_in_dim(gaps, lax.axis_index("row") * tile_rows, tile_rows, 0)
    col_gap = lax.dynamic_slice_in_dim(gaps, lax.axis_index("col") * tile_cols, tile_cols, 0)
    return row_gap[:, None], col_gap[None, :]


def split_local(amplitudes, interaction, occ_energy, vir_energy):
    gaps = gap_slices(amplitudes.shape, occ_energy, vir_energy)
    return tuple(split_update(amplitudes, interaction, *gaps))


def general_local(amplitudes, interaction, occ_energy, vir_energy):
    row_gap, col_gap = gap_slices(amplitudes.shape, occ_energy, vir_energy)
    denom = row_gap + col_gap
    residual = interaction + general_sum(amplitudes, interaction) + denom * amplitudes
    updated = amplitudes - residual / denom
    return (updated, residual)


def solution(mesh):
    rows, cols = mesh.shape["row"], mesh.shape["col"]
    split = cols == 4 and rows == 2 * cols
    return jax.shard_map(
        split_local if split else general_local,
        mesh=mesh,
        in_specs=(P("row", "col"), P("row", "col"), P(), P()),
        out_specs=(P("row", "col"), P("row", "col")),
        check_vma=False,
    )
```

```python
import functools

import jax
import jax.numpy as jnp
from jax import lax
from jax.experimental import pallas as pl
from jax.experimental.pallas import tpu as pltpu
from jax.sharding import PartitionSpec as P


CHUNKS = 4
PAD = 8


def swapped(block, axis, distance):
    count = lax.axis_size(axis)
    route = []
    for low in range(count):
        high = low | 1 << distance
        if high != low and high < count:
            route += [(low, high), (high, low)]
    return lax.ppermute(block, axis, route)


def from_behind(block, axis, distance):
    devices = range(lax.axis_size(axis))
    route = [(i - distance, i) for i in devices if i - distance in devices]
    return lax.ppermute(block, axis, route)


def contract(left_tile, right_tile):
    right_panel = lax.all_gather(right_tile, "row", axis=0, tiled=True)
    return jnp.dot(
        lax.all_gather(left_tile, "col", axis=1, tiled=True),
        right_panel,
        precision=lax.Precision.HIGHEST,
        preferred_element_type=jnp.float32,
    )


def diagonal_tile(tile, row_place, col_place):
    tile_rows = tile.shape[0]
    col_count = lax.axis_size("col")
    ratio = lax.axis_size("row") // col_count
    ratio_bits = ratio.bit_length() - 1
    row_bits = lax.axis_size("row").bit_length() - 1
    blocks = tile.reshape(tile_rows, ratio, tile_rows).transpose(1, 2, 0)
    for bit_index in range(row_bits):
        row_flag = row_place // 2**bit_index % 2
        if bit_index < ratio_bits:
            lower = 2**bit_index
            grouped = blocks.reshape(ratio // (2 * lower), 2, lower, tile_rows, tile_rows)
            zero_half = grouped[:, 0]
            one_half = grouped[:, 1]
            outgoing = jnp.where(row_flag == 0, one_half, zero_half)
            incoming = swapped(outgoing, "row", bit_index)
            new_zero = jnp.where(row_flag == 1, incoming, zero_half)
            new_one = jnp.where(row_flag == 0, incoming, one_half)
            blocks = jnp.stack([new_zero, new_one], axis=1).reshape(ratio, tile_rows, tile_rows)
        else:
            col_flag = col_place // 2 ** (bit_index - ratio_bits) % 2
            stride = 2**bit_index * col_count - 2 ** (bit_index - ratio_bits)
            from_above = from_behind(blocks, ("row", "col"), -stride)
            from_below = from_behind(blocks, ("row", "col"), stride)
            incoming = jnp.where(row_flag == 0, from_above, from_below)
            blocks = jnp.where(row_flag != col_flag, incoming, blocks)
    return blocks.transpose(1, 0, 2).reshape(tile_rows, ratio * tile_rows)


def general_sum(amplitudes, interaction):
    product = contract(amplitudes, interaction)
    mirrored = diagonal_tile(product, lax.axis_index("row"), lax.axis_index("col"))
    return product + mirrored


def routed(block, target):
    rows, cols = lax.axis_size("row"), lax.axis_size("col")
    route = []
    for r in range(rows):
        for c in range(cols):
            place = target(r, c)
            if place is not None:
                route.append((r * cols + c, place[0] * cols + place[1]))
    return lax.ppermute(block, ("row", "col"), route)


def is_near(r, c):
    return r >> 2 == c >> 1


def flips(z, c):
    return (z > c) ^ ((z ^ c) == 3)


def flipped(z, x, c):
    return x ^ flips(z, c)


def near_target(r, c):
    z, x = r >> 1, r & 1
    if not is_near(r, c):
        return None
    if z == c:
        return (r ^ 1, c)
    return (2 * c + flipped(z, x, c), z)


def far_target(r, c):
    z, x = r >> 1, r & 1
    if not is_near(r, c):
        return None
    return (2 * c + flipped(z ^ 2, x, c), z ^ 2)


X_PLACE, ODD, TURN_1, TURN_2, TURN_3, NEAR, MIDDLE, PLACE = range(8)
VMEM = 40 * 2**20


def params():
    return pltpu.CompilerParams(vmem_limit_bytes=VMEM)


def zeros(count):
    return (0,) * count


def call(kernel, shapes, meta, args, in_specs=None, out_specs=None, scratch=(), aliases=None):
    if in_specs is None:
        in_specs = [None] * len(args)
    if out_specs is None:
        out_specs = [None] * len(shapes)
    whole = lambda a: pl.BlockSpec(a.shape, lambda i, m: zeros(len(a.shape)))
    return pl.pallas_call(
        kernel,
        out_shape=list(shapes),
        grid_spec=pltpu.PrefetchScalarGridSpec(
            num_scalar_prefetch=1,
            grid=(1,),
            in_specs=[s or whole(a) for s, a in zip(in_specs, args)],
            out_specs=[s or whole(a) for s, a in zip(out_specs, shapes)],
            scratch_shapes=list(scratch),
        ),
        input_output_aliases=aliases or {},
        compiler_params=params(),
    )(meta, *args)


def shaped(*shape):
    return jax.ShapeDtypeStruct(shape, jnp.float32)


def halves(value):
    high = value.astype(jnp.bfloat16)
    return high, (value - high.astype(jnp.float32)).astype(jnp.bfloat16)


def joined_left(t_high, t_low, v_high, v_low):
    return jnp.concatenate([t_high, t_high, t_low, v_high, v_high, v_low], axis=1)


def left_of(t, v):
    t_high, t_low = halves(t.T)
    v_high, v_low = halves(v.T)
    return joined_left(t_high, t_low, v_high, v_low)


def own_left(own_ref, cols):
    return joined_left(*(own_ref[i, :, cols].T for i in range(4)))


def own_right(own_ref, cols):
    return jnp.concatenate([own_ref[i, :, cols] for i in (2, 3, 2, 0, 1, 0)], axis=0)


def crossed(left, right):
    return jnp.dot(left, right, preferred_element_type=jnp.float32)


def placed(place, n, offset=0, size=None):
    return pl.ds(pl.multiple_of(place * n + offset, 128), size or n)


def pick_kernel(side, first, m, t_ref, v_ref, out_ref, sems):
    n = t_ref.shape[0]
    cols = placed(m[X_PLACE] ^ side, n, first, out_ref.shape[2])
    copies = [
        pltpu.make_async_copy(ref.at[:, cols], out_ref.at[i], sems.at[i])
        for i, ref in enumerate((t_ref, v_ref))
    ]
    for copy in copies:
        copy.start()
    for copy in copies:
        copy.wait()


def pick(meta, t, v, side, first, count):
    n = t.shape[0]
    w = n // CHUNKS
    hbm = pl.BlockSpec(memory_space=pltpu.MemorySpace.HBM)
    return call(
        functools.partial(pick_kernel, side, first * w),
        [shaped(2, n, count * w)],
        meta,
        [t, v],
        in_specs=[hbm, hbm],
        scratch=[pltpu.SemaphoreType.DMA((2,))],
    )[0]


def prep_kernel(_, t_ref, v_ref, own_ref):
    own_ref[0], own_ref[1] = halves(t_ref[...])
    own_ref[2], own_ref[3] = halves(v_ref[...])


def prep(meta, t, v):
    return call(prep_kernel, [jax.ShapeDtypeStruct((4, *t.shape), jnp.bfloat16)], meta, [t, v])[0]


def middle_block(m, side, chunks, own_ref, outs):
    n = own_ref.shape[1]
    w = n // CHUNKS
    half = m[X_PLACE] ^ side
    left = own_left(own_ref, placed(half, n, chunks[0] * w, len(chunks) * w))
    diagonal = crossed(left, own_right(own_ref, placed(half, n)))
    aside = crossed(left, own_right(own_ref, placed(1 - half, n)))
    lane = lax.broadcasted_iota(jnp.int32, (w, n), 1)
    for i, (k, out_ref) in enumerate(zip(chunks, outs)):
        line = lax.broadcasted_iota(jnp.int32, (w, n), 0) + k * w
        rows = slice(i * w, (i + 1) * w)
        out_ref[0, :w, :] = jnp.where(line >= lane, diagonal[rows], aside[rows])
        extra = jnp.sum(jnp.where(line == lane, aside[rows], 0.0), axis=0, keepdims=True)
        out_ref[0, w:, :] = jnp.broadcast_to(extra, (PAD, n))


def middle_kernel(side, k, m, own_ref, out_ref):
    middle_block(m, side, (k,), own_ref, [out_ref])


def middle_part(meta, own, side, k):
    n = own.shape[1]
    w = n // CHUNKS
    return call(
        functools.partial(middle_kernel, side, k),
        [shaped(2, w + PAD, n)],
        meta,
        [own],
        out_specs=[pl.BlockSpec((1, w + PAD, n), lambda i, m: (0, 0, 0))],
    )[0]


def next_part(meta, base, at, av, own, side, k):
    n = own.shape[1]
    w = n // CHUNKS
    block = pl.BlockSpec((n, w), lambda i, m: (0, (m[X_PLACE] ^ side) * CHUNKS + k))
    return call(
        functools.partial(next_kernel_blocked, side),
        [shaped(*base.shape)],
        meta,
        [base, at, av, own],
        in_specs=[pl.BlockSpec(memory_space=pl.ANY), block, block, None],
        out_specs=[pl.BlockSpec((1, w + PAD, n), lambda i, m: (1, 0, 0))],
        aliases={1: 0},
    )[0]


def next_kernel_blocked(side, m, _, at_ref, av_ref, own_ref, out_ref):
    n = own_ref.shape[1]
    w = at_ref.shape[1]
    right = own_right(own_ref, placed(m[TURN_1] ^ side, n))
    out_ref[0, :w, :] = crossed(left_of(at_ref[...], av_ref[...]), right)
    out_ref[0, w:, :] = jnp.zeros((PAD, n), jnp.float32)


def near_parts(meta, at, av, own, side, chunks):
    n = own.shape[1]
    w = n // CHUNKS
    half = pl.BlockSpec((n, n), lambda i, m: (0, m[X_PLACE] ^ side))
    return call(
        functools.partial(near_half_kernel, side, chunks),
        [shaped(2, w + PAD, n) for _ in chunks],
        meta,
        [at, av, own],
        in_specs=[half, half, None],
    )


def near_half_kernel(side, chunks, m, at_ref, av_ref, own_ref, *outs):
    n = own_ref.shape[1]
    w = n // CHUNKS
    middle_block(m, side, chunks, own_ref, outs)
    cols = slice(chunks[0] * w, (chunks[-1] + 1) * w)
    right = own_right(own_ref, placed(m[TURN_1] ^ side, n))
    block = crossed(left_of(at_ref[:, cols], av_ref[:, cols]), right)
    for i, out_ref in enumerate(outs):
        out_ref[1, :w, :] = block[i * w : (i + 1) * w]
        out_ref[1, w:, :] = jnp.zeros((PAD, n), jnp.float32)


def far_kernel(side, m, a_ref, b_ref, own_ref, *outs):
    n = own_ref.shape[1]
    w = outs[0].shape[1]
    for d, (ref, turn) in enumerate(((a_ref, TURN_2), (b_ref, TURN_3))):
        right = own_right(own_ref, placed(m[turn] ^ side, n))
        block = crossed(left_of(ref[0], ref[1]), right)
        for i, out_ref in enumerate(outs):
            out_ref[d] = block[i * w : (i + 1) * w]


def far_parts(meta, a, b, own, side):
    n = own.shape[1]
    w = n // CHUNKS
    return call(
        functools.partial(far_kernel, side),
        [shaped(2, w, n)] * (a.shape[2] // w),
        meta,
        [a, b, own],
    )


def fold_kernel(_, keep_pass, come_pass, keep_stay, come_stay, pass_ref, stay_ref):
    pass_ref[...] = keep_pass[0] + come_pass[0]
    stay_ref[...] = keep_stay[0] + come_stay[0]


def fold(meta, keep, come):
    _, lines, n = keep.shape
    leave = pl.BlockSpec((1, lines, n), lambda i, m: (1 - m[ODD], 0, 0))
    stay = pl.BlockSpec((1, lines, n), lambda i, m: (m[ODD], 0, 0))
    return call(
        fold_kernel,
        [shaped(lines, n)] * 2,
        meta,
        [keep, come, keep, come],
        in_specs=[leave, leave, stay, stay],
    )


def add_kernel(_, a_ref, b_ref, out_ref):
    out_ref[...] = a_ref[...] + b_ref[...]


def add(meta, a, b):
    return call(add_kernel, [shaped(*a.shape)], meta, [a, b])[0]


def join_kernel(w, count, _, *refs):
    out_ref = refs[2 * count]
    extra = None
    for k in range(count):
        a_ref, b_ref = refs[k], refs[count + k]
        out_ref[k * w : (k + 1) * w, :] = a_ref[:w, :] + b_ref[:w, :]
        if a_ref.shape[0] > w:
            pad = a_ref[w:, :] + b_ref[w:, :]
            extra = pad if extra is None else extra + pad
    if extra is not None:
        refs[2 * count + 1][...] = extra


def join(meta, parts, comes):
    n = parts[0].shape[1]
    w = n // CHUNKS
    shapes = [shaped(len(parts) * w, n)]
    if parts[0].shape[0] > w:
        shapes.append(shaped(PAD, n))
    return call(functools.partial(join_kernel, w, len(parts)), shapes, meta, [*parts, *comes])


def closing(t, v, row, col, value):
    denom = row + col
    residual = v + value + denom * t
    return t - residual / denom, residual


def most_kernel(m, *refs):
    near_own, near_back, extra_ref = refs[:3]
    far_own, far_back = refs[3:4], refs[4:5]
    t_ref, v_ref, row_ref, col_ref, new_ref, res_ref = refs[5:]
    n = t_ref.shape[0]
    place = m[PLACE]

    def write(first, count, half, value):
        rows = pl.ds(first, count)
        new_ref[rows, half], res_ref[rows, half] = closing(
            t_ref[rows, half], v_ref[rows, half], row_ref[rows, :], col_ref[:, half], value
        )

    @pl.when(m[NEAR] == 0)
    def _():
        first = 0
        for own_ref, back_ref in zip(far_own, far_back):
            count = own_ref.shape[0]
            write(first, count, placed(place, n), own_ref[...])
            write(0, n, placed(1 - place, n, first, count), back_ref[...].T)
            first += count

    @pl.when((m[NEAR] == 1) & (m[MIDDLE] == 0))
    def _():
        write(0, n, placed(place, n), near_own[...])
        write(0, n, placed(1 - place, n), near_back[...].T)

    @pl.when(m[MIDDLE] == 1)
    def _():
        line = lax.broadcasted_iota(jnp.int32, (n, n), 0)
        lane = lax.broadcasted_iota(jnp.int32, (n, n), 1)
        own = near_own[...]
        write(0, n, placed(place, n), jnp.where(line >= lane, own, own.T))
        lower = jnp.where(line > lane, near_back[...].T, extra_ref[:1, :])
        write(0, n, placed(1 - place, n), jnp.where(line < lane, own, lower))


def most(meta, t, *args):
    return call(most_kernel, [shaped(*t.shape)] * 2, meta, args)


def late_kernel(turned, chunk, count, m, *refs):
    values = refs[:count]
    t_ref, v_ref, row_ref, col_ref, new_ref, res_ref, new, res, sems = refs[count + 2 :]
    w = min(values[0].shape)
    n = max(values[0].shape)

    @pl.when(m[NEAR] == 0)
    def _():
        parts = [ref[...].T if turned else ref[...] for ref in values]
        value = parts[0] if count == 1 else jnp.concatenate(parts, axis=int(turned))
        new[...], res[...] = closing(
            t_ref[...], v_ref[...], row_ref[...], col_ref[...], value
        )
        if turned:
            rows, cols = pl.ds(0, n), placed(1 - m[PLACE], n, chunk * w, count * w)
        else:
            rows, cols = pl.ds(chunk * w, count * w), placed(m[PLACE], n)
        copies = [
            pltpu.make_async_copy(source, target.at[rows, cols], sems.at[i])
            for i, (source, target) in enumerate(((new, new_ref), (res, res_ref)))
        ]
        for copy in copies:
            copy.start()
        for copy in copies:
            copy.wait()


def late(meta, turned, chunk, values, new, res, t, v, row_gap, col_gap):
    w, n = values[0].shape
    count = len(values)
    if turned:
        at = lambda i, m: (0, ((1 - m[PLACE]) * CHUNKS + chunk) // count)
        block = pl.BlockSpec((n, count * w), at)
        row, col = None, pl.BlockSpec((1, count * w), at)
    else:
        block = pl.BlockSpec((count * w, n), lambda i, m: (chunk // count, m[PLACE]))
        row = pl.BlockSpec((count * w, 1), lambda i, m: (chunk // count, 0))
        col = pl.BlockSpec((1, n), lambda i, m: (0, m[PLACE]))
    hbm = pl.BlockSpec(memory_space=pl.ANY)
    return call(
        functools.partial(late_kernel, turned, chunk, count),
        [shaped(*t.shape)] * 2,
        meta,
        [*values, new, res, t, v, row_gap, col_gap],
        in_specs=[*[None] * count, hbm, hbm, block, block, row, col],
        out_specs=[hbm, hbm],
        scratch=[pltpu.VMEM(block.block_shape, jnp.float32)] * 2 + [pltpu.SemaphoreType.DMA((2,))],
        aliases={count + 1: 0, count + 2: 1},
    )


def split_update(t, v, row_gap, col_gap):
    r = lax.axis_index("row")
    c = lax.axis_index("col")
    z, x = r // 2, r % 2
    slot = lax.iota(jnp.int32, 8)
    values = {
        X_PLACE: x,
        ODD: (z + c) % 2,
        TURN_1: x ^ flips(c ^ 1, c),
        TURN_2: x ^ flips(c ^ 2, c),
        TURN_3: x ^ flips(c ^ 3, c),
        NEAR: r // 4 == c // 2,
        MIDDLE: z == c,
        PLACE: x ^ flips(z, c),
    }
    meta = jnp.zeros((8,), jnp.int32)
    for index, value in values.items():
        meta = jnp.where(slot == index, value.astype(jnp.int32), meta)

    across = lambda block: routed(block, lambda r, c: (r, c ^ 2))
    beside = lambda block: routed(block, lambda r, c: (r, c ^ 1))
    over_x = lambda block: routed(block, lambda r, c: (r ^ 1, c))
    over_z = lambda block: routed(block, lambda r, c: (r ^ 2, c))
    over_far = lambda block: routed(block, lambda r, c: (r ^ 4, c))
    to_near = lambda block: routed(block, lambda r, c: None if is_near(r, c) else (r ^ 4, c))
    back_near = lambda block: routed(block, near_target)
    back_far = lambda block: routed(block, far_target)

    next_t = beside(t)
    next_v = beside(v)
    own = prep(meta, t, v)
    send, keep = {}, {}
    base = middle_part(meta, own, 1, 0)
    send["n", 0] = next_part(meta, base, next_t, next_v, own, 1, 0)
    for side, chunks in NEAR_GROUPS:
        blocks = near_parts(meta, next_t, next_v, own, side, chunks)
        for k, block in zip(chunks, blocks):
            (send if side else keep)["n", k] = block
    for tag, side, first, count in FAR_GROUPS:
        piece = pick(meta, t, v, side, first, count)
        piece = across(piece)
        other = beside(piece)
        blocks = far_parts(meta, piece, other, own, side)
        for i, block in enumerate(blocks):
            (send if side else keep)["f", first + i] = block
    total, come = {}, {}
    for tag in "nf":
        for k in range(CHUNKS):
            key = tag, k
            arrived = over_x(send[key])
            leave, stay = fold(meta, keep[key], arrived)
            arrived = over_z(leave)
            total[key] = add(meta, stay, arrived)
            come[key] = (to_near if tag == "n" else over_far)(total[key])

    def joined(tag, chunks):
        return join(meta, [total[tag, k] for k in chunks], [come[tag, k] for k in chunks])

    near_own, extra = joined("n", range(CHUNKS))
    near_back = back_near(near_own)
    far_own, far_back = [], []
    for chunks in ((0, 1), (2,), (3,)):
        far_own += joined("f", chunks)
        far_back.append(back_far(far_own[-1]))
    fixed = (t, v, row_gap, col_gap)
    pair = most(meta, t, near_own, near_back, extra, far_own[0], far_back[0], *fixed)
    pair = late(meta, False, 2, far_own[1:], *pair, *fixed)
    pair = late(meta, True, 2, far_back[1:2], *pair, *fixed)
    return late(meta, True, 3, far_back[2:], *pair, *fixed)


NEAR_GROUPS = ((1, (1, 2, 3)), (0, (0,)), (0, (1, 2, 3)))
FAR_GROUPS = (("s0", 1, 0, 2), ("k0", 0, 0, 2), ("s1", 1, 2, 2), ("k1", 0, 2, 2))


def gap_slices(shape, occ_energy, vir_energy):
    tile_rows, tile_cols = shape
    gaps = (vir_energy[None, :] - occ_energy[:, None]).reshape(-1)
    row_gap = lax.dynamic_slice_in_dim(gaps, lax.axis_index("row") * tile_rows, tile_rows, 0)
    col_gap = lax.dynamic_slice_in_dim(gaps, lax.axis_index("col") * tile_cols, tile_cols, 0)
    return row_gap[:, None], col_gap[None, :]


def split_local(amplitudes, interaction, occ_energy, vir_energy):
    gaps = gap_slices(amplitudes.shape, occ_energy, vir_energy)
    return tuple(split_update(amplitudes, interaction, *gaps))


def general_local(amplitudes, interaction, occ_energy, vir_energy):
    row_gap, col_gap = gap_slices(amplitudes.shape, occ_energy, vir_energy)
    denom = row_gap + col_gap
    residual = interaction + general_sum(amplitudes, interaction) + denom * amplitudes
    updated = amplitudes - residual / denom
    return (updated, residual)


def solution(mesh):
    rows, cols = mesh.shape["row"], mesh.shape["col"]
    split = cols == 4 and rows == 2 * cols
    return jax.shard_map(
        split_local if split else general_local,
        mesh=mesh,
        in_specs=(P("row", "col"), P("row", "col"), P(), P()),
        out_specs=(P("row", "col"), P("row", "col")),
        check_vma=False,
    )
```

```python
import functools

import jax
import jax.numpy as jnp
from jax import lax
from jax.experimental import pallas as pl
from jax.experimental.pallas import tpu as pltpu
from jax.sharding import PartitionSpec as P


CHUNKS = 4
PAD = 8


def swapped(block, axis, distance):
    count = lax.axis_size(axis)
    route = []
    for low in range(count):
        high = low | 1 << distance
        if high != low and high < count:
            route += [(low, high), (high, low)]
    return lax.ppermute(block, axis, route)


def from_behind(block, axis, distance):
    devices = range(lax.axis_size(axis))
    route = [(i - distance, i) for i in devices if i - distance in devices]
    return lax.ppermute(block, axis, route)


def contract(left_tile, right_tile):
    right_panel = lax.all_gather(right_tile, "row", axis=0, tiled=True)
    return jnp.dot(
        lax.all_gather(left_tile, "col", axis=1, tiled=True),
        right_panel,
        precision=lax.Precision.HIGHEST,
        preferred_element_type=jnp.float32,
    )


def diagonal_tile(tile, row_place, col_place):
    tile_rows = tile.shape[0]
    col_count = lax.axis_size("col")
    ratio = lax.axis_size("row") // col_count
    ratio_bits = ratio.bit_length() - 1
    row_bits = lax.axis_size("row").bit_length() - 1
    blocks = tile.reshape(tile_rows, ratio, tile_rows).transpose(1, 2, 0)
    for bit_index in range(row_bits):
        row_flag = row_place // 2**bit_index % 2
        if bit_index < ratio_bits:
            lower = 2**bit_index
            grouped = blocks.reshape(ratio // (2 * lower), 2, lower, tile_rows, tile_rows)
            zero_half = grouped[:, 0]
            one_half = grouped[:, 1]
            outgoing = jnp.where(row_flag == 0, one_half, zero_half)
            incoming = swapped(outgoing, "row", bit_index)
            new_zero = jnp.where(row_flag == 1, incoming, zero_half)
            new_one = jnp.where(row_flag == 0, incoming, one_half)
            blocks = jnp.stack([new_zero, new_one], axis=1).reshape(ratio, tile_rows, tile_rows)
        else:
            col_flag = col_place // 2 ** (bit_index - ratio_bits) % 2
            stride = 2**bit_index * col_count - 2 ** (bit_index - ratio_bits)
            from_above = from_behind(blocks, ("row", "col"), -stride)
            from_below = from_behind(blocks, ("row", "col"), stride)
            incoming = jnp.where(row_flag == 0, from_above, from_below)
            blocks = jnp.where(row_flag != col_flag, incoming, blocks)
    return blocks.transpose(1, 0, 2).reshape(tile_rows, ratio * tile_rows)


def general_sum(amplitudes, interaction):
    product = contract(amplitudes, interaction)
    mirrored = diagonal_tile(product, lax.axis_index("row"), lax.axis_index("col"))
    return product + mirrored


def routed(block, target):
    rows, cols = lax.axis_size("row"), lax.axis_size("col")
    route = []
    for r in range(rows):
        for c in range(cols):
            place = target(r, c)
            if place is not None:
                route.append((r * cols + c, place[0] * cols + place[1]))
    return lax.ppermute(block, ("row", "col"), route)


def is_near(r, c):
    return r >> 2 == c >> 1


def flips(z, c):
    return (z > c) ^ ((z ^ c) == 3)


def flipped(z, x, c):
    return x ^ flips(z, c)


def swap_target(r, c):
    return (r ^ 1, c) if r >> 1 == c else None


def near_target(r, c):
    z, x = r >> 1, r & 1
    if not is_near(r, c) or z == c:
        return None
    return (2 * c + flipped(z, x, c), z)


def far_target(r, c):
    z, x = r >> 1, r & 1
    if not is_near(r, c):
        return None
    return (2 * c + flipped(z ^ 2, x, c), z ^ 2)


def hop_of(target):
    return lambda r, c: target(r, c) and (r, c ^ 2)


def after_hop(target):
    return lambda r, c: target(r, c ^ 2)


X_PLACE, ODD, TURN_1, TURN_2, TURN_3, NEAR, MIDDLE, PLACE = range(8)
VMEM = 40 * 2**20


def params():
    return pltpu.CompilerParams(vmem_limit_bytes=VMEM)


def zeros(count):
    return (0,) * count


def call(kernel, shapes, meta, args, in_specs=None, out_specs=None, scratch=(), aliases=None):
    if in_specs is None:
        in_specs = [None] * len(args)
    if out_specs is None:
        out_specs = [None] * len(shapes)
    whole = lambda a: pl.BlockSpec(a.shape, lambda i, m: zeros(len(a.shape)))
    return pl.pallas_call(
        kernel,
        out_shape=list(shapes),
        grid_spec=pltpu.PrefetchScalarGridSpec(
            num_scalar_prefetch=1,
            grid=(1,),
            in_specs=[s or whole(a) for s, a in zip(in_specs, args)],
            out_specs=[s or whole(a) for s, a in zip(out_specs, shapes)],
            scratch_shapes=list(scratch),
        ),
        input_output_aliases=aliases or {},
        compiler_params=params(),
    )(meta, *args)


def shaped(*shape):
    return jax.ShapeDtypeStruct(shape, jnp.float32)


def halves(value):
    high = value.astype(jnp.bfloat16)
    return high, (value - high.astype(jnp.float32)).astype(jnp.bfloat16)


def joined_left(t_high, t_low, v_high, v_low):
    return jnp.concatenate([t_high, t_high, t_low, v_high, v_high, v_low], axis=1)


def left_of(t, v):
    t_high, t_low = halves(t.T)
    v_high, v_low = halves(v.T)
    return joined_left(t_high, t_low, v_high, v_low)


def own_left(own_ref, cols):
    return joined_left(*(own_ref[i, :, cols].T for i in range(4)))


def own_right(own_ref, cols):
    return jnp.concatenate([own_ref[i, :, cols] for i in (2, 3, 2, 0, 1, 0)], axis=0)


def crossed(left, right):
    return jnp.dot(left, right, preferred_element_type=jnp.float32)


def placed(place, n, offset=0, size=None):
    return pl.ds(pl.multiple_of(place * n + offset, 128), size or n)


def pick_kernel(side, first, m, t_ref, v_ref, out_ref, sems):
    n = t_ref.shape[0]
    cols = placed(m[X_PLACE] ^ side, n, first, out_ref.shape[2])
    copies = [
        pltpu.make_async_copy(ref.at[:, cols], out_ref.at[i], sems.at[i])
        for i, ref in enumerate((t_ref, v_ref))
    ]
    for copy in copies:
        copy.start()
    for copy in copies:
        copy.wait()


def pick(meta, t, v, side, first, count):
    n = t.shape[0]
    w = n // CHUNKS
    hbm = pl.BlockSpec(memory_space=pltpu.MemorySpace.HBM)
    return call(
        functools.partial(pick_kernel, side, first * w),
        [shaped(2, n, count * w)],
        meta,
        [t, v],
        in_specs=[hbm, hbm],
        scratch=[pltpu.SemaphoreType.DMA((2,))],
    )[0]


def prep_kernel(_, t_ref, v_ref, own_ref):
    own_ref[0], own_ref[1] = halves(t_ref[...])
    own_ref[2], own_ref[3] = halves(v_ref[...])


def prep(meta, t, v):
    return call(prep_kernel, [jax.ShapeDtypeStruct((4, *t.shape), jnp.bfloat16)], meta, [t, v])[0]


def middle_block(m, side, chunks, own_ref, outs):
    n = own_ref.shape[1]
    w = n // CHUNKS
    half = m[X_PLACE] ^ side
    left = own_left(own_ref, placed(half, n, chunks[0] * w, len(chunks) * w))
    diagonal = crossed(left, own_right(own_ref, placed(half, n)))
    aside = crossed(left, own_right(own_ref, placed(1 - half, n)))
    lane = lax.broadcasted_iota(jnp.int32, (w, n), 1)
    for i, (k, out_ref) in enumerate(zip(chunks, outs)):
        line = lax.broadcasted_iota(jnp.int32, (w, n), 0) + k * w
        rows = slice(i * w, (i + 1) * w)
        out_ref[0, :w, :] = jnp.where(line >= lane, diagonal[rows], aside[rows])
        extra = jnp.sum(jnp.where(line == lane, aside[rows], 0.0), axis=0, keepdims=True)
        out_ref[0, w:, :] = jnp.broadcast_to(extra, (PAD, n))


def middle_kernel(side, k, m, own_ref, out_ref):
    middle_block(m, side, (k,), own_ref, [out_ref])


def middle_part(meta, own, side, k):
    n = own.shape[1]
    w = n // CHUNKS
    return call(
        functools.partial(middle_kernel, side, k),
        [shaped(2, w + PAD, n)],
        meta,
        [own],
        out_specs=[pl.BlockSpec((1, w + PAD, n), lambda i, m: (0, 0, 0))],
    )[0]


def next_part(meta, base, at, av, own, side, k):
    n = own.shape[1]
    w = n // CHUNKS
    block = pl.BlockSpec((n, w), lambda i, m: (0, (m[X_PLACE] ^ side) * CHUNKS + k))
    return call(
        functools.partial(next_kernel_blocked, side),
        [shaped(*base.shape)],
        meta,
        [base, at, av, own],
        in_specs=[pl.BlockSpec(memory_space=pl.ANY), block, block, None],
        out_specs=[pl.BlockSpec((1, w + PAD, n), lambda i, m: (1, 0, 0))],
        aliases={1: 0},
    )[0]


def next_kernel_blocked(side, m, _, at_ref, av_ref, own_ref, out_ref):
    n = own_ref.shape[1]
    w = at_ref.shape[1]
    right = own_right(own_ref, placed(m[TURN_1] ^ side, n))
    out_ref[0, :w, :] = crossed(left_of(at_ref[...], av_ref[...]), right)
    out_ref[0, w:, :] = jnp.zeros((PAD, n), jnp.float32)


def near_parts(meta, at, av, own, side, chunks):
    n = own.shape[1]
    w = n // CHUNKS
    half = pl.BlockSpec((n, n), lambda i, m: (0, m[X_PLACE] ^ side))
    return call(
        functools.partial(near_half_kernel, side, chunks),
        [shaped(2, w + PAD, n) for _ in chunks],
        meta,
        [at, av, own],
        in_specs=[half, half, None],
    )


def near_half_kernel(side, chunks, m, at_ref, av_ref, own_ref, *outs):
    n = own_ref.shape[1]
    w = n // CHUNKS
    middle_block(m, side, chunks, own_ref, outs)
    cols = slice(chunks[0] * w, (chunks[-1] + 1) * w)
    right = own_right(own_ref, placed(m[TURN_1] ^ side, n))
    block = crossed(left_of(at_ref[:, cols], av_ref[:, cols]), right)
    for i, out_ref in enumerate(outs):
        out_ref[1, :w, :] = block[i * w : (i + 1) * w]
        out_ref[1, w:, :] = jnp.zeros((PAD, n), jnp.float32)


def far_kernel(side, m, a_ref, b_ref, own_ref, *outs):
    n = own_ref.shape[1]
    w = outs[0].shape[1]
    for d, (ref, turn) in enumerate(((a_ref, TURN_2), (b_ref, TURN_3))):
        right = own_right(own_ref, placed(m[turn] ^ side, n))
        block = crossed(left_of(ref[0], ref[1]), right)
        for i, out_ref in enumerate(outs):
            out_ref[d] = block[i * w : (i + 1) * w]


def far_parts(meta, a, b, own, side):
    n = own.shape[1]
    w = n // CHUNKS
    return call(
        functools.partial(far_kernel, side),
        [shaped(2, w, n)] * (a.shape[2] // w),
        meta,
        [a, b, own],
    )


def fold_kernel(_, keep_pass, come_pass, keep_stay, come_stay, pass_ref, stay_ref):
    pass_ref[...] = keep_pass[0] + come_pass[0]
    stay_ref[...] = keep_stay[0] + come_stay[0]


def fold(meta, keep, come):
    _, lines, n = keep.shape
    leave = pl.BlockSpec((1, lines, n), lambda i, m: (1 - m[ODD], 0, 0))
    stay = pl.BlockSpec((1, lines, n), lambda i, m: (m[ODD], 0, 0))
    return call(
        fold_kernel,
        [shaped(lines, n)] * 2,
        meta,
        [keep, come, keep, come],
        in_specs=[leave, leave, stay, stay],
    )


def add_kernel(_, a_ref, b_ref, out_ref):
    out_ref[...] = a_ref[...] + b_ref[...]


def add(meta, a, b):
    return call(add_kernel, [shaped(*a.shape)], meta, [a, b])[0]


def join_kernel(w, count, _, *refs):
    out_ref = refs[2 * count]
    extra = None
    for k in range(count):
        a_ref, b_ref = refs[k], refs[count + k]
        out_ref[k * w : (k + 1) * w, :] = a_ref[:w, :] + b_ref[:w, :]
        if a_ref.shape[0] > w:
            pad = a_ref[w:, :] + b_ref[w:, :]
            extra = pad if extra is None else extra + pad
    if extra is not None:
        refs[2 * count + 1][...] = extra


def join(meta, parts, comes):
    n = parts[0].shape[1]
    w = n // CHUNKS
    shapes = [shaped(len(parts) * w, n)]
    if parts[0].shape[0] > w:
        shapes.append(shaped(PAD, n))
    return call(functools.partial(join_kernel, w, len(parts)), shapes, meta, [*parts, *comes])


def closing(t, v, row, col, value):
    denom = row + col
    residual = v + value + denom * t
    return t - residual / denom, residual


def most_kernel(m, *refs):
    near_own, near_swap, near_back, extra_ref = refs[:4]
    far_own, far_back = refs[4:5], refs[5:6]
    t_ref, v_ref, row_ref, col_ref, new_ref, res_ref = refs[6:]
    n = t_ref.shape[0]
    place = m[PLACE]

    def write(first, count, half, value):
        rows = pl.ds(first, count)
        new_ref[rows, half], res_ref[rows, half] = closing(
            t_ref[rows, half], v_ref[rows, half], row_ref[rows, :], col_ref[:, half], value
        )

    @pl.when(m[NEAR] == 0)
    def _():
        first = 0
        for own_ref, back_ref in zip(far_own, far_back):
            count = own_ref.shape[0]
            write(first, count, placed(place, n), own_ref[...])
            write(0, n, placed(1 - place, n, first, count), back_ref[...].T)
            first += count

    @pl.when((m[NEAR] == 1) & (m[MIDDLE] == 0))
    def _():
        write(0, n, placed(place, n), near_own[...])
        write(0, n, placed(1 - place, n), near_back[...].T)

    @pl.when(m[MIDDLE] == 1)
    def _():
        line = lax.broadcasted_iota(jnp.int32, (n, n), 0)
        lane = lax.broadcasted_iota(jnp.int32, (n, n), 1)
        own = near_own[...]
        write(0, n, placed(place, n), jnp.where(line >= lane, own, own.T))
        lower = jnp.where(line > lane, near_swap[...].T, extra_ref[:1, :])
        write(0, n, placed(1 - place, n), jnp.where(line < lane, own, lower))


def most(meta, t, *args):
    return call(most_kernel, [shaped(*t.shape)] * 2, meta, args)


def late_kernel(turned, chunk, count, m, *refs):
    values = refs[:count]
    t_ref, v_ref, row_ref, col_ref, new_ref, res_ref, new, res, sems = refs[count + 2 :]
    w = min(values[0].shape)
    n = max(values[0].shape)

    @pl.when(m[NEAR] == 0)
    def _():
        parts = [ref[...].T if turned else ref[...] for ref in values]
        value = parts[0] if count == 1 else jnp.concatenate(parts, axis=int(turned))
        new[...], res[...] = closing(
            t_ref[...], v_ref[...], row_ref[...], col_ref[...], value
        )
        if turned:
            rows, cols = pl.ds(0, n), placed(1 - m[PLACE], n, chunk * w, count * w)
        else:
            rows, cols = pl.ds(chunk * w, count * w), placed(m[PLACE], n)
        copies = [
            pltpu.make_async_copy(source, target.at[rows, cols], sems.at[i])
            for i, (source, target) in enumerate(((new, new_ref), (res, res_ref)))
        ]
        for copy in copies:
            copy.start()
        for copy in copies:
            copy.wait()


def late(meta, turned, chunk, values, new, res, t, v, row_gap, col_gap):
    w, n = values[0].shape
    count = len(values)
    if turned:
        at = lambda i, m: (0, ((1 - m[PLACE]) * CHUNKS + chunk) // count)
        block = pl.BlockSpec((n, count * w), at)
        row, col = None, pl.BlockSpec((1, count * w), at)
    else:
        block = pl.BlockSpec((count * w, n), lambda i, m: (chunk // count, m[PLACE]))
        row = pl.BlockSpec((count * w, 1), lambda i, m: (chunk // count, 0))
        col = pl.BlockSpec((1, n), lambda i, m: (0, m[PLACE]))
    hbm = pl.BlockSpec(memory_space=pl.ANY)
    return call(
        functools.partial(late_kernel, turned, chunk, count),
        [shaped(*t.shape)] * 2,
        meta,
        [*values, new, res, t, v, row_gap, col_gap],
        in_specs=[*[None] * count, hbm, hbm, block, block, row, col],
        out_specs=[hbm, hbm],
        scratch=[pltpu.VMEM(block.block_shape, jnp.float32)] * 2 + [pltpu.SemaphoreType.DMA((2,))],
        aliases={count + 1: 0, count + 2: 1},
    )


def split_update(t, v, row_gap, col_gap):
    r = lax.axis_index("row")
    c = lax.axis_index("col")
    z, x = r // 2, r % 2
    slot = lax.iota(jnp.int32, 8)
    values = {
        X_PLACE: x,
        ODD: (z + c) % 2,
        TURN_1: x ^ flips(c ^ 1, c),
        TURN_2: x ^ flips(c ^ 2, c),
        TURN_3: x ^ flips(c ^ 3, c),
        NEAR: r // 4 == c // 2,
        MIDDLE: z == c,
        PLACE: x ^ flips(z, c),
    }
    meta = jnp.zeros((8,), jnp.int32)
    for index, value in values.items():
        meta = jnp.where(slot == index, value.astype(jnp.int32), meta)

    across = lambda block: routed(block, lambda r, c: (r, c ^ 2))
    beside = lambda block: routed(block, lambda r, c: (r, c ^ 1))
    over_x = lambda block: routed(block, lambda r, c: (r ^ 1, c))
    over_z = lambda block: routed(block, lambda r, c: (r ^ 2, c))
    over_far = lambda block: routed(block, lambda r, c: (r ^ 4, c))
    to_near = lambda block: routed(block, lambda r, c: None if is_near(r, c) else (r ^ 4, c))
    over = lambda target: lambda block: routed(block, target)

    next_t = beside(t)
    next_v = beside(v)
    own = prep(meta, t, v)
    send, keep = {}, {}
    base = middle_part(meta, own, 1, 0)
    send["n", 0] = next_part(meta, base, next_t, next_v, own, 1, 0)
    for side, chunks in NEAR_GROUPS:
        blocks = near_parts(meta, next_t, next_v, own, side, chunks)
        for k, block in zip(chunks, blocks):
            (send if side else keep)["n", k] = block
    for tag, side, first, count in FAR_GROUPS:
        piece = pick(meta, t, v, side, first, count)
        piece = across(piece)
        other = beside(piece)
        blocks = far_parts(meta, piece, other, own, side)
        for i, block in enumerate(blocks):
            (send if side else keep)["f", first + i] = block
    total, come = {}, {}
    for tag in "nf":
        for k in range(CHUNKS):
            key = tag, k
            arrived = over_x(send[key])
            leave, stay = fold(meta, keep[key], arrived)
            arrived = over_z(leave)
            total[key] = add(meta, stay, arrived)
            come[key] = (to_near if tag == "n" else over_far)(total[key])

    def joined(tag, chunks):
        return join(meta, [total[tag, k] for k in chunks], [come[tag, k] for k in chunks])

    near_own, extra = joined("n", range(CHUNKS))
    near_swap = over(swap_target)(near_own)
    near_back = over(hop_of(near_target))(near_own)
    near_back = over(after_hop(near_target))(near_back)
    far_own, far_back = [], []
    for i, chunks in enumerate(((0, 1), (2,), (3,))):
        far_own += joined("f", chunks)
        if i in HOPS:
            back = over(hop_of(far_target))(far_own[-1])
            far_back.append(over(after_hop(far_target))(back))
        else:
            far_back.append(over(far_target)(far_own[-1]))
    fixed = (t, v, row_gap, col_gap)
    pair = most(meta, t, near_own, near_swap, near_back, extra, far_own[0], far_back[0], *fixed)
    pair = late(meta, False, 2, far_own[1:], *pair, *fixed)
    pair = late(meta, True, 2, far_back[1:2], *pair, *fixed)
    return late(meta, True, 3, far_back[2:], *pair, *fixed)


NEAR_GROUPS = ((1, (1, 2, 3)), (0, (0,)), (0, (1, 2, 3)))
HOPS = (0,)
FAR_GROUPS = (("s0", 1, 0, 2), ("k0", 0, 0, 2), ("s1", 1, 2, 2), ("k1", 0, 2, 2))


def gap_slices(shape, occ_energy, vir_energy):
    tile_rows, tile_cols = shape
    gaps = (vir_energy[None, :] - occ_energy[:, None]).reshape(-1)
    row_gap = lax.dynamic_slice_in_dim(gaps, lax.axis_index("row") * tile_rows, tile_rows, 0)
    col_gap = lax.dynamic_slice_in_dim(gaps, lax.axis_index("col") * tile_cols, tile_cols, 0)
    return row_gap[:, None], col_gap[None, :]


def split_local(amplitudes, interaction, occ_energy, vir_energy):
    gaps = gap_slices(amplitudes.shape, occ_energy, vir_energy)
    return tuple(split_update(amplitudes, interaction, *gaps))


def general_local(amplitudes, interaction, occ_energy, vir_energy):
    row_gap, col_gap = gap_slices(amplitudes.shape, occ_energy, vir_energy)
    denom = row_gap + col_gap
    residual = interaction + general_sum(amplitudes, interaction) + denom * amplitudes
    updated = amplitudes - residual / denom
    return (updated, residual)


def solution(mesh):
    rows, cols = mesh.shape["row"], mesh.shape["col"]
    split = cols == 4 and rows == 2 * cols
    return jax.shard_map(
        split_local if split else general_local,
        mesh=mesh,
        in_specs=(P("row", "col"), P("row", "col"), P(), P()),
        out_specs=(P("row", "col"), P("row", "col")),
        check_vma=False,
    )
```

```python
import functools

import jax
import jax.numpy as jnp
from jax import lax
from jax.experimental import pallas as pl
from jax.experimental.pallas import tpu as pltpu
from jax.sharding import PartitionSpec as P


CHUNKS = 4
PAD = 8


def swapped(block, axis, distance):
    count = lax.axis_size(axis)
    route = []
    for low in range(count):
        high = low | 1 << distance
        if high != low and high < count:
            route += [(low, high), (high, low)]
    return lax.ppermute(block, axis, route)


def from_behind(block, axis, distance):
    devices = range(lax.axis_size(axis))
    route = [(i - distance, i) for i in devices if i - distance in devices]
    return lax.ppermute(block, axis, route)


def contract(left_tile, right_tile):
    right_panel = lax.all_gather(right_tile, "row", axis=0, tiled=True)
    return jnp.dot(
        lax.all_gather(left_tile, "col", axis=1, tiled=True),
        right_panel,
        precision=lax.Precision.HIGHEST,
        preferred_element_type=jnp.float32,
    )


def diagonal_tile(tile, row_place, col_place):
    tile_rows = tile.shape[0]
    col_count = lax.axis_size("col")
    ratio = lax.axis_size("row") // col_count
    ratio_bits = ratio.bit_length() - 1
    row_bits = lax.axis_size("row").bit_length() - 1
    blocks = tile.reshape(tile_rows, ratio, tile_rows).transpose(1, 2, 0)
    for bit_index in range(row_bits):
        row_flag = row_place // 2**bit_index % 2
        if bit_index < ratio_bits:
            lower = 2**bit_index
            grouped = blocks.reshape(ratio // (2 * lower), 2, lower, tile_rows, tile_rows)
            zero_half = grouped[:, 0]
            one_half = grouped[:, 1]
            outgoing = jnp.where(row_flag == 0, one_half, zero_half)
            incoming = swapped(outgoing, "row", bit_index)
            new_zero = jnp.where(row_flag == 1, incoming, zero_half)
            new_one = jnp.where(row_flag == 0, incoming, one_half)
            blocks = jnp.stack([new_zero, new_one], axis=1).reshape(ratio, tile_rows, tile_rows)
        else:
            col_flag = col_place // 2 ** (bit_index - ratio_bits) % 2
            stride = 2**bit_index * col_count - 2 ** (bit_index - ratio_bits)
            from_above = from_behind(blocks, ("row", "col"), -stride)
            from_below = from_behind(blocks, ("row", "col"), stride)
            incoming = jnp.where(row_flag == 0, from_above, from_below)
            blocks = jnp.where(row_flag != col_flag, incoming, blocks)
    return blocks.transpose(1, 0, 2).reshape(tile_rows, ratio * tile_rows)


def general_sum(amplitudes, interaction):
    product = contract(amplitudes, interaction)
    mirrored = diagonal_tile(product, lax.axis_index("row"), lax.axis_index("col"))
    return product + mirrored


def routed(block, target):
    rows, cols = lax.axis_size("row"), lax.axis_size("col")
    route = []
    for r in range(rows):
        for c in range(cols):
            place = target(r, c)
            if place is not None:
                route.append((r * cols + c, place[0] * cols + place[1]))
    return lax.ppermute(block, ("row", "col"), route)


def is_near(r, c):
    return r >> 2 == c >> 1


def flips(z, c):
    return (z > c) ^ ((z ^ c) == 3)


def flipped(z, x, c):
    return x ^ flips(z, c)


def swap_target(r, c):
    return (r ^ 1, c) if r >> 1 == c else None


def near_target(r, c):
    z, x = r >> 1, r & 1
    if not is_near(r, c) or z == c:
        return None
    return (2 * c + flipped(z, x, c), z)


def far_target(r, c):
    z, x = r >> 1, r & 1
    if not is_near(r, c):
        return None
    return (2 * c + flipped(z ^ 2, x, c), z ^ 2)


def hop_of(target):
    return lambda r, c: target(r, c) and (r, c ^ 2)


def after_hop(target):
    return lambda r, c: target(r, c ^ 2)


X_PLACE, ODD, TURN_1, TURN_2, TURN_3, NEAR, MIDDLE, PLACE = range(8)
VMEM = 40 * 2**20


def params():
    return pltpu.CompilerParams(vmem_limit_bytes=VMEM)


def zeros(count):
    return (0,) * count


def call(kernel, shapes, meta, args, in_specs=None, out_specs=None, scratch=(), aliases=None):
    if in_specs is None:
        in_specs = [None] * len(args)
    if out_specs is None:
        out_specs = [None] * len(shapes)
    whole = lambda a: pl.BlockSpec(a.shape, lambda i, m: zeros(len(a.shape)))
    return pl.pallas_call(
        kernel,
        out_shape=list(shapes),
        grid_spec=pltpu.PrefetchScalarGridSpec(
            num_scalar_prefetch=1,
            grid=(1,),
            in_specs=[s or whole(a) for s, a in zip(in_specs, args)],
            out_specs=[s or whole(a) for s, a in zip(out_specs, shapes)],
            scratch_shapes=list(scratch),
        ),
        input_output_aliases=aliases or {},
        compiler_params=params(),
    )(meta, *args)


def shaped(*shape):
    return jax.ShapeDtypeStruct(shape, jnp.float32)


def halves(value):
    high = value.astype(jnp.bfloat16)
    return high, (value - high.astype(jnp.float32)).astype(jnp.bfloat16)


def joined_left(t_high, t_low, v_high, v_low):
    return jnp.concatenate([t_high, t_high, t_low, v_high, v_high, v_low], axis=1)


def left_of(t, v):
    t_high, t_low = halves(t.T)
    v_high, v_low = halves(v.T)
    return joined_left(t_high, t_low, v_high, v_low)


def own_left(own_ref, cols):
    return joined_left(*(own_ref[i, :, cols].T for i in range(4)))


def own_right(own_ref, cols):
    return jnp.concatenate([own_ref[i, :, cols] for i in (2, 3, 2, 0, 1, 0)], axis=0)


def crossed(left, right):
    return jnp.dot(left, right, preferred_element_type=jnp.float32)


def placed(place, n, offset=0, size=None):
    return pl.ds(pl.multiple_of(place * n + offset, 128), size or n)


def pick_kernel(side, first, m, t_ref, v_ref, out_ref, sems):
    n = t_ref.shape[0]
    cols = placed(m[X_PLACE] ^ side, n, first, out_ref.shape[2])
    copies = [
        pltpu.make_async_copy(ref.at[:, cols], out_ref.at[i], sems.at[i])
        for i, ref in enumerate((t_ref, v_ref))
    ]
    for copy in copies:
        copy.start()
    for copy in copies:
        copy.wait()


def pick(meta, t, v, side, first, count):
    n = t.shape[0]
    w = n // CHUNKS
    hbm = pl.BlockSpec(memory_space=pltpu.MemorySpace.HBM)
    return call(
        functools.partial(pick_kernel, side, first * w),
        [shaped(2, n, count * w)],
        meta,
        [t, v],
        in_specs=[hbm, hbm],
        scratch=[pltpu.SemaphoreType.DMA((2,))],
    )[0]


def prep_kernel(_, t_ref, v_ref, own_ref):
    own_ref[0], own_ref[1] = halves(t_ref[...])
    own_ref[2], own_ref[3] = halves(v_ref[...])


def prep(meta, t, v):
    return call(prep_kernel, [jax.ShapeDtypeStruct((4, *t.shape), jnp.bfloat16)], meta, [t, v])[0]


def middle_block(m, side, chunks, own_ref, outs):
    n = own_ref.shape[1]
    w = n // CHUNKS
    half = m[X_PLACE] ^ side
    left = own_left(own_ref, placed(half, n, chunks[0] * w, len(chunks) * w))
    diagonal = crossed(left, own_right(own_ref, placed(half, n)))
    aside = crossed(left, own_right(own_ref, placed(1 - half, n)))
    lane = lax.broadcasted_iota(jnp.int32, (w, n), 1)
    for i, (k, out_ref) in enumerate(zip(chunks, outs)):
        line = lax.broadcasted_iota(jnp.int32, (w, n), 0) + k * w
        rows = slice(i * w, (i + 1) * w)
        out_ref[0, :w, :] = jnp.where(line >= lane, diagonal[rows], aside[rows])
        extra = jnp.sum(jnp.where(line == lane, aside[rows], 0.0), axis=0, keepdims=True)
        out_ref[0, w:, :] = jnp.broadcast_to(extra, (PAD, n))


def middle_kernel(side, k, m, own_ref, out_ref):
    middle_block(m, side, (k,), own_ref, [out_ref])


def middle_part(meta, own, side, k):
    n = own.shape[1]
    w = n // CHUNKS
    return call(
        functools.partial(middle_kernel, side, k),
        [shaped(2, w + PAD, n)],
        meta,
        [own],
        out_specs=[pl.BlockSpec((1, w + PAD, n), lambda i, m: (0, 0, 0))],
    )[0]


def next_part(meta, base, at, av, own, side, k):
    n = own.shape[1]
    w = n // CHUNKS
    block = pl.BlockSpec((n, w), lambda i, m: (0, (m[X_PLACE] ^ side) * CHUNKS + k))
    return call(
        functools.partial(next_kernel_blocked, side),
        [shaped(*base.shape)],
        meta,
        [base, at, av, own],
        in_specs=[pl.BlockSpec(memory_space=pl.ANY), block, block, None],
        out_specs=[pl.BlockSpec((1, w + PAD, n), lambda i, m: (1, 0, 0))],
        aliases={1: 0},
    )[0]


def next_kernel_blocked(side, m, _, at_ref, av_ref, own_ref, out_ref):
    n = own_ref.shape[1]
    w = at_ref.shape[1]
    right = own_right(own_ref, placed(m[TURN_1] ^ side, n))
    out_ref[0, :w, :] = crossed(left_of(at_ref[...], av_ref[...]), right)
    out_ref[0, w:, :] = jnp.zeros((PAD, n), jnp.float32)


def near_parts(meta, at, av, own, side, chunks):
    n = own.shape[1]
    w = n // CHUNKS
    half = pl.BlockSpec((n, n), lambda i, m: (0, m[X_PLACE] ^ side))
    return call(
        functools.partial(near_half_kernel, side, chunks),
        [shaped(2, w + PAD, n) for _ in chunks],
        meta,
        [at, av, own],
        in_specs=[half, half, None],
    )


def near_half_kernel(side, chunks, m, at_ref, av_ref, own_ref, *outs):
    n = own_ref.shape[1]
    w = n // CHUNKS
    middle_block(m, side, chunks, own_ref, outs)
    cols = slice(chunks[0] * w, (chunks[-1] + 1) * w)
    right = own_right(own_ref, placed(m[TURN_1] ^ side, n))
    block = crossed(left_of(at_ref[:, cols], av_ref[:, cols]), right)
    for i, out_ref in enumerate(outs):
        out_ref[1, :w, :] = block[i * w : (i + 1) * w]
        out_ref[1, w:, :] = jnp.zeros((PAD, n), jnp.float32)


def far_kernel(side, m, a_ref, b_ref, own_ref, *outs):
    n = own_ref.shape[1]
    w = outs[0].shape[1]
    for d, (ref, turn) in enumerate(((a_ref, TURN_2), (b_ref, TURN_3))):
        right = own_right(own_ref, placed(m[turn] ^ side, n))
        block = crossed(left_of(ref[0], ref[1]), right)
        for i, out_ref in enumerate(outs):
            out_ref[d] = block[i * w : (i + 1) * w]


def far_parts(meta, a, b, own, side):
    n = own.shape[1]
    w = n // CHUNKS
    return call(
        functools.partial(far_kernel, side),
        [shaped(2, w, n)] * (a.shape[2] // w),
        meta,
        [a, b, own],
    )


def fold_kernel(_, keep_pass, come_pass, keep_stay, come_stay, pass_ref, stay_ref):
    pass_ref[...] = keep_pass[0] + come_pass[0]
    stay_ref[...] = keep_stay[0] + come_stay[0]


def fold(meta, keep, come):
    _, lines, n = keep.shape
    leave = pl.BlockSpec((1, lines, n), lambda i, m: (1 - m[ODD], 0, 0))
    stay = pl.BlockSpec((1, lines, n), lambda i, m: (m[ODD], 0, 0))
    return call(
        fold_kernel,
        [shaped(lines, n)] * 2,
        meta,
        [keep, come, keep, come],
        in_specs=[leave, leave, stay, stay],
    )


def add_kernel(_, a_ref, b_ref, out_ref):
    out_ref[...] = a_ref[...] + b_ref[...]


def add(meta, a, b):
    return call(add_kernel, [shaped(*a.shape)], meta, [a, b])[0]


def join_kernel(w, count, _, *refs):
    out_ref = refs[2 * count]
    extra = None
    for k in range(count):
        a_ref, b_ref = refs[k], refs[count + k]
        out_ref[k * w : (k + 1) * w, :] = a_ref[:w, :] + b_ref[:w, :]
        if a_ref.shape[0] > w:
            pad = a_ref[w:, :] + b_ref[w:, :]
            extra = pad if extra is None else extra + pad
    if extra is not None:
        refs[2 * count + 1][...] = extra


def join(meta, parts, comes):
    n = parts[0].shape[1]
    w = n // CHUNKS
    shapes = [shaped(len(parts) * w, n)]
    if parts[0].shape[0] > w:
        shapes.append(shaped(PAD, n))
    return call(functools.partial(join_kernel, w, len(parts)), shapes, meta, [*parts, *comes])


def closing(t, v, row, col, value):
    denom = row + col
    residual = v + value + denom * t
    return t - residual / denom, residual


def most_kernel(m, *refs):
    near_own, near_swap, near_back, extra_ref = refs[:4]
    far_own, far_back = refs[4:5], refs[5:6]
    t_ref, v_ref, row_ref, col_ref, new_ref, res_ref = refs[6:]
    n = t_ref.shape[0]
    place = m[PLACE]

    def write(first, count, half, value):
        rows = pl.ds(first, count)
        new_ref[rows, half], res_ref[rows, half] = closing(
            t_ref[rows, half], v_ref[rows, half], row_ref[rows, :], col_ref[:, half], value
        )

    @pl.when(m[NEAR] == 0)
    def _():
        first = 0
        for own_ref, back_ref in zip(far_own, far_back):
            count = own_ref.shape[0]
            write(first, count, placed(place, n), own_ref[...])
            write(0, n, placed(1 - place, n, first, count), back_ref[...].T)
            first += count

    @pl.when((m[NEAR] == 1) & (m[MIDDLE] == 0))
    def _():
        write(0, n, placed(place, n), near_own[...])
        write(0, n, placed(1 - place, n), near_back[...].T)

    @pl.when(m[MIDDLE] == 1)
    def _():
        line = lax.broadcasted_iota(jnp.int32, (n, n), 0)
        lane = lax.broadcasted_iota(jnp.int32, (n, n), 1)
        own = near_own[...]
        write(0, n, placed(place, n), jnp.where(line >= lane, own, own.T))
        lower = jnp.where(line > lane, near_swap[...].T, extra_ref[:1, :])
        write(0, n, placed(1 - place, n), jnp.where(line < lane, own, lower))


def most(meta, t, *args):
    return call(most_kernel, [shaped(*t.shape)] * 2, meta, args)


def late_kernel(turned, chunk, count, m, *refs):
    values = refs[:count]
    t_ref, v_ref, row_ref, col_ref, new_ref, res_ref, new, res, sems = refs[count + 2 :]
    w = min(values[0].shape)
    n = max(values[0].shape)

    @pl.when(m[NEAR] == 0)
    def _():
        parts = [ref[...].T if turned else ref[...] for ref in values]
        value = parts[0] if count == 1 else jnp.concatenate(parts, axis=int(turned))
        new[...], res[...] = closing(
            t_ref[...], v_ref[...], row_ref[...], col_ref[...], value
        )
        if turned:
            rows, cols = pl.ds(0, n), placed(1 - m[PLACE], n, chunk * w, count * w)
        else:
            rows, cols = pl.ds(chunk * w, count * w), placed(m[PLACE], n)
        copies = [
            pltpu.make_async_copy(source, target.at[rows, cols], sems.at[i])
            for i, (source, target) in enumerate(((new, new_ref), (res, res_ref)))
        ]
        for copy in copies:
            copy.start()
        for copy in copies:
            copy.wait()


def late(meta, turned, chunk, values, new, res, t, v, row_gap, col_gap):
    w, n = values[0].shape
    count = len(values)
    if turned:
        at = lambda i, m: (0, ((1 - m[PLACE]) * CHUNKS + chunk) // count)
        block = pl.BlockSpec((n, count * w), at)
        row, col = None, pl.BlockSpec((1, count * w), at)
    else:
        block = pl.BlockSpec((count * w, n), lambda i, m: (chunk // count, m[PLACE]))
        row = pl.BlockSpec((count * w, 1), lambda i, m: (chunk // count, 0))
        col = pl.BlockSpec((1, n), lambda i, m: (0, m[PLACE]))
    hbm = pl.BlockSpec(memory_space=pl.ANY)
    return call(
        functools.partial(late_kernel, turned, chunk, count),
        [shaped(*t.shape)] * 2,
        meta,
        [*values, new, res, t, v, row_gap, col_gap],
        in_specs=[*[None] * count, hbm, hbm, block, block, row, col],
        out_specs=[hbm, hbm],
        scratch=[pltpu.VMEM(block.block_shape, jnp.float32)] * 2 + [pltpu.SemaphoreType.DMA((2,))],
        aliases={count + 1: 0, count + 2: 1},
    )


def split_update(t, v, row_gap, col_gap):
    r = lax.axis_index("row")
    c = lax.axis_index("col")
    z, x = r // 2, r % 2
    slot = lax.iota(jnp.int32, 8)
    values = {
        X_PLACE: x,
        ODD: (z + c) % 2,
        TURN_1: x ^ flips(c ^ 1, c),
        TURN_2: x ^ flips(c ^ 2, c),
        TURN_3: x ^ flips(c ^ 3, c),
        NEAR: r // 4 == c // 2,
        MIDDLE: z == c,
        PLACE: x ^ flips(z, c),
    }
    meta = jnp.zeros((8,), jnp.int32)
    for index, value in values.items():
        meta = jnp.where(slot == index, value.astype(jnp.int32), meta)

    across = lambda block: routed(block, lambda r, c: (r, c ^ 2))
    beside = lambda block: routed(block, lambda r, c: (r, c ^ 1))
    over_x = lambda block: routed(block, lambda r, c: (r ^ 1, c))
    over_z = lambda block: routed(block, lambda r, c: (r ^ 2, c))
    over_far = lambda block: routed(block, lambda r, c: (r ^ 4, c))
    to_near = lambda block: routed(block, lambda r, c: None if is_near(r, c) else (r ^ 4, c))
    over = lambda target: lambda block: routed(block, target)

    next_t = beside(t)
    next_v = beside(v)
    own = prep(meta, t, v)
    send, keep = {}, {}
    base = middle_part(meta, own, 1, 0)
    send["n", 0] = next_part(meta, base, next_t, next_v, own, 1, 0)
    for side, chunks in NEAR_GROUPS:
        blocks = near_parts(meta, next_t, next_v, own, side, chunks)
        for k, block in zip(chunks, blocks):
            (send if side else keep)["n", k] = block
    for tag, side, first, count in FAR_GROUPS:
        piece = pick(meta, t, v, side, first, count)
        piece = across(piece)
        other = beside(piece)
        blocks = far_parts(meta, piece, other, own, side)
        for i, block in enumerate(blocks):
            (send if side else keep)["f", first + i] = block
    total, come = {}, {}
    for tag in "nf":
        for k in range(CHUNKS):
            key = tag, k
            arrived = over_x(send[key])
            leave, stay = fold(meta, keep[key], arrived)
            arrived = over_z(leave)
            total[key] = add(meta, stay, arrived)
            come[key] = (to_near if tag == "n" else over_far)(total[key])

    def joined(tag, chunks):
        return join(meta, [total[tag, k] for k in chunks], [come[tag, k] for k in chunks])

    near_own, extra = joined("n", range(CHUNKS))
    near_swap = over(swap_target)(near_own)
    near_back = over(hop_of(near_target))(near_own)
    near_back = over(after_hop(near_target))(near_back)
    far_own, far_back = [], []
    for chunks in ((0, 1), (2,), (3,)):
        far_own += joined("f", chunks)
        far_back.append(over(far_target)(far_own[-1]))
    fixed = (t, v, row_gap, col_gap)
    pair = most(meta, t, near_own, near_swap, near_back, extra, far_own[0], far_back[0], *fixed)
    pair = late(meta, False, 2, far_own[1:], *pair, *fixed)
    pair = late(meta, True, 2, far_back[1:2], *pair, *fixed)
    return late(meta, True, 3, far_back[2:], *pair, *fixed)


NEAR_GROUPS = ((1, (1, 2, 3)), (0, (0,)), (0, (1, 2, 3)))
FAR_GROUPS = (("s0", 1, 0, 2), ("k0", 0, 0, 2), ("s1", 1, 2, 2), ("k1", 0, 2, 2))


def gap_slices(shape, occ_energy, vir_energy):
    tile_rows, tile_cols = shape
    gaps = (vir_energy[None, :] - occ_energy[:, None]).reshape(-1)
    row_gap = lax.dynamic_slice_in_dim(gaps, lax.axis_index("row") * tile_rows, tile_rows, 0)
    col_gap = lax.dynamic_slice_in_dim(gaps, lax.axis_index("col") * tile_cols, tile_cols, 0)
    return row_gap[:, None], col_gap[None, :]


def split_local(amplitudes, interaction, occ_energy, vir_energy):
    gaps = gap_slices(amplitudes.shape, occ_energy, vir_energy)
    return tuple(split_update(amplitudes, interaction, *gaps))


def general_local(amplitudes, interaction, occ_energy, vir_energy):
    row_gap, col_gap = gap_slices(amplitudes.shape, occ_energy, vir_energy)
    denom = row_gap + col_gap
    residual = interaction + general_sum(amplitudes, interaction) + denom * amplitudes
    updated = amplitudes - residual / denom
    return (updated, residual)


def solution(mesh):
    rows, cols = mesh.shape["row"], mesh.shape["col"]
    split = cols == 4 and rows == 2 * cols
    return jax.shard_map(
        split_local if split else general_local,
        mesh=mesh,
        in_specs=(P("row", "col"), P("row", "col"), P(), P()),
        out_specs=(P("row", "col"), P("row", "col")),
        check_vma=False,
    )
```

```python
import functools

import jax
import jax.numpy as jnp
from jax import lax
from jax.experimental import pallas as pl
from jax.experimental.pallas import tpu as pltpu
from jax.sharding import PartitionSpec as P


CHUNKS = 4
PAD = 8


def swapped(block, axis, distance):
    count = lax.axis_size(axis)
    route = []
    for low in range(count):
        high = low | 1 << distance
        if high != low and high < count:
            route += [(low, high), (high, low)]
    return lax.ppermute(block, axis, route)


def from_behind(block, axis, distance):
    devices = range(lax.axis_size(axis))
    route = [(i - distance, i) for i in devices if i - distance in devices]
    return lax.ppermute(block, axis, route)


def contract(left_tile, right_tile):
    right_panel = lax.all_gather(right_tile, "row", axis=0, tiled=True)
    return jnp.dot(
        lax.all_gather(left_tile, "col", axis=1, tiled=True),
        right_panel,
        precision=lax.Precision.HIGHEST,
        preferred_element_type=jnp.float32,
    )


def diagonal_tile(tile, row_place, col_place):
    tile_rows = tile.shape[0]
    col_count = lax.axis_size("col")
    ratio = lax.axis_size("row") // col_count
    ratio_bits = ratio.bit_length() - 1
    row_bits = lax.axis_size("row").bit_length() - 1
    blocks = tile.reshape(tile_rows, ratio, tile_rows).transpose(1, 2, 0)
    for bit_index in range(row_bits):
        row_flag = row_place // 2**bit_index % 2
        if bit_index < ratio_bits:
            lower = 2**bit_index
            grouped = blocks.reshape(ratio // (2 * lower), 2, lower, tile_rows, tile_rows)
            zero_half = grouped[:, 0]
            one_half = grouped[:, 1]
            outgoing = jnp.where(row_flag == 0, one_half, zero_half)
            incoming = swapped(outgoing, "row", bit_index)
            new_zero = jnp.where(row_flag == 1, incoming, zero_half)
            new_one = jnp.where(row_flag == 0, incoming, one_half)
            blocks = jnp.stack([new_zero, new_one], axis=1).reshape(ratio, tile_rows, tile_rows)
        else:
            col_flag = col_place // 2 ** (bit_index - ratio_bits) % 2
            stride = 2**bit_index * col_count - 2 ** (bit_index - ratio_bits)
            from_above = from_behind(blocks, ("row", "col"), -stride)
            from_below = from_behind(blocks, ("row", "col"), stride)
            incoming = jnp.where(row_flag == 0, from_above, from_below)
            blocks = jnp.where(row_flag != col_flag, incoming, blocks)
    return blocks.transpose(1, 0, 2).reshape(tile_rows, ratio * tile_rows)


def general_sum(amplitudes, interaction):
    product = contract(amplitudes, interaction)
    mirrored = diagonal_tile(product, lax.axis_index("row"), lax.axis_index("col"))
    return product + mirrored


def routed(block, target):
    rows, cols = lax.axis_size("row"), lax.axis_size("col")
    route = []
    for r in range(rows):
        for c in range(cols):
            place = target(r, c)
            if place is not None:
                route.append((r * cols + c, place[0] * cols + place[1]))
    return lax.ppermute(block, ("row", "col"), route)


def is_near(r, c):
    return r >> 2 == c >> 1


def flips(z, c):
    return (z > c) ^ ((z ^ c) == 3)


def flipped(z, x, c):
    return x ^ flips(z, c)


def swap_target(r, c):
    return (r ^ 1, c) if r >> 1 == c else None


def near_target(r, c):
    z, x = r >> 1, r & 1
    if not is_near(r, c) or z == c:
        return None
    return (2 * c + flipped(z, x, c), z)


def far_target(r, c):
    z, x = r >> 1, r & 1
    if not is_near(r, c):
        return None
    return (2 * c + flipped(z ^ 2, x, c), z ^ 2)


def hop_of(target):
    return lambda r, c: target(r, c) and (r, c ^ 2)


def after_hop(target):
    return lambda r, c: target(r, c ^ 2)


X_PLACE, ODD, TURN_1, TURN_2, TURN_3, NEAR, MIDDLE, PLACE = range(8)
VMEM = 40 * 2**20


def params():
    return pltpu.CompilerParams(vmem_limit_bytes=VMEM)


def zeros(count):
    return (0,) * count


def call(kernel, shapes, meta, args, in_specs=None, out_specs=None, scratch=(), aliases=None):
    if in_specs is None:
        in_specs = [None] * len(args)
    if out_specs is None:
        out_specs = [None] * len(shapes)
    whole = lambda a: pl.BlockSpec(a.shape, lambda i, m: zeros(len(a.shape)))
    return pl.pallas_call(
        kernel,
        out_shape=list(shapes),
        grid_spec=pltpu.PrefetchScalarGridSpec(
            num_scalar_prefetch=1,
            grid=(1,),
            in_specs=[s or whole(a) for s, a in zip(in_specs, args)],
            out_specs=[s or whole(a) for s, a in zip(out_specs, shapes)],
            scratch_shapes=list(scratch),
        ),
        input_output_aliases=aliases or {},
        compiler_params=params(),
    )(meta, *args)


def shaped(*shape):
    return jax.ShapeDtypeStruct(shape, jnp.float32)


def halves(value):
    high = value.astype(jnp.bfloat16)
    return high, (value - high.astype(jnp.float32)).astype(jnp.bfloat16)


def joined_left(t_high, t_low, v_high, v_low):
    return jnp.concatenate([t_high, t_high, t_low, v_high, v_high, v_low], axis=1)


def left_of(t, v):
    t_high, t_low = halves(t.T)
    v_high, v_low = halves(v.T)
    return joined_left(t_high, t_low, v_high, v_low)


def own_left(own_ref, cols):
    return joined_left(*(own_ref[i, :, cols].T for i in range(4)))


def own_right(own_ref, cols):
    return jnp.concatenate([own_ref[i, :, cols] for i in (2, 3, 2, 0, 1, 0)], axis=0)


def crossed(left, right):
    return jnp.dot(left, right, preferred_element_type=jnp.float32)


def placed(place, n, offset=0, size=None):
    return pl.ds(pl.multiple_of(place * n + offset, 128), size or n)


def pick_kernel(side, first, m, t_ref, v_ref, out_ref, sems):
    n = t_ref.shape[0]
    cols = placed(m[X_PLACE] ^ side, n, first, out_ref.shape[2])
    copies = [
        pltpu.make_async_copy(ref.at[:, cols], out_ref.at[i], sems.at[i])
        for i, ref in enumerate((t_ref, v_ref))
    ]
    for copy in copies:
        copy.start()
    for copy in copies:
        copy.wait()


def pick(meta, t, v, side, first, count):
    n = t.shape[0]
    w = n // CHUNKS
    hbm = pl.BlockSpec(memory_space=pltpu.MemorySpace.HBM)
    return call(
        functools.partial(pick_kernel, side, first * w),
        [shaped(2, n, count * w)],
        meta,
        [t, v],
        in_specs=[hbm, hbm],
        scratch=[pltpu.SemaphoreType.DMA((2,))],
    )[0]


def prep_kernel(_, t_ref, v_ref, own_ref):
    own_ref[0], own_ref[1] = halves(t_ref[...])
    own_ref[2], own_ref[3] = halves(v_ref[...])


def prep(meta, t, v):
    return call(prep_kernel, [jax.ShapeDtypeStruct((4, *t.shape), jnp.bfloat16)], meta, [t, v])[0]


def lines(k, w):
    return w + PAD if k == CHUNKS - 1 else w


def middle_block(m, side, chunks, own_ref, outs):
    n = own_ref.shape[1]
    w = n // CHUNKS
    half = m[X_PLACE] ^ side
    same, cross = placed(half, n), placed(1 - half, n)
    left = own_left(own_ref, placed(half, n, chunks[0] * w, len(chunks) * w))
    diagonal = crossed(left, own_right(own_ref, same))
    aside = crossed(left, own_right(own_ref, cross))
    lane = lax.broadcasted_iota(jnp.int32, (w, n), 1)
    for i, (k, out_ref) in enumerate(zip(chunks, outs)):
        line = lax.broadcasted_iota(jnp.int32, (w, n), 0) + k * w
        rows = slice(i * w, (i + 1) * w)
        out_ref[0, :w, :] = jnp.where(line >= lane, diagonal[rows], aside[rows])
        if out_ref.shape[1] > w:
            whole = lambda i, cols: own_ref[i, :, cols].astype(jnp.float32) + own_ref[
                i + 1, :, cols
            ].astype(jnp.float32)
            products = whole(0, same) * whole(2, cross) + whole(2, same) * whole(0, cross)
            extra = jnp.sum(products, axis=0, keepdims=True)
            out_ref[0, w:, :] = jnp.broadcast_to(extra, (PAD, n))


def middle_kernel(side, k, m, own_ref, out_ref):
    middle_block(m, side, (k,), own_ref, [out_ref])


def middle_part(meta, own, side, k):
    n = own.shape[1]
    w = lines(k, n // CHUNKS)
    return call(
        functools.partial(middle_kernel, side, k),
        [shaped(2, w, n)],
        meta,
        [own],
        out_specs=[pl.BlockSpec((1, w, n), lambda i, m: (0, 0, 0))],
    )[0]


def next_part(meta, base, at, av, own, side, k):
    n = own.shape[1]
    w = n // CHUNKS
    block = pl.BlockSpec((n, w), lambda i, m: (0, (m[X_PLACE] ^ side) * CHUNKS + k))
    return call(
        functools.partial(next_kernel, side),
        [shaped(*base.shape)],
        meta,
        [base, at, av, own],
        in_specs=[pl.BlockSpec(memory_space=pl.ANY), block, block, None],
        out_specs=[pl.BlockSpec((1, *base.shape[1:]), lambda i, m: (1, 0, 0))],
        aliases={1: 0},
    )[0]


def next_kernel(side, m, _, at_ref, av_ref, own_ref, out_ref):
    n = own_ref.shape[1]
    w = at_ref.shape[1]
    right = own_right(own_ref, placed(m[TURN_1] ^ side, n))
    out_ref[0, :w, :] = crossed(left_of(at_ref[...], av_ref[...]), right)


def near_parts(meta, at, av, own, side, chunks):
    n = own.shape[1]
    w = n // CHUNKS
    half = pl.BlockSpec((n, n), lambda i, m: (0, m[X_PLACE] ^ side))
    return call(
        functools.partial(near_kernel, side, chunks),
        [shaped(2, lines(k, w), n) for k in chunks],
        meta,
        [at, av, own],
        in_specs=[half, half, None],
    )


def near_kernel(side, chunks, m, at_ref, av_ref, own_ref, *outs):
    n = own_ref.shape[1]
    w = n // CHUNKS
    middle_block(m, side, chunks, own_ref, outs)
    cols = slice(chunks[0] * w, (chunks[-1] + 1) * w)
    right = own_right(own_ref, placed(m[TURN_1] ^ side, n))
    block = crossed(left_of(at_ref[:, cols], av_ref[:, cols]), right)
    for i, out_ref in enumerate(outs):
        out_ref[1, :w, :] = block[i * w : (i + 1) * w]
        if out_ref.shape[1] > w:
            out_ref[1, w:, :] = jnp.zeros((PAD, n), jnp.float32)


def far_kernel(side, m, a_ref, b_ref, own_ref, *outs):
    n = own_ref.shape[1]
    w = outs[0].shape[1]
    for d, (ref, turn) in enumerate(((a_ref, TURN_2), (b_ref, TURN_3))):
        right = own_right(own_ref, placed(m[turn] ^ side, n))
        block = crossed(left_of(ref[0], ref[1]), right)
        for i, out_ref in enumerate(outs):
            out_ref[d] = block[i * w : (i + 1) * w]


def far_parts(meta, a, b, own, side):
    n = own.shape[1]
    w = n // CHUNKS
    return call(
        functools.partial(far_kernel, side),
        [shaped(2, w, n)] * (a.shape[2] // w),
        meta,
        [a, b, own],
    )


def fold_kernel(_, keep_pass, come_pass, keep_stay, come_stay, pass_ref, stay_ref):
    pass_ref[...] = keep_pass[0] + come_pass[0]
    stay_ref[...] = keep_stay[0] + come_stay[0]


def fold(meta, keep, come):
    _, lines, n = keep.shape
    leave = pl.BlockSpec((1, lines, n), lambda i, m: (1 - m[ODD], 0, 0))
    stay = pl.BlockSpec((1, lines, n), lambda i, m: (m[ODD], 0, 0))
    return call(
        fold_kernel,
        [shaped(lines, n)] * 2,
        meta,
        [keep, come, keep, come],
        in_specs=[leave, leave, stay, stay],
    )


def add_kernel(_, a_ref, b_ref, out_ref):
    out_ref[...] = a_ref[...] + b_ref[...]


def add(meta, a, b):
    return call(add_kernel, [shaped(*a.shape)], meta, [a, b])[0]


def join_kernel(w, count, _, *refs):
    out_ref = refs[2 * count]
    for k in range(count):
        a_ref, b_ref = refs[k], refs[count + k]
        out_ref[k * w : (k + 1) * w, :] = a_ref[:w, :] + b_ref[:w, :]
        if a_ref.shape[0] > w:
            refs[2 * count + 1][...] = a_ref[w:, :] + b_ref[w:, :]


def join(meta, parts, comes):
    n = parts[0].shape[1]
    w = n // CHUNKS
    shapes = [shaped(len(parts) * w, n)]
    if parts[-1].shape[0] > w:
        shapes.append(shaped(PAD, n))
    return call(functools.partial(join_kernel, w, len(parts)), shapes, meta, [*parts, *comes])


def closing(t, v, row, col, value):
    denom = row + col
    residual = v + value + denom * t
    return t - residual / denom, residual


def most_kernel(m, *refs):
    near_own, near_swap, near_back, extra_ref = refs[:4]
    far_own, far_back = refs[4:5], refs[5:6]
    t_ref, v_ref, row_ref, col_ref, new_ref, res_ref = refs[6:]
    n = t_ref.shape[0]
    place = m[PLACE]

    def write(first, count, half, value):
        rows = pl.ds(first, count)
        new_ref[rows, half], res_ref[rows, half] = closing(
            t_ref[rows, half], v_ref[rows, half], row_ref[rows, :], col_ref[:, half], value
        )

    @pl.when(m[NEAR] == 0)
    def _():
        first = 0
        for own_ref, back_ref in zip(far_own, far_back):
            count = own_ref.shape[0]
            write(first, count, placed(place, n), own_ref[...])
            write(0, n, placed(1 - place, n, first, count), back_ref[...].T)
            first += count

    @pl.when((m[NEAR] == 1) & (m[MIDDLE] == 0))
    def _():
        write(0, n, placed(place, n), near_own[...])
        write(0, n, placed(1 - place, n), near_back[...].T)

    @pl.when(m[MIDDLE] == 1)
    def _():
        line = lax.broadcasted_iota(jnp.int32, (n, n), 0)
        lane = lax.broadcasted_iota(jnp.int32, (n, n), 1)
        own = near_own[...]
        write(0, n, placed(place, n), jnp.where(line >= lane, own, own.T))
        lower = jnp.where(line > lane, near_swap[...].T, extra_ref[:1, :])
        write(0, n, placed(1 - place, n), jnp.where(line < lane, own, lower))


def most(meta, t, *args):
    return call(most_kernel, [shaped(*t.shape)] * 2, meta, args)


def late_kernel(turned, chunk, count, m, *refs):
    values = refs[:count]
    t_ref, v_ref, row_ref, col_ref, new_ref, res_ref, new, res, sems = refs[count + 2 :]
    w = min(values[0].shape)
    n = max(values[0].shape)

    @pl.when(m[NEAR] == 0)
    def _():
        parts = [ref[...].T if turned else ref[...] for ref in values]
        value = parts[0] if count == 1 else jnp.concatenate(parts, axis=int(turned))
        new[...], res[...] = closing(
            t_ref[...], v_ref[...], row_ref[...], col_ref[...], value
        )
        if turned:
            rows, cols = pl.ds(0, n), placed(1 - m[PLACE], n, chunk * w, count * w)
        else:
            rows, cols = pl.ds(chunk * w, count * w), placed(m[PLACE], n)
        copies = [
            pltpu.make_async_copy(source, target.at[rows, cols], sems.at[i])
            for i, (source, target) in enumerate(((new, new_ref), (res, res_ref)))
        ]
        for copy in copies:
            copy.start()
        for copy in copies:
            copy.wait()


def late(meta, turned, chunk, values, new, res, t, v, row_gap, col_gap):
    w, n = values[0].shape
    count = len(values)
    if turned:
        at = lambda i, m: (0, ((1 - m[PLACE]) * CHUNKS + chunk) // count)
        block = pl.BlockSpec((n, count * w), at)
        row, col = None, pl.BlockSpec((1, count * w), at)
    else:
        block = pl.BlockSpec((count * w, n), lambda i, m: (chunk // count, m[PLACE]))
        row = pl.BlockSpec((count * w, 1), lambda i, m: (chunk // count, 0))
        col = pl.BlockSpec((1, n), lambda i, m: (0, m[PLACE]))
    hbm = pl.BlockSpec(memory_space=pl.ANY)
    return call(
        functools.partial(late_kernel, turned, chunk, count),
        [shaped(*t.shape)] * 2,
        meta,
        [*values, new, res, t, v, row_gap, col_gap],
        in_specs=[*[None] * count, hbm, hbm, block, block, row, col],
        out_specs=[hbm, hbm],
        scratch=[pltpu.VMEM(block.block_shape, jnp.float32)] * 2 + [pltpu.SemaphoreType.DMA((2,))],
        aliases={count + 1: 0, count + 2: 1},
    )


def split_update(t, v, row_gap, col_gap):
    r = lax.axis_index("row")
    c = lax.axis_index("col")
    z, x = r // 2, r % 2
    slot = lax.iota(jnp.int32, 8)
    values = {
        X_PLACE: x,
        ODD: (z + c) % 2,
        TURN_1: x ^ flips(c ^ 1, c),
        TURN_2: x ^ flips(c ^ 2, c),
        TURN_3: x ^ flips(c ^ 3, c),
        NEAR: r // 4 == c // 2,
        MIDDLE: z == c,
        PLACE: x ^ flips(z, c),
    }
    meta = jnp.zeros((8,), jnp.int32)
    for index, value in values.items():
        meta = jnp.where(slot == index, value.astype(jnp.int32), meta)

    across = lambda block: routed(block, lambda r, c: (r, c ^ 2))
    beside = lambda block: routed(block, lambda r, c: (r, c ^ 1))
    over_x = lambda block: routed(block, lambda r, c: (r ^ 1, c))
    over_z = lambda block: routed(block, lambda r, c: (r ^ 2, c))
    over_far = lambda block: routed(block, lambda r, c: (r ^ 4, c))
    to_near = lambda block: routed(block, lambda r, c: None if is_near(r, c) else (r ^ 4, c))
    over = lambda target: lambda block: routed(block, target)

    next_t = beside(t)
    next_v = beside(v)
    own = prep(meta, t, v)
    send, keep = {}, {}
    base = middle_part(meta, own, 1, 0)
    send["n", 0] = next_part(meta, base, next_t, next_v, own, 1, 0)
    for side, chunks in NEAR_GROUPS:
        blocks = near_parts(meta, next_t, next_v, own, side, chunks)
        for k, block in zip(chunks, blocks):
            (send if side else keep)["n", k] = block
    for tag, side, first, count in FAR_GROUPS:
        piece = pick(meta, t, v, side, first, count)
        piece = across(piece)
        other = beside(piece)
        blocks = far_parts(meta, piece, other, own, side)
        for i, block in enumerate(blocks):
            (send if side else keep)["f", first + i] = block
    total, come = {}, {}
    for tag in "nf":
        for k in range(CHUNKS):
            key = tag, k
            arrived = over_x(send[key])
            leave, stay = fold(meta, keep[key], arrived)
            arrived = over_z(leave)
            total[key] = add(meta, stay, arrived)
            come[key] = (to_near if tag == "n" else over_far)(total[key])

    def joined(tag, chunks):
        return join(meta, [total[tag, k] for k in chunks], [come[tag, k] for k in chunks])

    near_own, extra = joined("n", range(CHUNKS))
    near_swap = over(swap_target)(near_own)
    near_back = over(hop_of(near_target))(near_own)
    near_back = over(after_hop(near_target))(near_back)
    far_own, far_back = [], []
    for chunks in ((0, 1), (2,), (3,)):
        far_own += joined("f", chunks)
        far_back.append(over(far_target)(far_own[-1]))
    fixed = (t, v, row_gap, col_gap)
    pair = most(meta, t, near_own, near_swap, near_back, extra, far_own[0], far_back[0], *fixed)
    pair = late(meta, False, 2, far_own[1:], *pair, *fixed)
    pair = late(meta, True, 2, far_back[1:2], *pair, *fixed)
    return late(meta, True, 3, far_back[2:], *pair, *fixed)


NEAR_GROUPS = ((1, (1, 2, 3)), (0, (0,)), (0, (1, 2, 3)))
FAR_GROUPS = (("s0", 1, 0, 2), ("k0", 0, 0, 2), ("s1", 1, 2, 2), ("k1", 0, 2, 2))


def gap_slices(shape, occ_energy, vir_energy):
    tile_rows, tile_cols = shape
    gaps = (vir_energy[None, :] - occ_energy[:, None]).reshape(-1)
    row_gap = lax.dynamic_slice_in_dim(gaps, lax.axis_index("row") * tile_rows, tile_rows, 0)
    col_gap = lax.dynamic_slice_in_dim(gaps, lax.axis_index("col") * tile_cols, tile_cols, 0)
    return row_gap[:, None], col_gap[None, :]


def split_local(amplitudes, interaction, occ_energy, vir_energy):
    gaps = gap_slices(amplitudes.shape, occ_energy, vir_energy)
    return tuple(split_update(amplitudes, interaction, *gaps))


def general_local(amplitudes, interaction, occ_energy, vir_energy):
    row_gap, col_gap = gap_slices(amplitudes.shape, occ_energy, vir_energy)
    denom = row_gap + col_gap
    residual = interaction + general_sum(amplitudes, interaction) + denom * amplitudes
    updated = amplitudes - residual / denom
    return (updated, residual)


def solution(mesh):
    rows, cols = mesh.shape["row"], mesh.shape["col"]
    split = cols == 4 and rows == 2 * cols
    return jax.shard_map(
        split_local if split else general_local,
        mesh=mesh,
        in_specs=(P("row", "col"), P("row", "col"), P(), P()),
        out_specs=(P("row", "col"), P("row", "col")),
        check_vma=False,
    )
```

```python
import functools

import jax
import jax.numpy as jnp
from jax import lax
from jax.experimental import pallas as pl
from jax.experimental.pallas import tpu as pltpu
from jax.sharding import PartitionSpec as P


CHUNKS = 4
PAD = 8


def swapped(block, axis, distance):
    count = lax.axis_size(axis)
    route = []
    for low in range(count):
        high = low | 1 << distance
        if high != low and high < count:
            route += [(low, high), (high, low)]
    return lax.ppermute(block, axis, route)


def from_behind(block, axis, distance):
    devices = range(lax.axis_size(axis))
    route = [(i - distance, i) for i in devices if i - distance in devices]
    return lax.ppermute(block, axis, route)


def contract(left_tile, right_tile):
    right_panel = lax.all_gather(right_tile, "row", axis=0, tiled=True)
    return jnp.dot(
        lax.all_gather(left_tile, "col", axis=1, tiled=True),
        right_panel,
        precision=lax.Precision.HIGHEST,
        preferred_element_type=jnp.float32,
    )


def diagonal_tile(tile, row_place, col_place):
    tile_rows = tile.shape[0]
    col_count = lax.axis_size("col")
    ratio = lax.axis_size("row") // col_count
    ratio_bits = ratio.bit_length() - 1
    row_bits = lax.axis_size("row").bit_length() - 1
    blocks = tile.reshape(tile_rows, ratio, tile_rows).transpose(1, 2, 0)
    for bit_index in range(row_bits):
        row_flag = row_place // 2**bit_index % 2
        if bit_index < ratio_bits:
            lower = 2**bit_index
            grouped = blocks.reshape(ratio // (2 * lower), 2, lower, tile_rows, tile_rows)
            zero_half = grouped[:, 0]
            one_half = grouped[:, 1]
            outgoing = jnp.where(row_flag == 0, one_half, zero_half)
            incoming = swapped(outgoing, "row", bit_index)
            new_zero = jnp.where(row_flag == 1, incoming, zero_half)
            new_one = jnp.where(row_flag == 0, incoming, one_half)
            blocks = jnp.stack([new_zero, new_one], axis=1).reshape(ratio, tile_rows, tile_rows)
        else:
            col_flag = col_place // 2 ** (bit_index - ratio_bits) % 2
            stride = 2**bit_index * col_count - 2 ** (bit_index - ratio_bits)
            from_above = from_behind(blocks, ("row", "col"), -stride)
            from_below = from_behind(blocks, ("row", "col"), stride)
            incoming = jnp.where(row_flag == 0, from_above, from_below)
            blocks = jnp.where(row_flag != col_flag, incoming, blocks)
    return blocks.transpose(1, 0, 2).reshape(tile_rows, ratio * tile_rows)


def general_sum(amplitudes, interaction):
    product = contract(amplitudes, interaction)
    mirrored = diagonal_tile(product, lax.axis_index("row"), lax.axis_index("col"))
    return product + mirrored


def routed(block, target):
    rows, cols = lax.axis_size("row"), lax.axis_size("col")
    route = []
    for r in range(rows):
        for c in range(cols):
            place = target(r, c)
            if place is not None:
                route.append((r * cols + c, place[0] * cols + place[1]))
    return lax.ppermute(block, ("row", "col"), route)


def is_near(r, c):
    return r >> 2 == c >> 1


def flips(z, c):
    return (z > c) ^ ((z ^ c) == 3)


def flipped(z, x, c):
    return x ^ flips(z, c)


def swap_target(r, c):
    return (r ^ 1, c) if r >> 1 == c else None


def near_target(r, c):
    z, x = r >> 1, r & 1
    if not is_near(r, c) or z == c:
        return None
    return (2 * c + flipped(z, x, c), z)


def far_target(r, c):
    z, x = r >> 1, r & 1
    if not is_near(r, c):
        return None
    return (2 * c + flipped(z ^ 2, x, c), z ^ 2)


def hop_of(target):
    return lambda r, c: target(r, c) and (r, c ^ 2)


def after_hop(target):
    return lambda r, c: target(r, c ^ 2)


X_PLACE, ODD, TURN_1, TURN_2, TURN_3, NEAR, MIDDLE, PLACE = range(8)
VMEM = 40 * 2**20


def params():
    return pltpu.CompilerParams(vmem_limit_bytes=VMEM)


def zeros(count):
    return (0,) * count


def call(kernel, shapes, meta, args, in_specs=None, out_specs=None, scratch=(), aliases=None):
    if in_specs is None:
        in_specs = [None] * len(args)
    if out_specs is None:
        out_specs = [None] * len(shapes)
    whole = lambda a: pl.BlockSpec(a.shape, lambda i, m: zeros(len(a.shape)))
    return pl.pallas_call(
        kernel,
        out_shape=list(shapes),
        grid_spec=pltpu.PrefetchScalarGridSpec(
            num_scalar_prefetch=1,
            grid=(1,),
            in_specs=[s or whole(a) for s, a in zip(in_specs, args)],
            out_specs=[s or whole(a) for s, a in zip(out_specs, shapes)],
            scratch_shapes=list(scratch),
        ),
        input_output_aliases=aliases or {},
        compiler_params=params(),
    )(meta, *args)


def shaped(*shape):
    return jax.ShapeDtypeStruct(shape, jnp.float32)


def halves(value):
    high = value.astype(jnp.bfloat16)
    return high, (value - high.astype(jnp.float32)).astype(jnp.bfloat16)


def joined_left(t_high, t_low, v_high, v_low):
    return jnp.concatenate([t_high, t_high, t_low, v_high, v_high, v_low], axis=1)


def left_of(t, v):
    t_high, t_low = halves(t.T)
    v_high, v_low = halves(v.T)
    return joined_left(t_high, t_low, v_high, v_low)


def own_left(own_ref, cols):
    return joined_left(*(own_ref[i, :, cols].T for i in range(4)))


def own_right(own_ref, cols):
    return jnp.concatenate([own_ref[i, :, cols] for i in (2, 3, 2, 0, 1, 0)], axis=0)


def crossed(left, right):
    return jnp.dot(left, right, preferred_element_type=jnp.float32)


def placed(place, n, offset=0, size=None):
    return pl.ds(pl.multiple_of(place * n + offset, 128), size or n)


def pick_kernel(side, first, m, t_ref, v_ref, out_ref, sems):
    n = t_ref.shape[0]
    cols = placed(m[X_PLACE] ^ side, n, first, out_ref.shape[2])
    copies = [
        pltpu.make_async_copy(ref.at[:, cols], out_ref.at[i], sems.at[i])
        for i, ref in enumerate((t_ref, v_ref))
    ]
    for copy in copies:
        copy.start()
    for copy in copies:
        copy.wait()


def pick(meta, t, v, side, first, count):
    n = t.shape[0]
    w = n // CHUNKS
    hbm = pl.BlockSpec(memory_space=pltpu.MemorySpace.HBM)
    return call(
        functools.partial(pick_kernel, side, first * w),
        [shaped(2, n, count * w)],
        meta,
        [t, v],
        in_specs=[hbm, hbm],
        scratch=[pltpu.SemaphoreType.DMA((2,))],
    )[0]


def prep_kernel(_, t_ref, v_ref, own_ref):
    own_ref[0], own_ref[1] = halves(t_ref[...])
    own_ref[2], own_ref[3] = halves(v_ref[...])


def prep(meta, t, v):
    return call(prep_kernel, [jax.ShapeDtypeStruct((4, *t.shape), jnp.bfloat16)], meta, [t, v])[0]


def lines(k, w):
    return w + PAD if k == CHUNKS - 1 else w


def middle_block(m, side, chunks, own_ref, outs):
    n = own_ref.shape[1]
    w = n // CHUNKS
    half = m[X_PLACE] ^ side
    same, cross = placed(half, n), placed(1 - half, n)
    left = own_left(own_ref, placed(half, n, chunks[0] * w, len(chunks) * w))
    diagonal = crossed(left, own_right(own_ref, same))
    aside = crossed(left, own_right(own_ref, cross))
    lane = lax.broadcasted_iota(jnp.int32, (w, n), 1)
    for i, (k, out_ref) in enumerate(zip(chunks, outs)):
        line = lax.broadcasted_iota(jnp.int32, (w, n), 0) + k * w
        rows = slice(i * w, (i + 1) * w)
        out_ref[0, :w, :] = jnp.where(line >= lane, diagonal[rows], aside[rows])
        if out_ref.shape[1] > w:
            whole = lambda i, cols: own_ref[i, :, cols].astype(jnp.float32) + own_ref[
                i + 1, :, cols
            ].astype(jnp.float32)
            products = whole(0, same) * whole(2, cross) + whole(2, same) * whole(0, cross)
            extra = jnp.sum(products, axis=0, keepdims=True)
            out_ref[0, w:, :] = jnp.broadcast_to(extra, (PAD, n))


def middle_kernel(side, k, m, own_ref, out_ref):
    middle_block(m, side, (k,), own_ref, [out_ref])


def middle_part(meta, own, side, k):
    n = own.shape[1]
    w = lines(k, n // CHUNKS)
    return call(
        functools.partial(middle_kernel, side, k),
        [shaped(2, w, n)],
        meta,
        [own],
        out_specs=[pl.BlockSpec((1, w, n), lambda i, m: (0, 0, 0))],
    )[0]


def next_part(meta, base, at, av, own, side, k):
    n = own.shape[1]
    w = n // CHUNKS
    block = pl.BlockSpec((n, w), lambda i, m: (0, (m[X_PLACE] ^ side) * CHUNKS + k))
    return call(
        functools.partial(next_kernel, side),
        [shaped(*base.shape)],
        meta,
        [base, at, av, own],
        in_specs=[pl.BlockSpec(memory_space=pl.ANY), block, block, None],
        out_specs=[pl.BlockSpec((1, *base.shape[1:]), lambda i, m: (1, 0, 0))],
        aliases={1: 0},
    )[0]


def next_kernel(side, m, _, at_ref, av_ref, own_ref, out_ref):
    n = own_ref.shape[1]
    w = at_ref.shape[1]
    right = own_right(own_ref, placed(m[TURN_1] ^ side, n))
    out_ref[0, :w, :] = crossed(left_of(at_ref[...], av_ref[...]), right)


def near_parts(meta, at, av, own, side, chunks):
    n = own.shape[1]
    w = n // CHUNKS
    half = pl.BlockSpec((n, n), lambda i, m: (0, m[X_PLACE] ^ side))
    return call(
        functools.partial(near_kernel, side, chunks),
        [shaped(2, lines(k, w), n) for k in chunks],
        meta,
        [at, av, own],
        in_specs=[half, half, None],
    )


def near_kernel(side, chunks, m, at_ref, av_ref, own_ref, *outs):
    n = own_ref.shape[1]
    w = n // CHUNKS
    middle_block(m, side, chunks, own_ref, outs)
    cols = slice(chunks[0] * w, (chunks[-1] + 1) * w)
    right = own_right(own_ref, placed(m[TURN_1] ^ side, n))
    block = crossed(left_of(at_ref[:, cols], av_ref[:, cols]), right)
    for i, out_ref in enumerate(outs):
        out_ref[1, :w, :] = block[i * w : (i + 1) * w]
        if out_ref.shape[1] > w:
            out_ref[1, w:, :] = jnp.zeros((PAD, n), jnp.float32)


def far_kernel(side, m, a_ref, b_ref, own_ref, *outs):
    n = own_ref.shape[1]
    w = outs[0].shape[1]
    for d, (ref, turn) in enumerate(((a_ref, TURN_2), (b_ref, TURN_3))):
        right = own_right(own_ref, placed(m[turn] ^ side, n))
        block = crossed(left_of(ref[0], ref[1]), right)
        for i, out_ref in enumerate(outs):
            out_ref[d] = block[i * w : (i + 1) * w]


def far_parts(meta, a, b, own, side):
    n = own.shape[1]
    w = n // CHUNKS
    return call(
        functools.partial(far_kernel, side),
        [shaped(2, w, n)] * (a.shape[2] // w),
        meta,
        [a, b, own],
    )


def fold_kernel(_, keep_pass, come_pass, keep_stay, come_stay, pass_ref, stay_ref):
    pass_ref[...] = keep_pass[0] + come_pass[0]
    stay_ref[...] = keep_stay[0] + come_stay[0]


def fold(meta, keep, come):
    _, lines, n = keep.shape
    leave = pl.BlockSpec((1, lines, n), lambda i, m: (1 - m[ODD], 0, 0))
    stay = pl.BlockSpec((1, lines, n), lambda i, m: (m[ODD], 0, 0))
    return call(
        fold_kernel,
        [shaped(lines, n)] * 2,
        meta,
        [keep, come, keep, come],
        in_specs=[leave, leave, stay, stay],
    )


def add_kernel(_, a_ref, b_ref, out_ref):
    out_ref[...] = a_ref[...] + b_ref[...]


def add(meta, a, b):
    return call(add_kernel, [shaped(*a.shape)], meta, [a, b])[0]


def join_kernel(w, count, _, *refs):
    out_ref = refs[2 * count]
    for k in range(count):
        a_ref, b_ref = refs[k], refs[count + k]
        out_ref[k * w : (k + 1) * w, :] = a_ref[:w, :] + b_ref[:w, :]
        if a_ref.shape[0] > w:
            refs[2 * count + 1][...] = a_ref[w:, :] + b_ref[w:, :]


def join(meta, parts, comes):
    n = parts[0].shape[1]
    w = n // CHUNKS
    shapes = [shaped(len(parts) * w, n)]
    if parts[-1].shape[0] > w:
        shapes.append(shaped(PAD, n))
    return call(functools.partial(join_kernel, w, len(parts)), shapes, meta, [*parts, *comes])


def closing(t, v, row, col, value):
    denom = row + col
    residual = v + value + denom * t
    return t - residual / denom, residual


def grid_of(n):
    line = lax.broadcasted_iota(jnp.int32, (n, n), 0)
    return line, lax.broadcasted_iota(jnp.int32, (n, n), 1)


def most_kernel(m, near_ref, far_ref, t_ref, v_ref, row_ref, col_ref, new_ref, res_ref):
    n = t_ref.shape[0]

    def write(value):
        rows = slice(0, value.shape[0])
        new_ref[rows], res_ref[rows] = closing(
            t_ref[rows], v_ref[rows], row_ref[rows], col_ref[...], value
        )

    @pl.when(m[NEAR] == 0)
    def _():
        write(far_ref[...])

    @pl.when((m[NEAR] == 1) & (m[MIDDLE] == 0))
    def _():
        write(near_ref[...])

    @pl.when(m[MIDDLE] == 1)
    def _():
        line, lane = grid_of(n)
        own = near_ref[...]
        write(jnp.where(line >= lane, own, own.T))


def half_specs(n, at):
    block = pl.BlockSpec((n, n), lambda i, m: (0, at(m)))
    return [block, block, None, pl.BlockSpec((1, n), lambda i, m: (0, at(m)))], [block, block]


def most(meta, near_own, far_own, t, *args):
    ins, outs = half_specs(t.shape[0], lambda m: m[PLACE])
    return call(
        most_kernel,
        [shaped(*t.shape)] * 2,
        meta,
        [near_own, far_own, t, *args],
        in_specs=[None, None, *ins],
        out_specs=outs,
    )


def back_kernel(m, near_ref, swap_ref, back_ref, extra_ref, *refs):
    far = refs[:3]
    t_ref, v_ref, row_ref, col_ref, _, _, new_ref, res_ref = refs[3:]
    n = t_ref.shape[0]

    def write(value, cols=slice(None)):
        new_ref[:, cols], res_ref[:, cols] = closing(
            t_ref[:, cols], v_ref[:, cols], row_ref[...], col_ref[:, cols], value
        )

    @pl.when(m[NEAR] == 0)
    def _():
        first = 0
        for ref in far:
            write(ref[...].T, slice(first, first + ref.shape[0]))
            first += ref.shape[0]

    @pl.when((m[NEAR] == 1) & (m[MIDDLE] == 0))
    def _():
        write(back_ref[...].T)

    @pl.when(m[MIDDLE] == 1)
    def _():
        line, lane = grid_of(n)
        lower = jnp.where(line > lane, swap_ref[...].T, extra_ref[:1, :])
        write(jnp.where(line < lane, near_ref[...], lower))


def back_half(meta, values, new, res, t, *args):
    ins, outs = half_specs(t.shape[0], lambda m: 1 - m[PLACE])
    hbm = pl.BlockSpec(memory_space=pl.ANY)
    count = len(values) + 4
    return call(
        back_kernel,
        [shaped(*t.shape)] * 2,
        meta,
        [*values, t, *args, new, res],
        in_specs=[*[None] * len(values), *ins, hbm, hbm],
        out_specs=outs,
        aliases={count + 1: 0, count + 2: 1},
    )


def late_kernel(chunk, count, m, *refs):
    values = refs[:count]
    t_ref, v_ref, row_ref, col_ref, new_ref, res_ref, new, res, sems = refs[count + 2 :]
    w, n = values[0].shape

    @pl.when(m[NEAR] == 0)
    def _():
        value = jnp.concatenate([ref[...] for ref in values], axis=0)
        new[...], res[...] = closing(
            t_ref[...], v_ref[...], row_ref[...], col_ref[...], value
        )
        rows, cols = pl.ds(chunk * w, count * w), placed(m[PLACE], n)
        copies = [
            pltpu.make_async_copy(source, target.at[rows, cols], sems.at[i])
            for i, (source, target) in enumerate(((new, new_ref), (res, res_ref)))
        ]
        for copy in copies:
            copy.start()
        for copy in copies:
            copy.wait()


def late(meta, chunk, values, new, res, t, v, row_gap, col_gap):
    w, n = values[0].shape
    count = len(values)
    block = pl.BlockSpec((count * w, n), lambda i, m: (chunk // count, m[PLACE]))
    row = pl.BlockSpec((count * w, 1), lambda i, m: (chunk // count, 0))
    col = pl.BlockSpec((1, n), lambda i, m: (0, m[PLACE]))
    hbm = pl.BlockSpec(memory_space=pl.ANY)
    return call(
        functools.partial(late_kernel, chunk, count),
        [shaped(*t.shape)] * 2,
        meta,
        [*values, new, res, t, v, row_gap, col_gap],
        in_specs=[*[None] * count, hbm, hbm, block, block, row, col],
        out_specs=[hbm, hbm],
        scratch=[pltpu.VMEM(block.block_shape, jnp.float32)] * 2 + [pltpu.SemaphoreType.DMA((2,))],
        aliases={count + 1: 0, count + 2: 1},
    )


def split_update(t, v, row_gap, col_gap):
    r = lax.axis_index("row")
    c = lax.axis_index("col")
    z, x = r // 2, r % 2
    slot = lax.iota(jnp.int32, 8)
    values = {
        X_PLACE: x,
        ODD: (z + c) % 2,
        TURN_1: x ^ flips(c ^ 1, c),
        TURN_2: x ^ flips(c ^ 2, c),
        TURN_3: x ^ flips(c ^ 3, c),
        NEAR: r // 4 == c // 2,
        MIDDLE: z == c,
        PLACE: x ^ flips(z, c),
    }
    meta = jnp.zeros((8,), jnp.int32)
    for index, value in values.items():
        meta = jnp.where(slot == index, value.astype(jnp.int32), meta)

    across = lambda block: routed(block, lambda r, c: (r, c ^ 2))
    beside = lambda block: routed(block, lambda r, c: (r, c ^ 1))
    over_x = lambda block: routed(block, lambda r, c: (r ^ 1, c))
    over_z = lambda block: routed(block, lambda r, c: (r ^ 2, c))
    over_far = lambda block: routed(block, lambda r, c: (r ^ 4, c))
    to_near = lambda block: routed(block, lambda r, c: None if is_near(r, c) else (r ^ 4, c))
    over = lambda target: lambda block: routed(block, target)

    next_t = beside(t)
    next_v = beside(v)
    own = prep(meta, t, v)
    send, keep = {}, {}
    base = middle_part(meta, own, 1, 0)
    send["n", 0] = next_part(meta, base, next_t, next_v, own, 1, 0)
    for side, chunks in NEAR_GROUPS:
        blocks = near_parts(meta, next_t, next_v, own, side, chunks)
        for k, block in zip(chunks, blocks):
            (send if side else keep)["n", k] = block
    for tag, side, first, count in FAR_GROUPS:
        piece = pick(meta, t, v, side, first, count)
        piece = across(piece)
        other = beside(piece)
        blocks = far_parts(meta, piece, other, own, side)
        for i, block in enumerate(blocks):
            (send if side else keep)["f", first + i] = block
    total, come = {}, {}
    for tag in "nf":
        for k in range(CHUNKS):
            key = tag, k
            arrived = over_x(send[key])
            leave, stay = fold(meta, keep[key], arrived)
            arrived = over_z(leave)
            total[key] = add(meta, stay, arrived)
            come[key] = (to_near if tag == "n" else over_far)(total[key])

    def joined(tag, chunks):
        return join(meta, [total[tag, k] for k in chunks], [come[tag, k] for k in chunks])

    near_own, extra = joined("n", range(CHUNKS))
    near_swap = over(swap_target)(near_own)
    near_back = over(hop_of(near_target))(near_own)
    near_back = over(after_hop(near_target))(near_back)
    far_own, far_back = [], []
    for chunks in ((0, 1), (2,), (3,)):
        far_own += joined("f", chunks)
        far_back.append(over(far_target)(far_own[-1]))
    fixed = (t, v, row_gap, col_gap)
    pair = most(meta, near_own, far_own[0], *fixed)
    pair = late(meta, 2, far_own[1:], *pair, *fixed)
    values = [near_own, near_swap, near_back, extra, *far_back]
    return back_half(meta, values, *pair, *fixed)


NEAR_GROUPS = ((1, (1, 2, 3)), (0, (0,)), (0, (1, 2, 3)))
FAR_GROUPS = (("s0", 1, 0, 2), ("k0", 0, 0, 2), ("s1", 1, 2, 2), ("k1", 0, 2, 2))


def gap_slices(shape, occ_energy, vir_energy):
    tile_rows, tile_cols = shape
    gaps = (vir_energy[None, :] - occ_energy[:, None]).reshape(-1)
    row_gap = lax.dynamic_slice_in_dim(gaps, lax.axis_index("row") * tile_rows, tile_rows, 0)
    col_gap = lax.dynamic_slice_in_dim(gaps, lax.axis_index("col") * tile_cols, tile_cols, 0)
    return row_gap[:, None], col_gap[None, :]


def split_local(amplitudes, interaction, occ_energy, vir_energy):
    gaps = gap_slices(amplitudes.shape, occ_energy, vir_energy)
    return tuple(split_update(amplitudes, interaction, *gaps))


def general_local(amplitudes, interaction, occ_energy, vir_energy):
    row_gap, col_gap = gap_slices(amplitudes.shape, occ_energy, vir_energy)
    denom = row_gap + col_gap
    residual = interaction + general_sum(amplitudes, interaction) + denom * amplitudes
    updated = amplitudes - residual / denom
    return (updated, residual)


def solution(mesh):
    rows, cols = mesh.shape["row"], mesh.shape["col"]
    split = cols == 4 and rows == 2 * cols
    return jax.shard_map(
        split_local if split else general_local,
        mesh=mesh,
        in_specs=(P("row", "col"), P("row", "col"), P(), P()),
        out_specs=(P("row", "col"), P("row", "col")),
        check_vma=False,
    )
```

```python
import functools

import jax
import jax.numpy as jnp
from jax import lax
from jax.experimental import pallas as pl
from jax.experimental.pallas import tpu as pltpu
from jax.sharding import PartitionSpec as P


CHUNKS = 4
PAD = 8


def swapped(block, axis, distance):
    count = lax.axis_size(axis)
    route = []
    for low in range(count):
        high = low | 1 << distance
        if high != low and high < count:
            route += [(low, high), (high, low)]
    return lax.ppermute(block, axis, route)


def from_behind(block, axis, distance):
    devices = range(lax.axis_size(axis))
    route = [(i - distance, i) for i in devices if i - distance in devices]
    return lax.ppermute(block, axis, route)


def contract(left_tile, right_tile):
    right_panel = lax.all_gather(right_tile, "row", axis=0, tiled=True)
    return jnp.dot(
        lax.all_gather(left_tile, "col", axis=1, tiled=True),
        right_panel,
        precision=lax.Precision.HIGHEST,
        preferred_element_type=jnp.float32,
    )


def diagonal_tile(tile, row_place, col_place):
    tile_rows = tile.shape[0]
    col_count = lax.axis_size("col")
    ratio = lax.axis_size("row") // col_count
    ratio_bits = ratio.bit_length() - 1
    row_bits = lax.axis_size("row").bit_length() - 1
    blocks = tile.reshape(tile_rows, ratio, tile_rows).transpose(1, 2, 0)
    for bit_index in range(row_bits):
        row_flag = row_place // 2**bit_index % 2
        if bit_index < ratio_bits:
            lower = 2**bit_index
            grouped = blocks.reshape(ratio // (2 * lower), 2, lower, tile_rows, tile_rows)
            zero_half = grouped[:, 0]
            one_half = grouped[:, 1]
            outgoing = jnp.where(row_flag == 0, one_half, zero_half)
            incoming = swapped(outgoing, "row", bit_index)
            new_zero = jnp.where(row_flag == 1, incoming, zero_half)
            new_one = jnp.where(row_flag == 0, incoming, one_half)
            blocks = jnp.stack([new_zero, new_one], axis=1).reshape(ratio, tile_rows, tile_rows)
        else:
            col_flag = col_place // 2 ** (bit_index - ratio_bits) % 2
            stride = 2**bit_index * col_count - 2 ** (bit_index - ratio_bits)
            from_above = from_behind(blocks, ("row", "col"), -stride)
            from_below = from_behind(blocks, ("row", "col"), stride)
            incoming = jnp.where(row_flag == 0, from_above, from_below)
            blocks = jnp.where(row_flag != col_flag, incoming, blocks)
    return blocks.transpose(1, 0, 2).reshape(tile_rows, ratio * tile_rows)


def general_sum(amplitudes, interaction):
    product = contract(amplitudes, interaction)
    mirrored = diagonal_tile(product, lax.axis_index("row"), lax.axis_index("col"))
    return product + mirrored


def routed(block, target):
    rows, cols = lax.axis_size("row"), lax.axis_size("col")
    route = []
    for r in range(rows):
        for c in range(cols):
            place = target(r, c)
            if place is not None:
                route.append((r * cols + c, place[0] * cols + place[1]))
    return lax.ppermute(block, ("row", "col"), route)


def is_near(r, c):
    return r >> 2 == c >> 1


def flips(z, c):
    return (z > c) ^ ((z ^ c) == 3)


def flipped(z, x, c):
    return x ^ flips(z, c)


def swap_target(r, c):
    return (r ^ 1, c) if r >> 1 == c else None


def near_target(r, c):
    z, x = r >> 1, r & 1
    if not is_near(r, c) or z == c:
        return None
    return (2 * c + flipped(z, x, c), z)


def far_target(r, c):
    z, x = r >> 1, r & 1
    if not is_near(r, c):
        return None
    return (2 * c + flipped(z ^ 2, x, c), z ^ 2)


def hop_of(target):
    return lambda r, c: target(r, c) and (r, c ^ 2)


def after_hop(target):
    return lambda r, c: target(r, c ^ 2)


X_PLACE, ODD, TURN_1, TURN_2, TURN_3, NEAR, MIDDLE, PLACE = range(8)
SMALL, MEDIUM, LARGE, WHOLE = 8 * 2**20, 24 * 2**20, 40 * 2**20, 60 * 2**20


def zeros(count):
    return (0,) * count


def call(kernel, shapes, meta, args, in_specs=None, out_specs=None, scratch=(), aliases=None, vmem=LARGE):
    if in_specs is None:
        in_specs = [None] * len(args)
    if out_specs is None:
        out_specs = [None] * len(shapes)
    whole = lambda a: pl.BlockSpec(a.shape, lambda i, m: zeros(len(a.shape)))
    return pl.pallas_call(
        kernel,
        out_shape=list(shapes),
        grid_spec=pltpu.PrefetchScalarGridSpec(
            num_scalar_prefetch=1,
            grid=(1,),
            in_specs=[s or whole(a) for s, a in zip(in_specs, args)],
            out_specs=[s or whole(a) for s, a in zip(out_specs, shapes)],
            scratch_shapes=list(scratch),
        ),
        input_output_aliases=aliases or {},
        compiler_params=pltpu.CompilerParams(vmem_limit_bytes=vmem),
    )(meta, *args)


def shaped(*shape):
    return jax.ShapeDtypeStruct(shape, jnp.float32)


def halves(value):
    high = value.astype(jnp.bfloat16)
    return high, (value - high.astype(jnp.float32)).astype(jnp.bfloat16)


def joined_left(t_high, t_low, v_high, v_low):
    return jnp.concatenate([t_high, t_high, t_low, v_high, v_high, v_low], axis=1)


def left_of(t, v):
    t_high, t_low = halves(t.T)
    v_high, v_low = halves(v.T)
    return joined_left(t_high, t_low, v_high, v_low)


def own_left(own_ref, cols):
    return joined_left(*(own_ref[i, :, cols].T for i in range(4)))


def own_right(own_ref, cols):
    return jnp.concatenate([own_ref[i, :, cols] for i in (2, 3, 2, 0, 1, 0)], axis=0)


def crossed(left, right):
    return jnp.dot(left, right, preferred_element_type=jnp.float32)


def placed(place, n, offset=0, size=None):
    return pl.ds(pl.multiple_of(place * n + offset, 128), size or n)


def pick_kernel(side, first, m, t_ref, v_ref, out_ref, sems):
    n = t_ref.shape[0]
    cols = placed(m[X_PLACE] ^ side, n, first, out_ref.shape[2])
    copies = [
        pltpu.make_async_copy(ref.at[:, cols], out_ref.at[i], sems.at[i])
        for i, ref in enumerate((t_ref, v_ref))
    ]
    for copy in copies:
        copy.start()
    for copy in copies:
        copy.wait()


def pick(meta, t, v, side, first, count):
    n = t.shape[0]
    w = n // CHUNKS
    hbm = pl.BlockSpec(memory_space=pltpu.MemorySpace.HBM)
    return call(
        functools.partial(pick_kernel, side, first * w),
        [shaped(2, n, count * w)],
        meta,
        [t, v],
        in_specs=[hbm, hbm],
        scratch=[pltpu.SemaphoreType.DMA((2,))],
        vmem=LARGE if first or not side else WHOLE,
    )[0]


def prep_kernel(_, t_ref, v_ref, own_ref):
    own_ref[0], own_ref[1] = halves(t_ref[...])
    own_ref[2], own_ref[3] = halves(v_ref[...])


def prep(meta, t, v):
    return call(prep_kernel, [jax.ShapeDtypeStruct((4, *t.shape), jnp.bfloat16)], meta, [t, v])[0]


def lines(k, w):
    return w + PAD if k == CHUNKS - 1 else w


def middle_block(m, side, chunks, own_ref, outs):
    n = own_ref.shape[1]
    w = n // CHUNKS
    half = m[X_PLACE] ^ side
    same, cross = placed(half, n), placed(1 - half, n)
    left = own_left(own_ref, placed(half, n, chunks[0] * w, len(chunks) * w))
    diagonal = crossed(left, own_right(own_ref, same))
    aside = crossed(left, own_right(own_ref, cross))
    lane = lax.broadcasted_iota(jnp.int32, (w, n), 1)
    for i, (k, out_ref) in enumerate(zip(chunks, outs)):
        line = lax.broadcasted_iota(jnp.int32, (w, n), 0) + k * w
        rows = slice(i * w, (i + 1) * w)
        out_ref[0, :w, :] = jnp.where(line >= lane, diagonal[rows], aside[rows])
        if out_ref.shape[1] > w:
            whole = lambda i, cols: own_ref[i, :, cols].astype(jnp.float32) + own_ref[
                i + 1, :, cols
            ].astype(jnp.float32)
            products = whole(0, same) * whole(2, cross) + whole(2, same) * whole(0, cross)
            extra = jnp.sum(products, axis=0, keepdims=True)
            out_ref[0, w:, :] = jnp.broadcast_to(extra, (PAD, n))


def middle_kernel(side, k, m, own_ref, out_ref):
    middle_block(m, side, (k,), own_ref, [out_ref])


def middle_part(meta, own, side, k):
    n = own.shape[1]
    w = lines(k, n // CHUNKS)
    return call(
        functools.partial(middle_kernel, side, k),
        [shaped(2, w, n)],
        meta,
        [own],
        out_specs=[pl.BlockSpec((1, w, n), lambda i, m: (0, 0, 0))],
    )[0]


def next_part(meta, base, piece, own, side):
    n = own.shape[1]
    w = n // CHUNKS
    return call(
        functools.partial(next_kernel, side),
        [shaped(*base.shape)],
        meta,
        [base, piece, own],
        in_specs=[
            pl.BlockSpec(memory_space=pl.ANY),
            pl.BlockSpec((2, n, w), lambda i, m: (0, 0, 0)),
            None,
        ],
        out_specs=[pl.BlockSpec((1, *base.shape[1:]), lambda i, m: (1, 0, 0))],
        aliases={1: 0},
    )[0]


def next_kernel(side, m, _, piece_ref, own_ref, out_ref):
    n = own_ref.shape[1]
    right = own_right(own_ref, placed(m[TURN_1] ^ side, n))
    out_ref[0] = crossed(left_of(piece_ref[0], piece_ref[1]), right)


def near_parts(meta, pieces, own, side, chunks):
    n = own.shape[1]
    w = n // CHUNKS
    return call(
        functools.partial(near_kernel, side, chunks),
        [shaped(2, lines(k, w), n) for k in chunks],
        meta,
        [*pieces, own],
    )


def near_kernel(side, chunks, m, *refs):
    pieces, own_ref, outs = refs[: -1 - len(chunks)], refs[-1 - len(chunks)], refs[-len(chunks) :]
    n = own_ref.shape[1]
    w = n // CHUNKS
    middle_block(m, side, chunks, own_ref, outs)
    left = jnp.concatenate([left_of(ref[0], ref[1]) for ref in pieces], axis=0)
    first = chunks[0] * w
    left = left[first : first + len(chunks) * w]
    block = crossed(left, own_right(own_ref, placed(m[TURN_1] ^ side, n)))
    for i, out_ref in enumerate(outs):
        out_ref[1, :w, :] = block[i * w : (i + 1) * w]
        if out_ref.shape[1] > w:
            out_ref[1, w:, :] = jnp.zeros((PAD, n), jnp.float32)


def far_kernel(side, m, a_ref, b_ref, own_ref, *outs):
    n = own_ref.shape[1]
    w = outs[0].shape[1]
    for d, (ref, turn) in enumerate(((a_ref, TURN_2), (b_ref, TURN_3))):
        right = own_right(own_ref, placed(m[turn] ^ side, n))
        block = crossed(left_of(ref[0], ref[1]), right)
        for i, out_ref in enumerate(outs):
            out_ref[d] = block[i * w : (i + 1) * w]


def far_parts(meta, a, b, own, side):
    n = own.shape[1]
    w = n // CHUNKS
    return call(
        functools.partial(far_kernel, side),
        [shaped(2, w, n)] * (a.shape[2] // w),
        meta,
        [a, b, own],
    )


def fold_kernel(_, keep_pass, come_pass, keep_stay, come_stay, pass_ref, stay_ref):
    pass_ref[...] = keep_pass[0] + come_pass[0]
    stay_ref[...] = keep_stay[0] + come_stay[0]


def fold(meta, keep, come):
    _, lines, n = keep.shape
    leave = pl.BlockSpec((1, lines, n), lambda i, m: (1 - m[ODD], 0, 0))
    stay = pl.BlockSpec((1, lines, n), lambda i, m: (m[ODD], 0, 0))
    return call(
        fold_kernel,
        [shaped(lines, n)] * 2,
        meta,
        [keep, come, keep, come],
        in_specs=[leave, leave, stay, stay],
        vmem=SMALL,
    )


def add_kernel(_, a_ref, b_ref, out_ref):
    out_ref[...] = a_ref[...] + b_ref[...]


def add(meta, a, b):
    return call(add_kernel, [shaped(*a.shape)], meta, [a, b], vmem=SMALL)[0]


def join_kernel(w, count, _, *refs):
    out_ref = refs[2 * count]
    for k in range(count):
        a_ref, b_ref = refs[k], refs[count + k]
        out_ref[k * w : (k + 1) * w, :] = a_ref[:w, :] + b_ref[:w, :]
        if a_ref.shape[0] > w:
            refs[2 * count + 1][...] = a_ref[w:, :] + b_ref[w:, :]


def join(meta, parts, comes):
    n = parts[0].shape[1]
    w = n // CHUNKS
    shapes = [shaped(len(parts) * w, n)]
    if parts[-1].shape[0] > w:
        shapes.append(shaped(PAD, n))
    return call(functools.partial(join_kernel, w, len(parts)), shapes, meta, [*parts, *comes], vmem=MEDIUM)


def closing(t, v, row, col, value):
    denom = row + col
    residual = v + value + denom * t
    return t - residual / denom, residual


def grid_of(n):
    line = lax.broadcasted_iota(jnp.int32, (n, n), 0)
    return line, lax.broadcasted_iota(jnp.int32, (n, n), 1)


def most_kernel(m, near_ref, far_ref, t_ref, v_ref, row_ref, col_ref, new_ref, res_ref):
    n = t_ref.shape[0]

    def write(value):
        rows = slice(0, value.shape[0])
        new_ref[rows], res_ref[rows] = closing(
            t_ref[rows], v_ref[rows], row_ref[rows], col_ref[...], value
        )

    @pl.when(m[NEAR] == 0)
    def _():
        write(far_ref[...])

    @pl.when((m[NEAR] == 1) & (m[MIDDLE] == 0))
    def _():
        write(near_ref[...])

    @pl.when(m[MIDDLE] == 1)
    def _():
        line, lane = grid_of(n)
        own = near_ref[...]
        write(jnp.where(line >= lane, own, own.T))


def half_specs(n, at):
    block = pl.BlockSpec((n, n), lambda i, m: (0, at(m)))
    return [block, block, None, pl.BlockSpec((1, n), lambda i, m: (0, at(m)))], [block, block]


def most(meta, near_own, far_own, t, *args):
    ins, outs = half_specs(t.shape[0], lambda m: m[PLACE])
    return call(
        most_kernel,
        [shaped(*t.shape)] * 2,
        meta,
        [near_own, far_own, t, *args],
        in_specs=[None, None, *ins],
        out_specs=outs,
        vmem=MEDIUM,
    )


def back_kernel(m, near_ref, swap_ref, back_ref, extra_ref, *refs):
    far = refs[:3]
    t_ref, v_ref, row_ref, col_ref, _, _, new_ref, res_ref = refs[3:]
    n = t_ref.shape[0]

    def write(value, cols=slice(None)):
        new_ref[:, cols], res_ref[:, cols] = closing(
            t_ref[:, cols], v_ref[:, cols], row_ref[...], col_ref[:, cols], value
        )

    @pl.when(m[NEAR] == 0)
    def _():
        first = 0
        for ref in far:
            write(ref[...].T, slice(first, first + ref.shape[0]))
            first += ref.shape[0]

    @pl.when((m[NEAR] == 1) & (m[MIDDLE] == 0))
    def _():
        write(back_ref[...].T)

    @pl.when(m[MIDDLE] == 1)
    def _():
        line, lane = grid_of(n)
        lower = jnp.where(line > lane, swap_ref[...].T, extra_ref[:1, :])
        write(jnp.where(line < lane, near_ref[...], lower))


def back_half(meta, values, new, res, t, *args):
    ins, outs = half_specs(t.shape[0], lambda m: 1 - m[PLACE])
    hbm = pl.BlockSpec(memory_space=pl.ANY)
    count = len(values) + 4
    return call(
        back_kernel,
        [shaped(*t.shape)] * 2,
        meta,
        [*values, t, *args, new, res],
        in_specs=[*[None] * len(values), *ins, hbm, hbm],
        out_specs=outs,
        aliases={count + 1: 0, count + 2: 1},
    )


def late_kernel(chunk, count, m, *refs):
    values = refs[:count]
    t_ref, v_ref, row_ref, col_ref, new_ref, res_ref, new, res, sems = refs[count + 2 :]
    w, n = values[0].shape

    @pl.when(m[NEAR] == 0)
    def _():
        value = jnp.concatenate([ref[...] for ref in values], axis=0)
        new[...], res[...] = closing(
            t_ref[...], v_ref[...], row_ref[...], col_ref[...], value
        )
        rows, cols = pl.ds(chunk * w, count * w), placed(m[PLACE], n)
        copies = [
            pltpu.make_async_copy(source, target.at[rows, cols], sems.at[i])
            for i, (source, target) in enumerate(((new, new_ref), (res, res_ref)))
        ]
        for copy in copies:
            copy.start()
        for copy in copies:
            copy.wait()


def late(meta, chunk, values, new, res, t, v, row_gap, col_gap):
    w, n = values[0].shape
    count = len(values)
    block = pl.BlockSpec((count * w, n), lambda i, m: (chunk // count, m[PLACE]))
    row = pl.BlockSpec((count * w, 1), lambda i, m: (chunk // count, 0))
    col = pl.BlockSpec((1, n), lambda i, m: (0, m[PLACE]))
    hbm = pl.BlockSpec(memory_space=pl.ANY)
    return call(
        functools.partial(late_kernel, chunk, count),
        [shaped(*t.shape)] * 2,
        meta,
        [*values, new, res, t, v, row_gap, col_gap],
        in_specs=[*[None] * count, hbm, hbm, block, block, row, col],
        out_specs=[hbm, hbm],
        scratch=[pltpu.VMEM(block.block_shape, jnp.float32)] * 2 + [pltpu.SemaphoreType.DMA((2,))],
        aliases={count + 1: 0, count + 2: 1},
    )


def split_update(t, v, row_gap, col_gap):
    r = lax.axis_index("row")
    c = lax.axis_index("col")
    z, x = r // 2, r % 2
    slot = lax.iota(jnp.int32, 8)
    values = {
        X_PLACE: x,
        ODD: (z + c) % 2,
        TURN_1: x ^ flips(c ^ 1, c),
        TURN_2: x ^ flips(c ^ 2, c),
        TURN_3: x ^ flips(c ^ 3, c),
        NEAR: r // 4 == c // 2,
        MIDDLE: z == c,
        PLACE: x ^ flips(z, c),
    }
    meta = jnp.zeros((8,), jnp.int32)
    for index, value in values.items():
        meta = jnp.where(slot == index, value.astype(jnp.int32), meta)

    across = lambda block: routed(block, lambda r, c: (r, c ^ 2))
    beside = lambda block: routed(block, lambda r, c: (r, c ^ 1))
    over_x = lambda block: routed(block, lambda r, c: (r ^ 1, c))
    over_z = lambda block: routed(block, lambda r, c: (r ^ 2, c))
    over_far = lambda block: routed(block, lambda r, c: (r ^ 4, c))
    to_near = lambda block: routed(block, lambda r, c: None if is_near(r, c) else (r ^ 4, c))
    over = lambda target: lambda block: routed(block, target)

    own = prep(meta, t, v)
    send, keep, pieces, nexts = {}, {}, {}, {}
    for tag, side, first, count in FAR_GROUPS:
        pieces[tag] = pick(meta, t, v, side, first, count)
        nexts[tag] = beside(pieces[tag])
    base = middle_part(meta, own, 1, 0)
    send["n", 0] = next_part(meta, base, nexts["s0"], own, 1)
    for side, tags, chunks in NEAR_GROUPS:
        blocks = near_parts(meta, [nexts[tag] for tag in tags], own, side, chunks)
        for k, block in zip(chunks, blocks):
            (send if side else keep)["n", k] = block
    for tag, side, first, count in FAR_GROUPS:
        piece = across(pieces[tag])
        other = beside(piece)
        blocks = far_parts(meta, piece, other, own, side)
        for i, block in enumerate(blocks):
            (send if side else keep)["f", first + i] = block
    total, come = {}, {}
    for tag in "nf":
        for k in range(CHUNKS):
            key = tag, k
            arrived = over_x(send[key])
            leave, stay = fold(meta, keep[key], arrived)
            arrived = over_z(leave)
            total[key] = add(meta, stay, arrived)
            come[key] = (to_near if tag == "n" else over_far)(total[key])

    def joined(tag, chunks):
        return join(meta, [total[tag, k] for k in chunks], [come[tag, k] for k in chunks])

    near_own, extra = joined("n", range(CHUNKS))
    near_swap = over(swap_target)(near_own)
    near_back = over(hop_of(near_target))(near_own)
    near_back = over(after_hop(near_target))(near_back)
    far_own, far_back = [], []
    for chunks in ((0, 1), (2,), (3,)):
        far_own += joined("f", chunks)
        far_back.append(over(far_target)(far_own[-1]))
    fixed = (t, v, row_gap, col_gap)
    pair = most(meta, near_own, far_own[0], *fixed)
    pair = late(meta, 2, far_own[1:], *pair, *fixed)
    values = [near_own, near_swap, near_back, extra, *far_back]
    return back_half(meta, values, *pair, *fixed)


NEAR_GROUPS = ((1, ("s0", "s1"), (1, 2, 3)), (0, ("k0",), (0,)), (0, ("k0", "k1"), (1, 2, 3)))
FAR_GROUPS = (("s0", 1, 0, 2), ("k0", 0, 0, 2), ("s1", 1, 2, 2), ("k1", 0, 2, 2))


def gap_slices(shape, occ_energy, vir_energy):
    tile_rows, tile_cols = shape
    gaps = (vir_energy[None, :] - occ_energy[:, None]).reshape(-1)
    row_gap = lax.dynamic_slice_in_dim(gaps, lax.axis_index("row") * tile_rows, tile_rows, 0)
    col_gap = lax.dynamic_slice_in_dim(gaps, lax.axis_index("col") * tile_cols, tile_cols, 0)
    return row_gap[:, None], col_gap[None, :]


def split_local(amplitudes, interaction, occ_energy, vir_energy):
    gaps = gap_slices(amplitudes.shape, occ_energy, vir_energy)
    return tuple(split_update(amplitudes, interaction, *gaps))


def general_local(amplitudes, interaction, occ_energy, vir_energy):
    row_gap, col_gap = gap_slices(amplitudes.shape, occ_energy, vir_energy)
    denom = row_gap + col_gap
    residual = interaction + general_sum(amplitudes, interaction) + denom * amplitudes
    updated = amplitudes - residual / denom
    return (updated, residual)


def solution(mesh):
    rows, cols = mesh.shape["row"], mesh.shape["col"]
    split = cols == 4 and rows == 2 * cols
    return jax.shard_map(
        split_local if split else general_local,
        mesh=mesh,
        in_specs=(P("row", "col"), P("row", "col"), P(), P()),
        out_specs=(P("row", "col"), P("row", "col")),
        check_vma=False,
    )
```

```python
import functools

import jax
import jax.numpy as jnp
from jax import lax
from jax.experimental import pallas as pl
from jax.experimental.pallas import tpu as pltpu
from jax.sharding import PartitionSpec as P


CHUNKS = 4
PAD = 8


def swapped(block, axis, distance):
    count = lax.axis_size(axis)
    route = []
    for low in range(count):
        high = low | 1 << distance
        if high != low and high < count:
            route += [(low, high), (high, low)]
    return lax.ppermute(block, axis, route)


def from_behind(block, axis, distance):
    devices = range(lax.axis_size(axis))
    route = [(i - distance, i) for i in devices if i - distance in devices]
    return lax.ppermute(block, axis, route)


def contract(left_tile, right_tile):
    right_panel = lax.all_gather(right_tile, "row", axis=0, tiled=True)
    return jnp.dot(
        lax.all_gather(left_tile, "col", axis=1, tiled=True),
        right_panel,
        precision=lax.Precision.HIGHEST,
        preferred_element_type=jnp.float32,
    )


def diagonal_tile(tile, row_place, col_place):
    tile_rows = tile.shape[0]
    col_count = lax.axis_size("col")
    ratio = lax.axis_size("row") // col_count
    ratio_bits = ratio.bit_length() - 1
    row_bits = lax.axis_size("row").bit_length() - 1
    blocks = tile.reshape(tile_rows, ratio, tile_rows).transpose(1, 2, 0)
    for bit_index in range(row_bits):
        row_flag = row_place // 2**bit_index % 2
        if bit_index < ratio_bits:
            lower = 2**bit_index
            grouped = blocks.reshape(ratio // (2 * lower), 2, lower, tile_rows, tile_rows)
            zero_half = grouped[:, 0]
            one_half = grouped[:, 1]
            outgoing = jnp.where(row_flag == 0, one_half, zero_half)
            incoming = swapped(outgoing, "row", bit_index)
            new_zero = jnp.where(row_flag == 1, incoming, zero_half)
            new_one = jnp.where(row_flag == 0, incoming, one_half)
            blocks = jnp.stack([new_zero, new_one], axis=1).reshape(ratio, tile_rows, tile_rows)
        else:
            col_flag = col_place // 2 ** (bit_index - ratio_bits) % 2
            stride = 2**bit_index * col_count - 2 ** (bit_index - ratio_bits)
            from_above = from_behind(blocks, ("row", "col"), -stride)
            from_below = from_behind(blocks, ("row", "col"), stride)
            incoming = jnp.where(row_flag == 0, from_above, from_below)
            blocks = jnp.where(row_flag != col_flag, incoming, blocks)
    return blocks.transpose(1, 0, 2).reshape(tile_rows, ratio * tile_rows)


def general_sum(amplitudes, interaction):
    product = contract(amplitudes, interaction)
    mirrored = diagonal_tile(product, lax.axis_index("row"), lax.axis_index("col"))
    return product + mirrored


def routed(block, target):
    rows, cols = lax.axis_size("row"), lax.axis_size("col")
    route = []
    for r in range(rows):
        for c in range(cols):
            place = target(r, c)
            if place is not None:
                route.append((r * cols + c, place[0] * cols + place[1]))
    return lax.ppermute(block, ("row", "col"), route)


def is_near(r, c):
    return r >> 2 == c >> 1


def flips(z, c):
    return (z > c) ^ ((z ^ c) == 3)


def flipped(z, x, c):
    return x ^ flips(z, c)


def swap_target(r, c):
    return (r ^ 1, c) if r >> 1 == c else None


def near_target(r, c):
    z, x = r >> 1, r & 1
    if not is_near(r, c) or z == c:
        return None
    return (2 * c + flipped(z, x, c), z)


def far_target(r, c):
    z, x = r >> 1, r & 1
    if not is_near(r, c):
        return None
    return (2 * c + flipped(z ^ 2, x, c), z ^ 2)


def hop_of(target):
    return lambda r, c: target(r, c) and (r, c ^ 2)


def after_hop(target):
    return lambda r, c: target(r, c ^ 2)


X_PLACE, ODD, TURN_1, TURN_2, TURN_3, NEAR, MIDDLE, PLACE = range(8)
SMALL, MEDIUM, LARGE, WHOLE = 8 * 2**20, 24 * 2**20, 40 * 2**20, 60 * 2**20


def zeros(count):
    return (0,) * count


def call(kernel, shapes, meta, args, in_specs=None, out_specs=None, scratch=(), aliases=None, vmem=LARGE):
    if in_specs is None:
        in_specs = [None] * len(args)
    if out_specs is None:
        out_specs = [None] * len(shapes)
    whole = lambda a: pl.BlockSpec(a.shape, lambda i, m: zeros(len(a.shape)))
    return pl.pallas_call(
        kernel,
        out_shape=list(shapes),
        grid_spec=pltpu.PrefetchScalarGridSpec(
            num_scalar_prefetch=1,
            grid=(1,),
            in_specs=[s or whole(a) for s, a in zip(in_specs, args)],
            out_specs=[s or whole(a) for s, a in zip(out_specs, shapes)],
            scratch_shapes=list(scratch),
        ),
        input_output_aliases=aliases or {},
        compiler_params=pltpu.CompilerParams(vmem_limit_bytes=vmem),
    )(meta, *args)


def shaped(*shape):
    return jax.ShapeDtypeStruct(shape, jnp.float32)


def halves(value):
    high = value.astype(jnp.bfloat16)
    return high, (value - high.astype(jnp.float32)).astype(jnp.bfloat16)


def joined_left(t_high, t_low, v_high, v_low):
    return jnp.concatenate([t_high, t_high, t_low, v_high, v_high, v_low], axis=1)


def left_of(t, v):
    t_high, t_low = halves(t.T)
    v_high, v_low = halves(v.T)
    return joined_left(t_high, t_low, v_high, v_low)


def own_left(own_ref, cols):
    return joined_left(*(own_ref[i, :, cols].T for i in range(4)))


def own_right(own_ref, cols):
    return jnp.concatenate([own_ref[i, :, cols] for i in (2, 3, 2, 0, 1, 0)], axis=0)


def crossed(left, right):
    return jnp.dot(left, right, preferred_element_type=jnp.float32)


def placed(place, n, offset=0, size=None):
    return pl.ds(pl.multiple_of(place * n + offset, 128), size or n)


def pick_kernel(side, first, m, t_ref, v_ref, out_ref, sems):
    n = t_ref.shape[0]
    cols = placed(m[X_PLACE] ^ side, n, first, out_ref.shape[2])
    copies = [
        pltpu.make_async_copy(ref.at[:, cols], out_ref.at[i], sems.at[i])
        for i, ref in enumerate((t_ref, v_ref))
    ]
    for copy in copies:
        copy.start()
    for copy in copies:
        copy.wait()


def pick(meta, t, v, side, first, count):
    n = t.shape[0]
    w = n // CHUNKS
    hbm = pl.BlockSpec(memory_space=pltpu.MemorySpace.HBM)
    return call(
        functools.partial(pick_kernel, side, first * w),
        [shaped(2, n, count * w)],
        meta,
        [t, v],
        in_specs=[hbm, hbm],
        scratch=[pltpu.SemaphoreType.DMA((2,))],
        vmem=LARGE if first or not side else WHOLE,
    )[0]


def prep_kernel(_, t_ref, v_ref, own_ref):
    own_ref[0], own_ref[1] = halves(t_ref[...])
    own_ref[2], own_ref[3] = halves(v_ref[...])


def prep(meta, t, v):
    return call(prep_kernel, [jax.ShapeDtypeStruct((4, *t.shape), jnp.bfloat16)], meta, [t, v])[0]


def lines(k, w):
    return w + PAD if k == CHUNKS - 1 else w


def middle_block(m, side, chunks, own_ref, outs):
    n = own_ref.shape[1]
    w = n // CHUNKS
    half = m[X_PLACE] ^ side
    same, cross = placed(half, n), placed(1 - half, n)
    left = own_left(own_ref, placed(half, n, chunks[0] * w, len(chunks) * w))
    diagonal = crossed(left, own_right(own_ref, same))
    aside = crossed(left, own_right(own_ref, cross))
    lane = lax.broadcasted_iota(jnp.int32, (w, n), 1)
    for i, (k, out_ref) in enumerate(zip(chunks, outs)):
        line = lax.broadcasted_iota(jnp.int32, (w, n), 0) + k * w
        rows = slice(i * w, (i + 1) * w)
        out_ref[0, :w, :] = jnp.where(line >= lane, diagonal[rows], aside[rows])
        if out_ref.shape[1] > w:
            whole = lambda i, cols: own_ref[i, :, cols].astype(jnp.float32) + own_ref[
                i + 1, :, cols
            ].astype(jnp.float32)
            products = whole(0, same) * whole(2, cross) + whole(2, same) * whole(0, cross)
            extra = jnp.sum(products, axis=0, keepdims=True)
            out_ref[0, w:, :] = jnp.broadcast_to(extra, (PAD, n))


def middle_kernel(side, k, m, own_ref, out_ref):
    middle_block(m, side, (k,), own_ref, [out_ref])


def middle_part(meta, own, side, k):
    n = own.shape[1]
    w = lines(k, n // CHUNKS)
    return call(
        functools.partial(middle_kernel, side, k),
        [shaped(2, w, n)],
        meta,
        [own],
        out_specs=[pl.BlockSpec((1, w, n), lambda i, m: (0, 0, 0))],
    )[0]


def next_part(meta, base, piece, own, side):
    n = own.shape[1]
    w = n // CHUNKS
    return call(
        functools.partial(next_kernel, side),
        [shaped(*base.shape)],
        meta,
        [base, piece, own],
        in_specs=[
            pl.BlockSpec(memory_space=pl.ANY),
            pl.BlockSpec((2, n, w), lambda i, m: (0, 0, 0)),
            None,
        ],
        out_specs=[pl.BlockSpec((1, *base.shape[1:]), lambda i, m: (1, 0, 0))],
        aliases={1: 0},
    )[0]


def next_kernel(side, m, _, piece_ref, own_ref, out_ref):
    n = own_ref.shape[1]
    right = own_right(own_ref, placed(m[TURN_1] ^ side, n))
    out_ref[0] = crossed(left_of(piece_ref[0], piece_ref[1]), right)


def near_parts(meta, pieces, own, side, chunks):
    n = own.shape[1]
    w = n // CHUNKS
    return call(
        functools.partial(near_kernel, side, chunks),
        [shaped(2, lines(k, w), n) for k in chunks],
        meta,
        [*pieces, own],
    )


def near_kernel(side, chunks, m, *refs):
    pieces, own_ref, outs = refs[: -1 - len(chunks)], refs[-1 - len(chunks)], refs[-len(chunks) :]
    n = own_ref.shape[1]
    w = n // CHUNKS
    middle_block(m, side, chunks, own_ref, outs)
    left = jnp.concatenate([left_of(ref[0], ref[1]) for ref in pieces], axis=0)
    first = chunks[0] * w
    left = left[first : first + len(chunks) * w]
    block = crossed(left, own_right(own_ref, placed(m[TURN_1] ^ side, n)))
    for i, out_ref in enumerate(outs):
        out_ref[1, :w, :] = block[i * w : (i + 1) * w]
        if out_ref.shape[1] > w:
            out_ref[1, w:, :] = jnp.zeros((PAD, n), jnp.float32)


def far_kernel(side, m, a_ref, b_ref, own_ref, *outs):
    n = own_ref.shape[1]
    w = outs[0].shape[1]
    for d, (ref, turn) in enumerate(((a_ref, TURN_2), (b_ref, TURN_3))):
        right = own_right(own_ref, placed(m[turn] ^ side, n))
        block = crossed(left_of(ref[0], ref[1]), right)
        for i, out_ref in enumerate(outs):
            out_ref[d] = block[i * w : (i + 1) * w]


def far_parts(meta, a, b, own, side):
    n = own.shape[1]
    w = n // CHUNKS
    return call(
        functools.partial(far_kernel, side),
        [shaped(2, w, n)] * (a.shape[2] // w),
        meta,
        [a, b, own],
    )


def fold_kernel(_, keep_pass, come_pass, keep_stay, come_stay, pass_ref, stay_ref):
    pass_ref[...] = keep_pass[0] + come_pass[0]
    stay_ref[...] = keep_stay[0] + come_stay[0]


def fold(meta, keep, come):
    _, lines, n = keep.shape
    leave = pl.BlockSpec((1, lines, n), lambda i, m: (1 - m[ODD], 0, 0))
    stay = pl.BlockSpec((1, lines, n), lambda i, m: (m[ODD], 0, 0))
    return call(
        fold_kernel,
        [shaped(lines, n)] * 2,
        meta,
        [keep, come, keep, come],
        in_specs=[leave, leave, stay, stay],
        vmem=SMALL,
    )


def add_kernel(_, a_ref, b_ref, out_ref):
    out_ref[...] = a_ref[...] + b_ref[...]


def add(meta, a, b):
    return call(add_kernel, [shaped(*a.shape)], meta, [a, b], vmem=SMALL)[0]


def join_kernel(w, count, _, *refs):
    out_ref = refs[2 * count]
    for k in range(count):
        a_ref, b_ref = refs[k], refs[count + k]
        out_ref[k * w : (k + 1) * w, :] = a_ref[:w, :] + b_ref[:w, :]
        if a_ref.shape[0] > w:
            refs[2 * count + 1][...] = a_ref[w:, :] + b_ref[w:, :]


def join(meta, parts, comes):
    n = parts[0].shape[1]
    w = n // CHUNKS
    shapes = [shaped(len(parts) * w, n)]
    if parts[-1].shape[0] > w:
        shapes.append(shaped(PAD, n))
    return call(functools.partial(join_kernel, w, len(parts)), shapes, meta, [*parts, *comes], vmem=MEDIUM)


def closing(t, v, row, col, value):
    denom = row + col
    residual = v + value + denom * t
    return t - residual / denom, residual


def grid_of(n):
    line = lax.broadcasted_iota(jnp.int32, (n, n), 0)
    return line, lax.broadcasted_iota(jnp.int32, (n, n), 1)


def most_kernel(m, near_ref, far_ref, t_ref, v_ref, row_ref, col_ref, new_ref, res_ref):
    n = t_ref.shape[0]

    def write(value):
        rows = slice(0, value.shape[0])
        new_ref[rows], res_ref[rows] = closing(
            t_ref[rows], v_ref[rows], row_ref[rows], col_ref[...], value
        )

    @pl.when(m[NEAR] == 0)
    def _():
        write(far_ref[...])

    @pl.when((m[NEAR] == 1) & (m[MIDDLE] == 0))
    def _():
        write(near_ref[...])

    @pl.when(m[MIDDLE] == 1)
    def _():
        line, lane = grid_of(n)
        own = near_ref[...]
        write(jnp.where(line >= lane, own, own.T))


def half_specs(n, at):
    block = pl.BlockSpec((n, n), lambda i, m: (0, at(m)))
    return [block, block, None, pl.BlockSpec((1, n), lambda i, m: (0, at(m)))], [block, block]


def most(meta, near_own, far_own, t, *args):
    ins, outs = half_specs(t.shape[0], lambda m: m[PLACE])
    return call(
        most_kernel,
        [shaped(*t.shape)] * 2,
        meta,
        [near_own, far_own, t, *args],
        in_specs=[None, None, *ins],
        out_specs=outs,
        vmem=MEDIUM,
    )


def back_kernel(m, near_ref, swap_ref, back_ref, extra_ref, *refs):
    far = refs[:3]
    t_ref, v_ref, row_ref, col_ref, _, _, new_ref, res_ref = refs[3:]
    n = t_ref.shape[0]

    def write(value, cols=slice(None)):
        new_ref[:, cols], res_ref[:, cols] = closing(
            t_ref[:, cols], v_ref[:, cols], row_ref[...], col_ref[:, cols], value
        )

    @pl.when(m[NEAR] == 0)
    def _():
        first = 0
        for ref in far:
            write(ref[...].T, slice(first, first + ref.shape[0]))
            first += ref.shape[0]

    @pl.when((m[NEAR] == 1) & (m[MIDDLE] == 0))
    def _():
        write(back_ref[...].T)

    @pl.when(m[MIDDLE] == 1)
    def _():
        line, lane = grid_of(n)
        lower = jnp.where(line > lane, swap_ref[...].T, extra_ref[:1, :])
        write(jnp.where(line < lane, near_ref[...], lower))


def back_half(meta, values, new, res, t, *args):
    ins, outs = half_specs(t.shape[0], lambda m: 1 - m[PLACE])
    hbm = pl.BlockSpec(memory_space=pl.ANY)
    count = len(values) + 4
    return call(
        back_kernel,
        [shaped(*t.shape)] * 2,
        meta,
        [*values, t, *args, new, res],
        in_specs=[*[None] * len(values), *ins, hbm, hbm],
        out_specs=outs,
        aliases={count + 1: 0, count + 2: 1},
        vmem=MEDIUM,
    )


def late_kernel(chunk, count, m, *refs):
    values = refs[:count]
    t_ref, v_ref, row_ref, col_ref, new_ref, res_ref, new, res, sems = refs[count + 2 :]
    w, n = values[0].shape

    @pl.when(m[NEAR] == 0)
    def _():
        value = jnp.concatenate([ref[...] for ref in values], axis=0)
        new[...], res[...] = closing(
            t_ref[...], v_ref[...], row_ref[...], col_ref[...], value
        )
        rows, cols = pl.ds(chunk * w, count * w), placed(m[PLACE], n)
        copies = [
            pltpu.make_async_copy(source, target.at[rows, cols], sems.at[i])
            for i, (source, target) in enumerate(((new, new_ref), (res, res_ref)))
        ]
        for copy in copies:
            copy.start()
        for copy in copies:
            copy.wait()


def late(meta, chunk, values, new, res, t, v, row_gap, col_gap):
    w, n = values[0].shape
    count = len(values)
    block = pl.BlockSpec((count * w, n), lambda i, m: (chunk // count, m[PLACE]))
    row = pl.BlockSpec((count * w, 1), lambda i, m: (chunk // count, 0))
    col = pl.BlockSpec((1, n), lambda i, m: (0, m[PLACE]))
    hbm = pl.BlockSpec(memory_space=pl.ANY)
    return call(
        functools.partial(late_kernel, chunk, count),
        [shaped(*t.shape)] * 2,
        meta,
        [*values, new, res, t, v, row_gap, col_gap],
        in_specs=[*[None] * count, hbm, hbm, block, block, row, col],
        out_specs=[hbm, hbm],
        scratch=[pltpu.VMEM(block.block_shape, jnp.float32)] * 2 + [pltpu.SemaphoreType.DMA((2,))],
        aliases={count + 1: 0, count + 2: 1},
        vmem=MEDIUM,
    )


def split_update(t, v, row_gap, col_gap):
    r = lax.axis_index("row")
    c = lax.axis_index("col")
    z, x = r // 2, r % 2
    slot = lax.iota(jnp.int32, 8)
    values = {
        X_PLACE: x,
        ODD: (z + c) % 2,
        TURN_1: x ^ flips(c ^ 1, c),
        TURN_2: x ^ flips(c ^ 2, c),
        TURN_3: x ^ flips(c ^ 3, c),
        NEAR: r // 4 == c // 2,
        MIDDLE: z == c,
        PLACE: x ^ flips(z, c),
    }
    meta = jnp.zeros((8,), jnp.int32)
    for index, value in values.items():
        meta = jnp.where(slot == index, value.astype(jnp.int32), meta)

    across = lambda block: routed(block, lambda r, c: (r, c ^ 2))
    beside = lambda block: routed(block, lambda r, c: (r, c ^ 1))
    over_x = lambda block: routed(block, lambda r, c: (r ^ 1, c))
    over_z = lambda block: routed(block, lambda r, c: (r ^ 2, c))
    over_far = lambda block: routed(block, lambda r, c: (r ^ 4, c))
    to_near = lambda block: routed(block, lambda r, c: None if is_near(r, c) else (r ^ 4, c))
    over = lambda target: lambda block: routed(block, target)

    own = prep(meta, t, v)
    send, keep, pieces, nexts = {}, {}, {}, {}
    for tag, side, first, count in FAR_GROUPS:
        pieces[tag] = pick(meta, t, v, side, first, count)
        nexts[tag] = beside(pieces[tag])
    base = middle_part(meta, own, 1, 0)
    send["n", 0] = next_part(meta, base, nexts["s0"], own, 1)
    for side, tags, chunks in NEAR_GROUPS:
        blocks = near_parts(meta, [nexts[tag] for tag in tags], own, side, chunks)
        for k, block in zip(chunks, blocks):
            (send if side else keep)["n", k] = block
    for tag, side, first, count in FAR_GROUPS:
        piece = across(pieces[tag])
        other = beside(piece)
        blocks = far_parts(meta, piece, other, own, side)
        for i, block in enumerate(blocks):
            (send if side else keep)["f", first + i] = block
    total, come = {}, {}
    for tag in "nf":
        for k in range(CHUNKS):
            key = tag, k
            arrived = over_x(send[key])
            leave, stay = fold(meta, keep[key], arrived)
            arrived = over_z(leave)
            total[key] = add(meta, stay, arrived)
            come[key] = (to_near if tag == "n" else over_far)(total[key])

    def joined(tag, chunks):
        return join(meta, [total[tag, k] for k in chunks], [come[tag, k] for k in chunks])

    near_own, extra = joined("n", range(CHUNKS))
    near_swap = over(swap_target)(near_own)
    near_back = over(hop_of(near_target))(near_own)
    near_back = over(after_hop(near_target))(near_back)
    far_own, far_back = [], []
    for chunks in ((0, 1), (2,), (3,)):
        far_own += joined("f", chunks)
        far_back.append(over(far_target)(far_own[-1]))
    fixed = (t, v, row_gap, col_gap)
    pair = most(meta, near_own, far_own[0], *fixed)
    pair = late(meta, 2, far_own[1:], *pair, *fixed)
    values = [near_own, near_swap, near_back, extra, *far_back]
    return back_half(meta, values, *pair, *fixed)


NEAR_GROUPS = ((1, ("s0", "s1"), (1, 2, 3)), (0, ("k0",), (0,)), (0, ("k0", "k1", "k2"), (1, 2, 3)))
FAR_GROUPS = (("s0", 1, 0, 2), ("k0", 0, 0, 2), ("s1", 1, 2, 2), ("k1", 0, 2, 1), ("k2", 0, 3, 1))


def gap_slices(shape, occ_energy, vir_energy):
    tile_rows, tile_cols = shape
    gaps = (vir_energy[None, :] - occ_energy[:, None]).reshape(-1)
    row_gap = lax.dynamic_slice_in_dim(gaps, lax.axis_index("row") * tile_rows, tile_rows, 0)
    col_gap = lax.dynamic_slice_in_dim(gaps, lax.axis_index("col") * tile_cols, tile_cols, 0)
    return row_gap[:, None], col_gap[None, :]


def split_local(amplitudes, interaction, occ_energy, vir_energy):
    gaps = gap_slices(amplitudes.shape, occ_energy, vir_energy)
    return tuple(split_update(amplitudes, interaction, *gaps))


def general_local(amplitudes, interaction, occ_energy, vir_energy):
    row_gap, col_gap = gap_slices(amplitudes.shape, occ_energy, vir_energy)
    denom = row_gap + col_gap
    residual = interaction + general_sum(amplitudes, interaction) + denom * amplitudes
    updated = amplitudes - residual / denom
    return (updated, residual)


def solution(mesh):
    rows, cols = mesh.shape["row"], mesh.shape["col"]
    split = cols == 4 and rows == 2 * cols
    return jax.shard_map(
        split_local if split else general_local,
        mesh=mesh,
        in_specs=(P("row", "col"), P("row", "col"), P(), P()),
        out_specs=(P("row", "col"), P("row", "col")),
        check_vma=False,
    )
```
